32 devices in a mesh: dp: 16 (over z, y, x), tensor: 2 (over core).
Axes of the slice: x: 2, y: 2, z: 4, core: 2. Of those that a mesh axis runs over, the one named last changes fastest.
Arguments:
- tokens: bfloat16 [16384, 1024], P('dp'), may hold values from -6 to 6
- page_ids: int32 [16384], P('dp'), may hold values from 0 to 31, as said below
- image_of_page: int32 [32], P('dp'), may hold values from 0 to 31, as said below
- memory: bfloat16 [32, 588, 1024], P('dp'), may hold values from -6 to 6
- ln0_gain: float32 [1024], replicated, may hold values from 0.25 to 1.75
- ln0_bias: float32 [1024], replicated, may hold values from -3 to 3
- w_self_query: bfloat16 [1024, 1024], P(None, 'tensor'), may hold values from -0.25 to 0.25
- b_self_query: float32 [1024], P('tensor'), may hold values from -3 to 3
- w_self_key: bfloat16 [1024, 1024], P(None, 'tensor'), may hold values from -0.1875 to 0.1875
- w_self_value: bfloat16 [1024, 1024], P(None, 'tensor'), may hold values from -0.1875 to 0.1875
- b_self_value: float32 [1024], P('tensor'), may hold values from -3 to 3
- w_self_out: bfloat16 [1024, 1024], P('tensor'), may hold values from -0.5 to 0.5
- b_self_out: float32 [1024], replicated, may hold values from -3 to 3
- ln1_gain: float32 [1024], replicated, may hold values from 0.25 to 1.75
- ln1_bias: float32 [1024], replicated, may hold values from -3 to 3
- w_query: bfloat16 [1024, 1024], P(None, 'tensor'), may hold values from -0.25 to 0.25
- b_query: float32 [1024], P('tensor'), may hold values from -3 to 3
- w_key: bfloat16 [1024, 1024], P(None, 'tensor'), may hold values from -0.1875 to 0.1875
- w_value: bfloat16 [1024, 1024], P(None, 'tensor'), may hold values from -0.1875 to 0.1875
- b_value: float32 [1024], P('tensor'), may hold values from -3 to 3
- w_out: bfloat16 [1024, 1024], P('tensor'), may hold values from -0.5 to 0.5
- b_out: float32 [1024], replicated, may hold values from -3 to 3
- ln2_gain: float32 [1024], replicated, may hold values from 0.25 to 1.75
- ln2_bias: float32 [1024], replicated, may hold values from -3 to 3
- w_up: bfloat16 [1024, 4096], P(None, 'tensor'), may hold values from -0.1875 to 0.1875
- b_up: float32 [4096], P('tensor'), may hold values from -3 to 3
- w_down: bfloat16 [4096, 1024], P('tensor'), may hold values from -0.125 to 0.125
- b_down: float32 [1024], replicated, may hold values from -3 to 3
- cotangent: bfloat16 [16384, 1024], P('dp'), may hold values from -6 to 6
Outputs:
- layer_out: bfloat16 [16384, 1024], P('dp')
- d_tokens: bfloat16 [16384, 1024], P('dp')
- d_memory: bfloat16 [32, 588, 1024], P('dp')
- d_ln0_gain: float32 [1024], replicated
- d_ln0_bias: float32 [1024], replicated
- d_w_self_query: float32 [1024, 1024], P('dp', 'tensor')
- d_b_self_query: float32 [1024], P('tensor')
- d_w_self_key: float32 [1024, 1024], P('dp', 'tensor')
- d_w_self_value: float32 [1024, 1024], P('dp', 'tensor')
- d_b_self_value: float32 [1024], P('tensor')
- d_w_self_out: float32 [1024, 1024], P('tensor', 'dp')
- d_b_self_out: float32 [1024], replicated
- d_ln1_gain: float32 [1024], replicated
- d_ln1_bias: float32 [1024], replicated
- d_w_query: float32 [1024, 1024], P('dp', 'tensor')
- d_b_query: float32 [1024], P('tensor')
- d_w_key: float32 [1024, 1024], P('dp', 'tensor')
- d_w_value: float32 [1024, 1024], P('dp', 'tensor')
- d_b_value: float32 [1024], P('tensor')
- d_w_out: float32 [1024, 1024], P('tensor', 'dp')
- d_b_out: float32 [1024], replicated
- d_ln2_gain: float32 [1024], replicated
- d_ln2_bias: float32 [1024], replicated
- d_w_up: float32 [1024, 4096], P('dp', 'tensor')
- d_b_up: float32 [4096], P('tensor')
- d_w_down: float32 [4096, 1024], P('tensor', 'dp')
- d_b_down: float32 [1024], replicated
The draws below stay inside these ranges and needn't reach their ends.
Inputs may be any that keep to these rules, and one draw needn't show every extreme that they name: `page_ids`: page numbers never fall from row to row. Each block of 1024 rows (rows b * 1024 to b * 1024 + 1023) has exactly 2 rows at which a new page starts, none among its first 256 rows, except that row 0 starts page 0; every other block begins with the last page of the block before. `image_of_page`: the 2 pages that start in block b read the images b * 2 to b * 2 + 1, each once.
All inputs are finite; a program needn't handle non-finite values.
Results may differ from the reference program's by a relative error of at most 0.023.
Values may be sent and summed in bfloat16 or wider, within the bound.
No kernel may reach another device: no remote copies, remote signals or barrier semaphores. Data moves between devices by JAX's collectives and lax.ppermute only.
A program may use at most 320 MiB of HBM per device.

```python
import math
import jax
import jax.numpy as jnp
from jax import lax

D = 1024
ATTENTION_HEADS = 16
HEAD_WIDTH = 64
FF = 4096
MEM = 588
TOKEN_BLOCK_ROWS = 1024
IMG_DEV = 2
TOKENS = 16384
IMAGES = 32


def draw_page_ids(key, part):
    base = jax.random.fold_in(key, 11)
    block_list = TOKENS // TOKEN_BLOCK_ROWS
    span = TOKEN_BLOCK_ROWS - TOKEN_BLOCK_ROWS // 4
    block_keys = jax.random.split(base, block_list)
    picks = jax.vmap(lambda single: jax.random.permutation(single, span)[:IMG_DEV])(block_keys).astype(jnp.int32) + TOKEN_BLOCK_ROWS // 4
    picks = picks.at[0, 0].set(0)
    starts = jnp.zeros((block_list, TOKEN_BLOCK_ROWS), jnp.int32).at[jnp.arange(block_list)[:, None], picks].set(1)
    return (jnp.cumsum(starts.reshape(-1)) - 1).astype(jnp.int32)


def draw_image_of_page(key, part):
    base = jax.random.fold_in(key, 23)
    block_list = IMAGES // IMG_DEV
    block_keys = jax.random.split(base, block_list)
    local = jax.vmap(lambda single: jax.random.permutation(single, IMG_DEV))(block_keys).astype(jnp.int32)
    return (local + jnp.arange(block_list, dtype=jnp.int32)[:, None] * IMG_DEV).reshape(-1).astype(jnp.int32)


def raised(drawn, own_key, source, target, blocks, factor):
    def block_of(dim):
        return (jnp.arange(drawn.shape[dim]) // (drawn.shape[dim] // blocks)).reshape((-1,) + (1,) * (drawn.ndim - 1 - dim))

    one_side = jax.random.permutation(own_key, blocks)[block_of(target)]
    second = (block_of(target) + blocks // 2) % blocks
    return jnp.where((block_of(source) == one_side) | (block_of(source) == second), factor * drawn, drawn)


def level_of(own_key, shape, pieces, least, largest):
    level, own = 1.0, jax.random.fold_in(own_key, 6)
    for dim, blocks in pieces:
        draws = jnp.exp(jax.random.uniform(jax.random.fold_in(own, dim), (blocks,), jnp.float32, least / len(pieces), largest / len(pieces)))
        level = level * jnp.repeat(draws, shape[dim] // blocks).reshape([-1 if axis == dim else 1 for axis in range(len(shape))])
    return level


def gaussian(stream_key, shape, width, limit, cuts=(), kind=jnp.bfloat16):
    drawn = jax.random.normal(stream_key, shape, jnp.float32) * width
    if len(cuts) > 0:
        drawn = level_of(stream_key, shape, cuts, -0.22, 0.18) * drawn
    return jnp.clip(drawn, min=-limit, max=limit).astype(kind)


def gaussian_with(stream_key, extent, scale, bound, cuts, heavy, held_as=jnp.bfloat16):
    drawn = scale * jax.random.normal(stream_key, extent, jnp.float32)
    if cuts:
        drawn = drawn * level_of(stream_key, extent, cuts, -0.22, 0.18)
    return jnp.clip(raised(drawn, jax.random.fold_in(stream_key, 3), *heavy), -bound, bound).astype(held_as)


def setup_inputs(seed: int = 0) -> dict:
    key_list = jax.random.split(jax.random.key(seed), 30)
    return {
        "tokens": gaussian_with(key_list[0], (TOKENS, D), 1.0, 6.0, ((0, 16),), (0, 1, 16, 2.0)),
        "page_ids": draw_page_ids(jax.random.fold_in(key_list[29], 71), 0),
        "image_of_page": draw_image_of_page(jax.random.fold_in(key_list[29], 71), 0),
        "memory": gaussian(key_list[3], (IMAGES, MEM, D), 1.0, 6.0, ((0, 16),)),
        "ln0_gain": jnp.clip(1.0 + 0.15 * jax.random.normal(key_list[4], (D,), jnp.float32), 0.25, 1.75),
        "ln0_bias": gaussian(key_list[5], (D,), 0.3, 3.0, (), jnp.float32),
        "w_self_query": gaussian(key_list[6], (D, D), (D // 2) ** -0.5, 0.25, ((1, 2),)),
        "b_self_query": gaussian(key_list[7], (D,), 0.3, 3.0, ((0, 2),), jnp.float32),
        "w_self_key": gaussian(key_list[8], (D, D), D ** -0.5, 0.1875, ((1, 2),)),
        "w_self_value": gaussian(key_list[9], (D, D), D ** -0.5, 0.1875, ((1, 2),)),
        "b_self_value": gaussian(key_list[10], (D,), 0.3, 3.0, ((0, 2),), jnp.float32),
        "w_self_out": gaussian(key_list[11], (D, D), (D // 8) ** -0.5, 0.5, ((0, 2),)),
        "b_self_out": gaussian(key_list[12], (D,), 0.3, 3.0, (), jnp.float32),
        "ln1_gain": jnp.clip(1.0 + 0.15 * jax.random.normal(key_list[13], (D,), jnp.float32), 0.25, 1.75),
        "ln1_bias": gaussian(key_list[14], (D,), 0.3, 3.0, (), jnp.float32),
        "w_query": gaussian(key_list[15], (D, D), (D // 2) ** -0.5, 0.25, ((1, 2),)),
        "b_query": gaussian(key_list[16], (D,), 0.3, 3.0, ((0, 2),), jnp.float32),
        "w_key": gaussian(key_list[17], (D, D), D ** -0.5, 0.1875, ((1, 2),)),
        "w_value": gaussian(key_list[18], (D, D), D ** -0.5, 0.1875, ((1, 2),)),
        "b_value": gaussian(key_list[19], (D,), 0.3, 3.0, ((0, 2),), jnp.float32),
        "w_out": gaussian(key_list[20], (D, D), (D // 8) ** -0.5, 0.5, ((0, 2),)),
        "b_out": gaussian(key_list[21], (D,), 0.3, 3.0, (), jnp.float32),
        "ln2_gain": jnp.clip(1.0 + 0.15 * jax.random.normal(key_list[22], (D,), jnp.float32), 0.25, 1.75),
        "ln2_bias": gaussian(key_list[23], (D,), 0.3, 3.0, (), jnp.float32),
        "w_up": gaussian(key_list[24], (D, FF), D ** -0.5, 0.1875, ((1, 2),)),
        "b_up": gaussian(key_list[25], (FF,), 0.3, 3.0, ((0, 2),), jnp.float32),
        "w_down": gaussian(key_list[26], (FF, D), (FF // 2) ** -0.5, 0.125, ((0, 2),)),
        "b_down": gaussian(key_list[27], (D,), 0.3, 3.0, (), jnp.float32),
        "cotangent": gaussian_with(key_list[28], (TOKENS, D), 1.0, 6.0, ((0, 16),), (0, 1, 16, 2.0)),
    }


@jax.custom_vjp
def lower_precision(v):
    return lax.optimization_barrier(v.astype(jnp.bfloat16)).astype(jnp.float32)

@jax.custom_vjp
def lower_precision_backward(v):
    return v

def low_keep(v):
    return (lower_precision(v), None)

def low_pass(kept, grad):
    return (grad,)

def back_keep(v):
    return (v, None)

def back_low(kept, grad):
    return (lower_precision(grad),)
lower_precision.defvjp(low_keep, low_pass)
lower_precision_backward.defvjp(back_keep, back_low)
EPSILON = 1e-05

def layer_norm(values, gain, bias):
    mean = lax.optimization_barrier(jnp.mean(values, axis=-1, keepdims=True))
    centered = values - mean
    variance = lax.optimization_barrier(jnp.mean(centered * centered, axis=-1, keepdims=True))
    return centered * lax.rsqrt(variance + EPSILON) * gain + bias

def matrix_multiply(left, right):
    return jnp.dot(left, right, precision=lax.Precision.HIGHEST, preferred_element_type=jnp.float32)

def masked_attention(query_block, key_table, value_table, allowed):
    scores = lower_precision_backward(jnp.einsum('thd,chd->htc', query_block, key_table, precision=lax.Precision.HIGHEST))
    scores = jnp.where(allowed[None], scores, -1e+30)
    weights = lower_precision(jax.nn.softmax(scores, axis=-1))
    return jnp.einsum('htc,chd->thd', weights, value_table, precision=lax.Precision.HIGHEST)

def reference(tokens, page_ids, image_of_page, memory, ln0_gain, ln0_bias, w_self_query, b_self_query, w_self_key, w_self_value, b_self_value, w_self_out, b_self_out, ln1_gain, ln1_bias, w_query, b_query, w_key, w_value, b_value, w_out, b_out, ln2_gain, ln2_bias, w_up, b_up, w_down, b_down, cotangent):
    scale = 1.0 / math.sqrt(HEAD_WIDTH)
    block_list = TOKENS // TOKEN_BLOCK_ROWS
    token_image = jnp.take(image_of_page, page_ids).astype(jnp.int32)
    image_blocks = token_image.reshape(block_list, TOKEN_BLOCK_ROWS)
    page_blocks = page_ids.reshape(block_list, TOKEN_BLOCK_ROWS).astype(jnp.int32)
    prior_pages = jnp.concatenate([jnp.full((1, TOKEN_BLOCK_ROWS), -1, jnp.int32), page_blocks[:-1]], 0)
    block_index = jnp.arange(block_list, dtype=jnp.int32)
    offsets = jnp.arange(2 * IMG_DEV, dtype=jnp.int32)
    positions = jnp.arange(TOKEN_BLOCK_ROWS, dtype=jnp.int32)

    def forward_pass(input_values, memory_input, self_norm_gain, self_norm_bias, self_query_weight, self_query_bias, self_key_weight, self_value_weight, self_value_bias, self_output_weight, self_output_bias, cross_norm_gain, cross_norm_bias, query_weight, query_bias, key_weight, value_weight, value_bias, output_weight, output_bias, feedforward_norm_gain, feedforward_norm_bias, upward_weight, upward_bias, down_weight, down_bias):
        self_normed_rows = lower_precision(layer_norm(input_values, self_norm_gain, self_norm_bias))
        self_queries = lower_precision(lower_precision_backward((matrix_multiply(self_normed_rows, self_query_weight) + self_query_bias) * scale)).reshape(block_list, TOKEN_BLOCK_ROWS, ATTENTION_HEADS, HEAD_WIDTH)
        self_key_rows = lower_precision(lower_precision_backward(matrix_multiply(self_normed_rows, self_key_weight))).reshape(block_list, TOKEN_BLOCK_ROWS, ATTENTION_HEADS, HEAD_WIDTH)
        self_values = lower_precision(lower_precision_backward(matrix_multiply(self_normed_rows, self_value_weight) + self_value_bias)).reshape(block_list, TOKEN_BLOCK_ROWS, ATTENTION_HEADS, HEAD_WIDTH)
        zero_block = jnp.zeros((1, TOKEN_BLOCK_ROWS, ATTENTION_HEADS, HEAD_WIDTH), jnp.float32)
        prior_keys = jnp.concatenate([zero_block, self_key_rows[:-1]], 0)
        prior_values = jnp.concatenate([zero_block, self_values[:-1]], 0)

        def self_attend(block):
            query_block, key_prior, key_own, value_prior, value_own, pages, earlier_pages = block
            own_ok = (pages[:, None] == pages[None, :]) & (positions[None, :] <= positions[:, None])
            prior_ok = earlier_pages[None, :] == pages[:, None]
            allowed = jnp.concatenate([prior_ok, own_ok], 1)
            key_table = jnp.concatenate([key_prior, key_own], 0)
            value_table = jnp.concatenate([value_prior, value_own], 0)
            return masked_attention(query_block, key_table, value_table, allowed).reshape(TOKEN_BLOCK_ROWS, D)
        self_out = lax.map(jax.checkpoint(self_attend), (self_queries, prior_keys, self_key_rows, prior_values, self_values, page_blocks, prior_pages))
        self_out = lower_precision(lower_precision_backward(self_out.reshape(TOKENS, D)))
        start = input_values + lower_precision_backward(matrix_multiply(self_out, self_output_weight) + self_output_bias)
        normed = lower_precision(layer_norm(start, cross_norm_gain, cross_norm_bias))
        queries = lower_precision(lower_precision_backward((matrix_multiply(normed, query_weight) + query_bias) * scale))
        flat_memory = memory_input.reshape(IMAGES * MEM, D)
        keys = lower_precision(lower_precision_backward(matrix_multiply(flat_memory, key_weight))).reshape(IMAGES, MEM, ATTENTION_HEADS, HEAD_WIDTH)
        values = lower_precision(lower_precision_backward(matrix_multiply(flat_memory, value_weight) + value_bias)).reshape(IMAGES, MEM, ATTENTION_HEADS, HEAD_WIDTH)

        def attend(block):
            query_block, image_block, index = block
            candidates = (index - 1) * IMG_DEV + offsets
            present = candidates >= 0
            safe = jnp.maximum(candidates, 0).astype(jnp.int32)
            block_keys = jnp.take(keys, safe, axis=0).reshape(2 * IMG_DEV * MEM, ATTENTION_HEADS, HEAD_WIDTH)
            block_values = jnp.take(values, safe, axis=0).reshape(2 * IMG_DEV * MEM, ATTENTION_HEADS, HEAD_WIDTH)
            key_image = jnp.repeat(jnp.where(present, candidates, -1).astype(jnp.int32), MEM)
            allowed = image_block[:, None] == key_image[None, :]
            return masked_attention(query_block, block_keys, block_values, allowed).reshape(TOKEN_BLOCK_ROWS, D)
        attended = lax.map(jax.checkpoint(attend), (queries.reshape(block_list, TOKEN_BLOCK_ROWS, ATTENTION_HEADS, HEAD_WIDTH), image_blocks, block_index))
        attended = lower_precision(lower_precision_backward(attended.reshape(TOKENS, D)))
        branch = lower_precision_backward(matrix_multiply(attended, output_weight) + output_bias)
        middle = start + branch
        normed_two = lower_precision(layer_norm(middle, feedforward_norm_gain, feedforward_norm_bias))
        hidden = lower_precision_backward(matrix_multiply(normed_two, upward_weight) + upward_bias)
        activated = lower_precision(jax.nn.gelu(hidden, approximate=False))
        return middle + matrix_multiply(activated, down_weight) + down_bias
    raw = (tokens, memory, ln0_gain, ln0_bias, w_self_query, b_self_query, w_self_key, w_self_value, b_self_value, w_self_out, b_self_out, ln1_gain, ln1_bias, w_query, b_query, w_key, w_value, b_value, w_out, b_out, ln2_gain, ln2_bias, w_up, b_up, w_down, b_down)
    floats = tuple((item.astype(jnp.float32) for item in raw))
    result, pullback = jax.vjp(forward_pass, *floats)
    grads = pullback(cotangent.astype(jnp.float32))
    return (result.astype(jnp.bfloat16), grads[0].astype(jnp.bfloat16), grads[1].astype(jnp.bfloat16), grads[2], grads[3], grads[4], grads[5], grads[6], grads[7], grads[8], grads[9], grads[10], grads[11], grads[12], grads[13], grads[14], grads[15], grads[16], grads[17], grads[18], grads[19], grads[20], grads[21], grads[22], grads[23], grads[24], grads[25])
```

```python
import math

import jax
import jax.numpy as jnp
from jax import lax
from jax.sharding import PartitionSpec as P

HEAD_WIDTH = 64


EPSILON = 1e-05


def shifted(value, axis, steps):
    count = lax.axis_size(axis)
    initial, last = (max(0, -steps), min(count, count - steps))
    return lax.ppermute(value, axis, [(source, source + steps) for source in range(initial, last)])


def core_sum(partial):
    low = partial.astype(jnp.bfloat16)
    other = lax.ppermute(low, "tensor", [(0, 1), (1, 0)])
    return low.astype(jnp.float32) + other.astype(jnp.float32)


def butterfly_sum(vectors):
    sizes = [vector.shape[0] for vector in vectors]
    total = jnp.concatenate(vectors).reshape(-1, 128)
    count = lax.axis_size("dp")
    bit = 1
    while bit < count:
        total = total + lax.ppermute(total, "dp", [(i, i ^ bit) for i in range(count)])
        bit *= 2
    flat = total.reshape(-1)
    pieces, at = [], 0
    for size in sizes:
        pieces.append(flat[at : at + size])
        at += size
    return pieces


def scattered(gradient, dimension):
    return lax.psum_scatter(
        gradient.astype(jnp.bfloat16), "dp", scatter_dimension=dimension, tiled=True
    ).astype(jnp.float32)


def layer_norm(values, gain, bias):
    mean = jnp.mean(values, axis=-1, keepdims=True)
    centered = values - mean
    inverse = lax.rsqrt(jnp.mean(centered * centered, axis=-1, keepdims=True) + EPSILON)
    normed = centered * inverse
    return (normed * gain + bias, normed, inverse)


def norm_back(grad, normed, inverse, gain):
    scaled = grad * gain
    inner = (
        scaled
        - jnp.mean(scaled, axis=-1, keepdims=True)
        - normed * jnp.mean(scaled * normed, axis=-1, keepdims=True)
    )
    return (inner * inverse, jnp.sum(grad * normed, axis=0), jnp.sum(grad, axis=0))


def block_scores(query_block, allowed_block, key_table):
    scores = jnp.einsum("thd,chd->htc", query_block, key_table, preferred_element_type=jnp.float32)
    return jnp.where(allowed_block[None], scores, -1e30)


def attend_forward(query_blocks, allowed, key_table, value_table):
    block_rows = query_blocks.shape[1]
    local_width = query_blocks.shape[2] * query_blocks.shape[3]

    def forward_block(carry, block):
        query_block, allowed_block = block
        scores = block_scores(query_block, allowed_block, key_table)
        highest = jnp.max(scores, axis=-1, keepdims=True)
        raised = jnp.exp(scores - highest)
        total = jnp.sum(raised, axis=-1, keepdims=True)
        weights = (raised / total).astype(jnp.bfloat16)
        mixed = jnp.einsum("htc,chd->thd", weights, value_table, preferred_element_type=jnp.float32)
        return (
            carry,
            (
                mixed.reshape(block_rows, local_width).astype(jnp.bfloat16),
                (highest + jnp.log(total))[..., 0],
            ),
        )

    unused_carry, (attended, log_totals) = lax.scan(
        forward_block, jnp.zeros((), jnp.float32), (query_blocks, allowed)
    )
    return (attended.reshape(-1, local_width), log_totals)


def attend_backward(query_blocks, allowed, log_totals, grad_rows, key_table, value_table):
    block_count, block_rows, local_heads, head_size = query_blocks.shape
    key_count = key_table.shape[0]

    def backward_block(carry, block):
        query_block, allowed_block, log_block, grad_block = block
        scores = block_scores(query_block, allowed_block, key_table)
        probs = jnp.exp(scores - log_block[..., None])
        weights = probs.astype(jnp.bfloat16)
        value_grads = carry[1] + jnp.einsum(
            "htc,thd->chd", weights, grad_block, preferred_element_type=jnp.float32
        )
        grad_probs = jnp.einsum(
            "thd,chd->htc", grad_block, value_table, preferred_element_type=jnp.float32
        )
        grad_scores = (
            probs * (grad_probs - jnp.sum(grad_probs * probs, axis=-1, keepdims=True))
        ).astype(jnp.bfloat16)
        grad_query = jnp.einsum(
            "htc,chd->thd", grad_scores, key_table, preferred_element_type=jnp.float32
        ).astype(jnp.bfloat16)
        key_grads = carry[0] + jnp.einsum(
            "htc,thd->chd", grad_scores, query_block, preferred_element_type=jnp.float32
        )
        return ((key_grads, value_grads), grad_query.reshape(block_rows, local_heads * head_size))

    empty_grads = jnp.zeros((key_count, local_heads, head_size), jnp.float32)
    grad_blocks = grad_rows.reshape(block_count, block_rows, local_heads, head_size)
    (key_grads, value_grads), grad_queries = lax.scan(
        backward_block, (empty_grads, empty_grads), (query_blocks, allowed, log_totals, grad_blocks)
    )
    local_width = local_heads * head_size
    return (
        key_grads.reshape(key_count, local_width),
        value_grads.reshape(key_count, local_width),
        grad_queries.reshape(-1, local_width),
    )


def per_device(
    tokens,
    page_ids,
    image_of_page,
    memory,
    ln0_gain,
    ln0_bias,
    w_self_query,
    b_self_query,
    w_self_key,
    w_self_value,
    b_self_value,
    w_self_out,
    b_self_out,
    ln1_gain,
    ln1_bias,
    w_query,
    b_query,
    w_key,
    w_value,
    b_value,
    w_out,
    b_out,
    ln2_gain,
    ln2_bias,
    w_up,
    b_up,
    w_down,
    b_down,
    cotangent,
):
    row_count, width = tokens.shape
    image_count, memory_rows = (memory.shape[0], memory.shape[1])
    half_width = w_query.shape[1]
    local_heads = half_width // HEAD_WIDTH
    scale = 1.0 / math.sqrt(HEAD_WIDTH)
    block_rows = min(row_count, 512)
    block_count = row_count // block_rows
    own_rows = image_count * memory_rows
    key_count = own_rows + memory_rows
    input_values = tokens.astype(jnp.float32)
    hidden_zero, self_normed_rows, inverse_zero = layer_norm(input_values, ln0_gain, ln0_bias)
    hidden_zero = hidden_zero.astype(jnp.bfloat16)
    self_queries = (
        (jnp.dot(hidden_zero, w_self_query, preferred_element_type=jnp.float32) + b_self_query)
        * scale
    ).astype(jnp.bfloat16)
    self_key_rows = jnp.dot(hidden_zero, w_self_key, preferred_element_type=jnp.float32).astype(
        jnp.bfloat16
    )
    self_values = (
        jnp.dot(hidden_zero, w_self_value, preferred_element_type=jnp.float32) + b_self_value
    ).astype(jnp.bfloat16)
    last_mark = (page_ids == page_ids[row_count - 1]).astype(jnp.bfloat16)
    prior_keys, prior_values, prior_mark = shifted((self_key_rows, self_values, last_mark), "dp", 1)
    self_key_table = jnp.concatenate([prior_keys, self_key_rows], 0).reshape(
        2 * row_count, local_heads, HEAD_WIDTH
    )
    self_value_table = jnp.concatenate([prior_values, self_values], 0).reshape(
        2 * row_count, local_heads, HEAD_WIDTH
    )
    positions = jnp.arange(row_count, dtype=jnp.int32)
    own_ok = (page_ids[:, None] == page_ids[None, :]) & (positions[None, :] <= positions[:, None])
    prior_ok = (prior_mark[None, :] > 0.5) & (page_ids == page_ids[0])[:, None]
    self_allowed = jnp.concatenate([prior_ok, own_ok], 1).reshape(
        block_count, block_rows, 2 * row_count
    )
    self_query_blocks = self_queries.reshape(block_count, block_rows, local_heads, HEAD_WIDTH)
    self_attended, self_logs = attend_forward(
        self_query_blocks, self_allowed, self_key_table, self_value_table
    )
    self_branch = (
        core_sum(jnp.dot(self_attended, w_self_out, preferred_element_type=jnp.float32))
        + b_self_out
    )
    start = input_values + self_branch
    first_page = lax.axis_index("dp") * image_count
    local_page = page_ids - first_page
    picked = local_page[:, None] == jnp.arange(image_count, dtype=jnp.int32)[None, :]
    token_image = jnp.sum(jnp.where(picked, image_of_page[None, :], 0), axis=1)
    token_slot = jnp.where(local_page >= 0, token_image - first_page, image_count)
    key_slot = jnp.repeat(jnp.arange(image_count + 1, dtype=jnp.int32), memory_rows)
    allowed = (token_slot[:, None] == key_slot[None, :]).reshape(block_count, block_rows, key_count)
    last_image = image_of_page[image_count - 1] - first_page
    flat_memory = memory.reshape(own_rows, width)
    keys_here = jnp.dot(flat_memory, w_key, preferred_element_type=jnp.float32).astype(jnp.bfloat16)
    values_here = (
        jnp.dot(flat_memory, w_value, preferred_element_type=jnp.float32) + b_value
    ).astype(jnp.bfloat16)

    def tail_rows(matrix):
        return lax.dynamic_slice_in_dim(matrix, last_image * memory_rows, memory_rows, 0)

    prior_image_keys, prior_image_values = shifted(
        (tail_rows(keys_here), tail_rows(values_here)), "dp", 1
    )
    all_keys = jnp.concatenate([keys_here, prior_image_keys], 0).reshape(
        key_count, local_heads, HEAD_WIDTH
    )
    all_values = jnp.concatenate([values_here, prior_image_values], 0).reshape(
        key_count, local_heads, HEAD_WIDTH
    )
    hidden_one, normed_one, inverse_one = layer_norm(start, ln1_gain, ln1_bias)
    hidden_one = hidden_one.astype(jnp.bfloat16)
    queries = (
        (jnp.dot(hidden_one, w_query, preferred_element_type=jnp.float32) + b_query) * scale
    ).astype(jnp.bfloat16)
    query_blocks = queries.reshape(block_count, block_rows, local_heads, HEAD_WIDTH)
    attended, log_totals = attend_forward(query_blocks, allowed, all_keys, all_values)
    branch = (
        core_sum(jnp.dot(attended, w_out, preferred_element_type=jnp.float32)) + b_out
    )
    middle = start + branch
    hidden_two, normed_two, inverse_two = layer_norm(middle, ln2_gain, ln2_bias)
    hidden_two = hidden_two.astype(jnp.bfloat16)
    up_value = jnp.dot(hidden_two, w_up, preferred_element_type=jnp.float32) + b_up
    activated = jax.nn.gelu(up_value, approximate=False).astype(jnp.bfloat16)
    down_sum = core_sum(jnp.dot(activated, w_down, preferred_element_type=jnp.float32))
    layer_out = (middle + down_sum + b_down).astype(jnp.bfloat16)
    grad_outer = cotangent.astype(jnp.float32)
    grad_down = jnp.einsum("tf,td->fd", activated, cotangent, preferred_element_type=jnp.float32)
    down_bias_grad = jnp.sum(grad_outer, axis=0)
    grad_act = jnp.einsum("td,fd->tf", cotangent, w_down, preferred_element_type=jnp.float32)
    unused_value, gelu_back = jax.vjp(lambda inner: jax.nn.gelu(inner, approximate=False), up_value)
    grad_upvalue = gelu_back(grad_act)[0].astype(jnp.bfloat16)
    grad_up = jnp.einsum("td,tf->df", hidden_two, grad_upvalue, preferred_element_type=jnp.float32)
    up_bias_grad = jnp.sum(grad_upvalue.astype(jnp.float32), axis=0)
    grad_hidden_two = core_sum(
        jnp.einsum("tf,df->td", grad_upvalue, w_up, preferred_element_type=jnp.float32)
    )
    back_two, gain_two_grad, bias_two_grad = norm_back(
        grad_hidden_two, normed_two, inverse_two, ln2_gain
    )
    grad_middle = grad_outer + back_two
    grad_branch = grad_middle.astype(jnp.bfloat16)
    grad_out = jnp.einsum("th,td->hd", attended, grad_branch, preferred_element_type=jnp.float32)
    out_bias_grad = jnp.sum(grad_branch.astype(jnp.float32), axis=0)
    grad_attended = jnp.einsum(
        "td,hd->th", grad_branch, w_out, preferred_element_type=jnp.float32
    ).astype(jnp.bfloat16)
    key_grads, value_grads, grad_queries = attend_backward(
        query_blocks, allowed, log_totals, grad_attended, all_keys, all_values
    )
    returned_keys, returned_values = (
        shifted(key_grads[own_rows:].astype(jnp.bfloat16), "dp", -1).astype(jnp.float32),
        shifted(value_grads[own_rows:].astype(jnp.bfloat16), "dp", -1).astype(jnp.float32),
    )

    def add_back(local_part, returned):
        begin = last_image * memory_rows
        current = lax.dynamic_slice_in_dim(local_part, begin, memory_rows, 0)
        return lax.dynamic_update_slice_in_dim(local_part, current + returned, begin, 0)

    key_total = add_back(key_grads[:own_rows], returned_keys).astype(jnp.bfloat16)
    value_total = add_back(value_grads[:own_rows], returned_values).astype(jnp.bfloat16)
    grad_key = jnp.einsum("md,me->de", flat_memory, key_total, preferred_element_type=jnp.float32)
    grad_value = jnp.einsum(
        "md,me->de", flat_memory, value_total, preferred_element_type=jnp.float32
    )
    value_bias_grad = jnp.sum(value_total.astype(jnp.float32), axis=0)
    memory_part = jnp.einsum(
        "me,de->md", key_total, w_key, preferred_element_type=jnp.float32
    ) + jnp.einsum("me,de->md", value_total, w_value, preferred_element_type=jnp.float32)
    grad_query_w = (
        jnp.einsum("td,th->dh", hidden_one, grad_queries, preferred_element_type=jnp.float32)
        * scale
    )
    query_bias_grad = jnp.sum(grad_queries.astype(jnp.float32), axis=0) * scale
    hidden_part = (
        jnp.einsum("th,dh->td", grad_queries, w_query, preferred_element_type=jnp.float32) * scale
    )
    grad_hidden_one, grad_memory = core_sum(hidden_part), core_sum(memory_part)
    back_one, gain_one_grad, bias_one_grad = norm_back(
        grad_hidden_one, normed_one, inverse_one, ln1_gain
    )
    grad_start = grad_middle + back_one
    d_memory = grad_memory.reshape(image_count, memory_rows, width).astype(jnp.bfloat16)
    grad_start_low = grad_start.astype(jnp.bfloat16)
    grad_self_out = jnp.einsum(
        "th,td->hd", self_attended, grad_start_low, preferred_element_type=jnp.float32
    )
    self_out_bias_grad = jnp.sum(grad_start_low.astype(jnp.float32), axis=0)
    grad_self_attended = jnp.einsum(
        "td,hd->th", grad_start_low, w_self_out, preferred_element_type=jnp.float32
    ).astype(jnp.bfloat16)
    self_key_grads, self_value_grads, grad_self_queries = attend_backward(
        self_query_blocks,
        self_allowed,
        self_logs,
        grad_self_attended,
        self_key_table,
        self_value_table,
    )
    later_keys, later_values = (
        shifted(self_key_grads[:row_count].astype(jnp.bfloat16), "dp", -1).astype(jnp.float32),
        shifted(self_value_grads[:row_count].astype(jnp.bfloat16), "dp", -1).astype(jnp.float32),
    )
    self_key_total = (self_key_grads[row_count:] + later_keys).astype(jnp.bfloat16)
    self_value_total = (self_value_grads[row_count:] + later_values).astype(jnp.bfloat16)
    grad_self_query_w = (
        jnp.einsum("td,th->dh", hidden_zero, grad_self_queries, preferred_element_type=jnp.float32)
        * scale
    )
    self_query_bias_grad = jnp.sum(grad_self_queries.astype(jnp.float32), axis=0) * scale
    grad_self_key_w = jnp.einsum(
        "td,th->dh", hidden_zero, self_key_total, preferred_element_type=jnp.float32
    )
    grad_self_value_w = jnp.einsum(
        "td,th->dh", hidden_zero, self_value_total, preferred_element_type=jnp.float32
    )
    self_value_bias_grad = jnp.sum(self_value_total.astype(jnp.float32), axis=0)
    zero_part = (
        jnp.einsum("th,dh->td", grad_self_queries, w_self_query, preferred_element_type=jnp.float32)
        * scale
        + jnp.einsum("th,dh->td", self_key_total, w_self_key, preferred_element_type=jnp.float32)
        + jnp.einsum(
            "th,dh->td", self_value_total, w_self_value, preferred_element_type=jnp.float32
        )
    )
    grad_hidden_zero = core_sum(zero_part)
    back_zero, gain_zero_grad, bias_zero_grad = norm_back(
        grad_hidden_zero, self_normed_rows, inverse_zero, ln0_gain
    )
    d_tokens = (grad_start + back_zero).astype(jnp.bfloat16)
    (
        s_squery,
        self_key_spec,
        s_svalue,
        s_sout,
        summed_query,
        summed_key,
        summed_value,
        summed_out,
        summed_up,
        summed_down,
    ) = (
        scattered(grad_self_query_w, 0),
        scattered(grad_self_key_w, 0),
        scattered(grad_self_value_w, 0),
        scattered(grad_self_out, 1),
        scattered(grad_query_w, 0),
        scattered(grad_key, 0),
        scattered(grad_value, 0),
        scattered(grad_out, 1),
        scattered(grad_up, 0),
        scattered(grad_down, 1),
    )
    small_sums = butterfly_sum(
        (
            gain_zero_grad,
            bias_zero_grad,
            self_query_bias_grad,
            self_value_bias_grad,
            self_out_bias_grad,
            gain_one_grad,
            bias_one_grad,
            query_bias_grad,
            value_bias_grad,
            out_bias_grad,
            gain_two_grad,
            bias_two_grad,
            up_bias_grad,
            down_bias_grad,
        )
    )
    return (
        layer_out,
        d_tokens,
        d_memory,
        small_sums[0],
        small_sums[1],
        s_squery,
        small_sums[2],
        self_key_spec,
        s_svalue,
        small_sums[3],
        s_sout,
        small_sums[4],
        small_sums[5],
        small_sums[6],
        summed_query,
        small_sums[7],
        summed_key,
        summed_value,
        small_sums[8],
        summed_out,
        small_sums[9],
        small_sums[10],
        small_sums[11],
        summed_up,
        small_sums[12],
        summed_down,
        small_sums[13],
    )


def solution(mesh):
    in_specs = (
        P("dp", None),
        P("dp"),
        P("dp"),
        P("dp", None, None),
        P(),
        P(),
        P(None, "tensor"),
        P("tensor"),
        P(None, "tensor"),
        P(None, "tensor"),
        P("tensor"),
        P("tensor", None),
        P(),
        P(),
        P(),
        P(None, "tensor"),
        P("tensor"),
        P(None, "tensor"),
        P(None, "tensor"),
        P("tensor"),
        P("tensor", None),
        P(),
        P(),
        P(),
        P(None, "tensor"),
        P("tensor"),
        P("tensor", None),
        P(),
        P("dp", None),
    )
    out_specs = (
        P("dp", None),
        P("dp", None),
        P("dp", None, None),
        P(),
        P(),
        P("dp", "tensor"),
        P("tensor"),
        P("dp", "tensor"),
        P("dp", "tensor"),
        P("tensor"),
        P("tensor", "dp"),
        P(),
        P(),
        P(),
        P("dp", "tensor"),
        P("tensor"),
        P("dp", "tensor"),
        P("dp", "tensor"),
        P("tensor"),
        P("tensor", "dp"),
        P(),
        P(),
        P(),
        P("dp", "tensor"),
        P("tensor"),
        P("tensor", "dp"),
        P(),
    )
    return jax.shard_map(
        per_device, mesh=mesh, in_specs=in_specs, out_specs=out_specs, check_vma=False
    )
```

```python
import functools
import math

import jax
import jax.numpy as jnp
from jax import lax
from jax.experimental import pallas as pl
from jax.experimental.pallas import tpu as pltpu
from jax.sharding import PartitionSpec as P

HEAD_WIDTH = 64


EPSILON = 1e-05


def shifted(value, axis, steps):
    count = lax.axis_size(axis)
    initial, last = (max(0, -steps), min(count, count - steps))
    return lax.ppermute(value, axis, [(source, source + steps) for source in range(initial, last)])


def core_sum(partial):
    low = partial.astype(jnp.bfloat16)
    other = lax.ppermute(low, "tensor", [(0, 1), (1, 0)])
    return low.astype(jnp.float32) + other.astype(jnp.float32)


def butterfly_sum(vectors):
    sizes = [vector.shape[0] for vector in vectors]
    total = jnp.concatenate(vectors).reshape(-1, 128)
    count = lax.axis_size("dp")
    bit = 1
    while bit < count:
        total = total + lax.ppermute(total, "dp", [(i, i ^ bit) for i in range(count)])
        bit *= 2
    flat = total.reshape(-1)
    pieces, at = [], 0
    for size in sizes:
        pieces.append(flat[at : at + size])
        at += size
    return pieces


def scattered(gradient, dimension):
    return lax.psum_scatter(
        gradient.astype(jnp.bfloat16), "dp", scatter_dimension=dimension, tiled=True
    ).astype(jnp.float32)


def layer_norm(values, gain, bias):
    mean = jnp.mean(values, axis=-1, keepdims=True)
    centered = values - mean
    inverse = lax.rsqrt(jnp.mean(centered * centered, axis=-1, keepdims=True) + EPSILON)
    normed = centered * inverse
    return (normed * gain + bias, normed, inverse)


def norm_back(grad, normed, inverse, gain):
    scaled = grad * gain
    inner = (
        scaled
        - jnp.mean(scaled, axis=-1, keepdims=True)
        - normed * jnp.mean(scaled * normed, axis=-1, keepdims=True)
    )
    return (inner * inverse, jnp.sum(grad * normed, axis=0), jnp.sum(grad, axis=0))


BF = jnp.bfloat16
F32 = jnp.float32
NEG = -1e30
TILE = 256
PAIR = 2 * HEAD_WIDTH
VMEM_LIMIT = 60 * 1024 * 1024


def nt(left, right):
    return lax.dot_general(left, right, (((1,), (1,)), ((), ())), preferred_element_type=F32)


def nn(left, right):
    return lax.dot_general(left, right, (((1,), (0,)), ((), ())), preferred_element_type=F32)


def head_half(pair, half):
    lane = lax.broadcasted_iota(jnp.int32, pair.shape, 1)
    keep = lane < HEAD_WIDTH if half == 0 else lane >= HEAD_WIDTH
    return jnp.where(keep, pair, jnp.zeros_like(pair))


def span(index, size=TILE):
    return pl.ds(pl.multiple_of(index * size, size), size)


HEAD_ROWS = 80


def column_max(values):
    rows = values.shape[0]
    groups = max(1, rows // 64)
    step = -(-(rows // groups) // 8) * 8
    parts = []
    at = 0
    while at < rows:
        end = min(rows, at + step)
        parts.append(jnp.max(values[at:end], axis=0, keepdims=True))
        at = end
    while len(parts) > 1:
        parts = [jnp.maximum(*parts[i : i + 2]) if i + 1 < len(parts) else parts[i] for i in range(0, len(parts), 2)]
    return parts[0]


def extended(values, target, columns):
    turned = values.T
    extra = jnp.where(lax.broadcasted_iota(jnp.int32, (HEAD_ROWS - HEAD_WIDTH, turned.shape[1]), 0) == 0, 1.0, 0.0).astype(BF)
    for h in range(turned.shape[0] // HEAD_WIDTH):
        base = h * HEAD_ROWS
        target[base : base + HEAD_WIDTH, columns] = turned[h * HEAD_WIDTH : (h + 1) * HEAD_WIDTH, :]
        target[base + HEAD_WIDTH : base + HEAD_ROWS, columns] = extra


def lane_rows(i):
    return i * TILE + lax.broadcasted_iota(jnp.int32, (1, TILE), 1)


def self_forward_body(meta, q_ref, kp_ref, k_ref, vp_ref, v_ref, o_ref, log_ref,
                      vpt, vt, qm, bias, m_s, acc, done, scores):
    rows = q_ref.shape[0]
    pairs = q_ref.shape[1] // PAIR
    b1, b2, p0 = meta[0], meta[1], meta[2]
    tiles = rows // TILE
    first_prior = p0 // TILE
    prior_rows = (b1 + TILE - 1) // TILE

    def turn_own(j, c):
        extended(v_ref[span(j), :], vt, span(j))
        return c

    lax.fori_loop(0, tiles, turn_own, 0)

    def turn_prior(j, c):
        extended(vp_ref[span(j), :], vpt, span(j))
        return c

    lax.fori_loop(jnp.where(b1 > 0, first_prior, tiles), tiles, turn_prior, 0)

    def key_step(keys, values_t, j):
        for pair in range(pairs):
            key_pair = keys[span(j), pair * PAIR : pair * PAIR + PAIR]
            for half in range(2):
                scores[2 * pair + half] = nt(key_pair, qm[2 * pair + half])
        for pair in range(pairs):
            for half in range(2):
                h = 2 * pair + half
                heads = slice(h * HEAD_ROWS, (h + 1) * HEAD_ROWS)
                s = scores[h] + bias[...]
                m_old = m_s[h : h + 1, :]
                m_new = jnp.maximum(m_old, column_max(s))
                alpha = jnp.exp(m_old - m_new)
                e = jnp.exp(s - m_new)
                m_s[h : h + 1, :] = m_new
                acc[heads, :] = acc[heads, :] * alpha + nn(values_t[heads, span(j)], e.astype(BF))

    def row_tile(i, c):
        t = lane_rows(i)
        start = jnp.where(t < b1, 0, jnp.where(t < b2, b1, b2))
        for pair in range(pairs):
            q_pair = q_ref[span(i), pair * PAIR : pair * PAIR + PAIR]
            for half in range(2):
                qm[2 * pair + half] = head_half(q_pair, half)
        m_s[...] = jnp.full_like(m_s, NEG)
        acc[...] = jnp.zeros_like(acc)

        def prior(j, c2):
            r = j * TILE + lax.broadcasted_iota(jnp.int32, (TILE, TILE), 0)
            bias[...] = jnp.where((r >= p0) & (t < b1), 0.0, NEG)
            key_step(kp_ref, vpt, j)
            return c2

        lax.fori_loop(jnp.where(i < prior_rows, first_prior, tiles), tiles, prior, 0)
        t_first = i * TILE
        lowest = jnp.where(t_first < b1, 0, jnp.where(t_first < b2, b1, b2))

        def own(j, c2):
            r = j * TILE + lax.broadcasted_iota(jnp.int32, (TILE, TILE), 0)
            bias[...] = jnp.where((r <= t) & (r >= start), 0.0, NEG)
            key_step(k_ref, vt, j)
            return c2

        lax.fori_loop(lowest // TILE, i + 1, own, 0)
        for h in range(2 * pairs):
            base = h * HEAD_ROWS
            total = acc[base + HEAD_WIDTH : base + HEAD_WIDTH + 1, :]
            log_ref[h : h + 1, span(i)] = m_s[h : h + 1, :] + jnp.log(total)
            done[h * HEAD_WIDTH : (h + 1) * HEAD_WIDTH, :] = acc[base : base + HEAD_WIDTH, :] * (1.0 / total)
        o_ref[span(i), :] = done[...].T.astype(BF)
        return c

    lax.fori_loop(0, tiles, row_tile, 0)


SMEM_SPEC = pl.BlockSpec(memory_space=pltpu.SMEM)
VMEM_SPEC = pl.BlockSpec(memory_space=pltpu.VMEM)


def self_forward(meta, q, k_prior, k, v_prior, v):
    rows, width = q.shape
    heads = width // HEAD_WIDTH
    return pl.pallas_call(
        self_forward_body,
        out_shape=(jax.ShapeDtypeStruct((rows, width), BF), jax.ShapeDtypeStruct((heads, rows), F32)),
        in_specs=[SMEM_SPEC] + [VMEM_SPEC] * 5,
        out_specs=(VMEM_SPEC, VMEM_SPEC),
        scratch_shapes=[
            pltpu.VMEM((heads * HEAD_ROWS, rows), BF),
            pltpu.VMEM((heads * HEAD_ROWS, rows), BF),
            pltpu.VMEM((heads, TILE, PAIR), BF),
            pltpu.VMEM((TILE, TILE), F32),
            pltpu.VMEM((heads, TILE), F32),
            pltpu.VMEM((heads * HEAD_ROWS, TILE), F32),
            pltpu.VMEM((width, TILE), F32),
            pltpu.VMEM((heads, TILE, TILE), F32),
        ],
        compiler_params=pltpu.CompilerParams(vmem_limit_bytes=VMEM_LIMIT),
        cost_estimate=pl.CostEstimate(flops=2 * 2 * rows * rows * width, bytes_accessed=8 * rows * width * 2, transcendentals=rows * rows * heads),
        name="self_forward",
    )(meta, q, k_prior, k, v_prior, v)


def grad_rows(do_ref, o_ref, i, width):
    heads = width // HEAD_WIDTH
    product = do_ref[span(i), :].astype(F32) * o_ref[span(i), :].astype(F32)
    high = product.astype(BF)
    low = (product - high.astype(F32)).astype(BF)
    head = lax.broadcasted_iota(jnp.int32, (heads, width), 0)
    column = lax.broadcasted_iota(jnp.int32, (heads, width), 1) // HEAD_WIDTH
    pick = jnp.where(head == column, 1.0, 0.0).astype(BF)
    return nt(pick, high) + nt(pick, low)


def halves(source, i, target, pairs):
    for pair in range(pairs):
        value = source[span(i), pair * PAIR : pair * PAIR + PAIR]
        for half in range(2):
            target[2 * pair + half] = head_half(value, half)


def grad_step(pairs, keys, values, keys_t, key_slice, key_lanes, qm, dom, shift, delta, bias, dk, dv, dqt, scores, grads):
    for pair in range(pairs):
        cols = slice(pair * PAIR, pair * PAIR + PAIR)
        key_pair = keys[key_slice, cols]
        value_pair = values[key_slice, cols]
        for half in range(2):
            h = 2 * pair + half
            scores[h] = nt(key_pair, qm[h])
            grads[h] = nt(value_pair, dom[h])
    for pair in range(pairs):
        cols = slice(pair * PAIR, pair * PAIR + PAIR)
        dv_pair = dv[key_slice, cols]
        dk_pair = dk[key_slice, cols]
        for half in range(2):
            h = 2 * pair + half
            heads = slice(h * HEAD_WIDTH, (h + 1) * HEAD_WIDTH)
            s = scores[h]
            if bias is not None:
                s = s + bias[...]
            p = jnp.exp(s - shift[h : h + 1, :])
            dp = grads[h]
            ds = (p * (dp - delta[h : h + 1, :])).astype(BF)
            dv_pair = dv_pair + nn(p.astype(BF), dom[h])
            dk_pair = dk_pair + nn(ds, qm[h])
            dqt[heads, :] = dqt[heads, :] + nn(keys_t[heads, key_lanes], ds)
        dv[key_slice, cols] = dv_pair
        dk[key_slice, cols] = dk_pair


def self_prior_back_body(meta, q_ref, do_ref, o_ref, log_ref, k_ref, v_ref, dk_ref, dv_ref, dq_ref,
                         kt, qm, dom, bias, delta, shift, dqt, dk, dv, scores, grads):
    rows, width = q_ref.shape
    pairs = width // PAIR
    b1, p0 = meta[0], meta[2]
    tiles = rows // TILE
    first_prior = p0 // TILE
    prior_rows = (b1 + TILE - 1) // TILE
    dk[...] = jnp.zeros_like(dk)
    dv[...] = jnp.zeros_like(dv)

    def turn(j, c):
        kt[:, span(j)] = k_ref[span(j), :].T
        return c

    lax.fori_loop(jnp.where(b1 > 0, first_prior, tiles), tiles, turn, 0)

    def row_tile(i, c):
        dqt[...] = jnp.zeros_like(dqt)
        t = lane_rows(i)

        @pl.when(i < prior_rows)
        def _():
            halves(q_ref, i, qm, pairs)
            halves(do_ref, i, dom, pairs)
            delta[...] = grad_rows(do_ref, o_ref, i, width)
            shift[...] = log_ref[:, span(i)]

        def prior(j, c2):
            r = j * TILE + lax.broadcasted_iota(jnp.int32, (TILE, TILE), 0)
            bias[...] = jnp.where((r >= p0) & (t < b1), 0.0, NEG)
            grad_step(pairs, k_ref, v_ref, kt, span(j), span(j), qm, dom, shift, delta, bias, dk, dv, dqt, scores, grads)
            return c2

        lax.fori_loop(jnp.where(i < prior_rows, first_prior, tiles), tiles, prior, 0)
        dq_ref[span(i), :] = dqt[...].T
        return c

    lax.fori_loop(0, tiles, row_tile, 0)
    dk_ref[...] = dk[...].astype(BF)
    dv_ref[...] = dv[...].astype(BF)


def self_own_back_body(meta, q_ref, do_ref, o_ref, log_ref, k_ref, v_ref, dqp_ref, dk_ref, dv_ref, dq_ref,
                       kt, qm, dom, bias, delta, shift, dqt, dk, dv, scores, grads):
    rows, width = q_ref.shape
    pairs = width // PAIR
    b1, b2 = meta[0], meta[1]
    tiles = rows // TILE
    dk[...] = jnp.zeros_like(dk)
    dv[...] = jnp.zeros_like(dv)

    def turn(j, c):
        kt[:, span(j)] = k_ref[span(j), :].T
        return c

    lax.fori_loop(0, tiles, turn, 0)

    def row_tile(i, c):
        dqt[...] = jnp.zeros_like(dqt)
        t = lane_rows(i)
        start = jnp.where(t < b1, 0, jnp.where(t < b2, b1, b2))
        halves(q_ref, i, qm, pairs)
        halves(do_ref, i, dom, pairs)
        delta[...] = grad_rows(do_ref, o_ref, i, width)
        shift[...] = log_ref[:, span(i)]
        t_first = i * TILE
        lowest = jnp.where(t_first < b1, 0, jnp.where(t_first < b2, b1, b2))

        def own(j, c2):
            r = j * TILE + lax.broadcasted_iota(jnp.int32, (TILE, TILE), 0)
            bias[...] = jnp.where((r <= t) & (r >= start), 0.0, NEG)
            grad_step(pairs, k_ref, v_ref, kt, span(j), span(j), qm, dom, shift, delta, bias, dk, dv, dqt, scores, grads)
            return c2

        lax.fori_loop(lowest // TILE, i + 1, own, 0)
        dq_ref[span(i), :] = (dqp_ref[span(i), :] + dqt[...].T).astype(BF)
        return c

    lax.fori_loop(0, tiles, row_tile, 0)
    dk_ref[...] = dk[...]
    dv_ref[...] = dv[...]


def self_back_scratch(rows, width):
    heads = width // HEAD_WIDTH
    return [
        pltpu.VMEM((width, rows), BF),
        pltpu.VMEM((heads, TILE, PAIR), BF),
        pltpu.VMEM((heads, TILE, PAIR), BF),
        pltpu.VMEM((TILE, TILE), F32),
        pltpu.VMEM((heads, TILE), F32),
        pltpu.VMEM((heads, TILE), F32),
        pltpu.VMEM((width, TILE), F32),
        pltpu.VMEM((rows, width), F32),
        pltpu.VMEM((rows, width), F32),
        pltpu.VMEM((heads, TILE, TILE), F32),
        pltpu.VMEM((heads, TILE, TILE), F32),
    ]


def self_prior_back(meta, q, do, o, logs, k_prior, v_prior):
    rows, width = q.shape
    return pl.pallas_call(
        self_prior_back_body,
        out_shape=(jax.ShapeDtypeStruct((rows, width), BF), jax.ShapeDtypeStruct((rows, width), BF),
                   jax.ShapeDtypeStruct((rows, width), F32)),
        in_specs=[SMEM_SPEC] + [VMEM_SPEC] * 6,
        out_specs=(VMEM_SPEC,) * 3,
        scratch_shapes=self_back_scratch(rows, width),
        compiler_params=pltpu.CompilerParams(vmem_limit_bytes=VMEM_LIMIT),
        cost_estimate=pl.CostEstimate(flops=3 * rows * rows * width, bytes_accessed=8 * rows * width * 2, transcendentals=rows * rows * 4),
        name="self_prior_back",
    )(meta, q, do, o, logs, k_prior, v_prior)


def self_own_back(meta, q, do, o, logs, k, v, dq_prior):
    rows, width = q.shape
    return pl.pallas_call(
        self_own_back_body,
        out_shape=(jax.ShapeDtypeStruct((rows, width), F32), jax.ShapeDtypeStruct((rows, width), F32),
                   jax.ShapeDtypeStruct((rows, width), BF)),
        in_specs=[SMEM_SPEC] + [VMEM_SPEC] * 7,
        out_specs=(VMEM_SPEC,) * 3,
        scratch_shapes=self_back_scratch(rows, width),
        compiler_params=pltpu.CompilerParams(vmem_limit_bytes=VMEM_LIMIT),
        cost_estimate=pl.CostEstimate(flops=5 * rows * rows * width, bytes_accessed=8 * rows * width * 2, transcendentals=rows * rows * 4),
        name="self_own_back",
    )(meta, q, do, o, logs, k, v, dq_prior)


def segments(meta, rows):
    return ((0, meta[0], meta[3]), (meta[0], meta[1], meta[4]), (meta[1], rows, meta[5]))


def cross_forward_body(used, meta, q_ref, k_ref, v_ref, o_ref, log_ref, vt, qm, acc, scores):
    rows, width = q_ref.shape
    pairs = width // PAIR
    padded = k_ref.shape[0] // 3
    for slot in range(3):
        extended(v_ref[slot * padded : (slot + 1) * padded, :], vt.at[slot], slice(None))
    for first, last, slot in segments(meta, rows):
        keys = pl.ds(pl.multiple_of(slot * padded, 16), padded)

        def tile(i, c):
            halves(q_ref, i, qm, pairs)
            t = lane_rows(i)
            inside = (t >= first) & (t < last)
            for pair in range(pairs):
                key_pair = k_ref[keys, pair * PAIR : pair * PAIR + PAIR]
                for half in range(2):
                    scores[2 * pair + half] = nt(key_pair, qm[2 * pair + half])
            for pair in range(pairs):
                for half in range(2):
                    h = 2 * pair + half
                    heads = slice(h * HEAD_WIDTH, (h + 1) * HEAD_WIDTH)
                    s = scores[h]
                    if used < padded:
                        row = lax.broadcasted_iota(jnp.int32, s.shape, 0)
                        s = jnp.where(row < used, s, NEG)
                    m = column_max(s)
                    e = jnp.exp(s - m)
                    mixed = nn(vt[slot, h * HEAD_ROWS : (h + 1) * HEAD_ROWS, :], e.astype(BF))
                    total = mixed[HEAD_WIDTH : HEAD_WIDTH + 1, :]
                    acc[heads, :] = mixed[:HEAD_WIDTH, :] * (1.0 / total)
                    log_ref[h : h + 1, span(i)] = jnp.where(
                        inside, m + jnp.log(total), log_ref[h : h + 1, span(i)]
                    )
            column = i * TILE + lax.broadcasted_iota(jnp.int32, (TILE, width), 0)
            keep = (column >= first) & (column < last)
            o_ref[span(i), :] = jnp.where(keep, acc[...].T, o_ref[span(i), :].astype(F32)).astype(BF)
            return c

        lax.fori_loop(first // TILE, jnp.where(last > first, (last + TILE - 1) // TILE, 0), tile, 0)


def cross_forward(used, meta, q, k, v):
    rows, width = q.shape
    heads = width // HEAD_WIDTH
    padded = k.shape[0] // 3
    return pl.pallas_call(
        functools.partial(cross_forward_body, used),
        out_shape=(jax.ShapeDtypeStruct((rows, width), BF), jax.ShapeDtypeStruct((heads, rows), F32)),
        in_specs=[SMEM_SPEC] + [VMEM_SPEC] * 3,
        out_specs=(VMEM_SPEC, VMEM_SPEC),
        scratch_shapes=[
            pltpu.VMEM((3, heads * HEAD_ROWS, padded), BF),
            pltpu.VMEM((heads, TILE, PAIR), BF),
            pltpu.VMEM((width, TILE), F32),
            pltpu.VMEM((heads, padded, TILE), F32),
        ],
        compiler_params=pltpu.CompilerParams(vmem_limit_bytes=VMEM_LIMIT),
        cost_estimate=pl.CostEstimate(flops=4 * rows * padded * width, bytes_accessed=8 * rows * width * 2, transcendentals=rows * padded * heads),
        name="cross_forward",
    )(meta, q, k, v)


def cross_back_body(used, meta, q_ref, do_ref, o_ref, log_ref, k_ref, v_ref, dk_ref, dv_ref, dq_ref,
                    kt, qm, dom, delta, shift, dqt, dk, dv, scores, grads):
    rows, width = q_ref.shape
    pairs = width // PAIR
    padded = k_ref.shape[0] // 3
    dk[...] = jnp.zeros_like(dk)
    dv[...] = jnp.zeros_like(dv)
    for slot in range(3):
        kt[slot] = k_ref[slot * padded : (slot + 1) * padded, :].T
    for first, last, slot in segments(meta, rows):
        keys = pl.ds(pl.multiple_of(slot * padded, 16), padded)

        def tile(i, c):
            halves(q_ref, i, qm, pairs)
            halves(do_ref, i, dom, pairs)
            t = lane_rows(i)
            inside = (t >= first) & (t < last)
            delta[...] = grad_rows(do_ref, o_ref, i, width)
            shift[...] = jnp.where(inside, log_ref[:, span(i)], -NEG)
            dqt[...] = jnp.zeros_like(dqt)
            grad_step(pairs, k_ref, v_ref, kt.at[slot], keys, slice(None), qm, dom, shift, delta, None, dk, dv, dqt, scores, grads)
            column = i * TILE + lax.broadcasted_iota(jnp.int32, (TILE, width), 0)
            keep = (column >= first) & (column < last)
            dq_ref[span(i), :] = jnp.where(keep, dqt[...].T, dq_ref[span(i), :].astype(F32)).astype(BF)
            return c

        lax.fori_loop(first // TILE, jnp.where(last > first, (last + TILE - 1) // TILE, 0), tile, 0)
    inner = lax.broadcasted_iota(jnp.int32, (padded, width), 0) < used
    for slot in range(3):
        part = slice(slot * padded, (slot + 1) * padded)
        dk_ref[part, :] = jnp.where(inner, dk[part, :], 0.0).astype(BF)
        dv_ref[part, :] = jnp.where(inner, dv[part, :], 0.0).astype(BF)


def cross_back(used, meta, q, do, o, logs, k, v):
    rows, width = q.shape
    heads = width // HEAD_WIDTH
    padded = k.shape[0] // 3
    return pl.pallas_call(
        functools.partial(cross_back_body, used),
        out_shape=(jax.ShapeDtypeStruct(k.shape, BF), jax.ShapeDtypeStruct(k.shape, BF),
                   jax.ShapeDtypeStruct((rows, width), BF)),
        in_specs=[SMEM_SPEC] + [VMEM_SPEC] * 6,
        out_specs=(VMEM_SPEC,) * 3,
        scratch_shapes=[
            pltpu.VMEM((3, width, padded), BF),
            pltpu.VMEM((heads, TILE, PAIR), BF),
            pltpu.VMEM((heads, TILE, PAIR), BF),
            pltpu.VMEM((heads, TILE), F32),
            pltpu.VMEM((heads, TILE), F32),
            pltpu.VMEM((width, TILE), F32),
            pltpu.VMEM(k.shape, F32),
            pltpu.VMEM(k.shape, F32),
            pltpu.VMEM((heads, padded, TILE), F32),
            pltpu.VMEM((heads, padded, TILE), F32),
        ],
        compiler_params=pltpu.CompilerParams(vmem_limit_bytes=VMEM_LIMIT),
        cost_estimate=pl.CostEstimate(flops=10 * rows * padded * width, bytes_accessed=12 * rows * width * 2, transcendentals=rows * padded * heads),
        name="cross_back",
    )(meta, q, do, o, logs, k, v)


def per_device(
    tokens,
    page_ids,
    image_of_page,
    memory,
    ln0_gain,
    ln0_bias,
    w_self_query,
    b_self_query,
    w_self_key,
    w_self_value,
    b_self_value,
    w_self_out,
    b_self_out,
    ln1_gain,
    ln1_bias,
    w_query,
    b_query,
    w_key,
    w_value,
    b_value,
    w_out,
    b_out,
    ln2_gain,
    ln2_bias,
    w_up,
    b_up,
    w_down,
    b_down,
    cotangent,
):
    row_count, width = tokens.shape
    image_count, memory_rows = (memory.shape[0], memory.shape[1])
    half_width = w_query.shape[1]
    scale = 1.0 / math.sqrt(HEAD_WIDTH)
    padded_rows = -(-memory_rows // 16) * 16
    own_rows = image_count * padded_rows
    first_page = lax.axis_index("dp") * image_count
    local_page = page_ids - first_page
    begins = [jnp.sum((local_page < page).astype(jnp.int32)) for page in range(image_count)]
    prior_begin = shifted(jnp.full((128,), begins[1], jnp.int32), "dp", 1)[0]
    slots = [jnp.int32(image_count)] + [image_of_page[page] - first_page for page in range(image_count)]
    meta = jnp.stack(begins + [prior_begin] + slots).astype(jnp.int32)
    input_values = tokens.astype(jnp.float32)
    hidden_zero, self_normed_rows, inverse_zero = layer_norm(input_values, ln0_gain, ln0_bias)
    hidden_zero = hidden_zero.astype(jnp.bfloat16)
    self_queries = (
        (jnp.dot(hidden_zero, w_self_query, preferred_element_type=jnp.float32) + b_self_query)
        * scale
    ).astype(jnp.bfloat16)
    self_key_rows = jnp.dot(hidden_zero, w_self_key, preferred_element_type=jnp.float32).astype(
        jnp.bfloat16
    )
    self_values = (
        jnp.dot(hidden_zero, w_self_value, preferred_element_type=jnp.float32) + b_self_value
    ).astype(jnp.bfloat16)
    prior_keys, prior_values = shifted((self_key_rows, self_values), "dp", 1)
    self_attended, self_logs = self_forward(
        meta, self_queries, prior_keys, self_key_rows, prior_values, self_values
    )
    self_branch = (
        core_sum(jnp.dot(self_attended, w_self_out, preferred_element_type=jnp.float32))
        + b_self_out
    )
    start = input_values + self_branch
    last_image = image_of_page[image_count - 1] - first_page
    flat_memory = jnp.pad(memory, ((0, 0), (0, padded_rows - memory_rows), (0, 0))).reshape(own_rows, width)
    keys_here = jnp.dot(flat_memory, w_key, preferred_element_type=jnp.float32).astype(jnp.bfloat16)
    values_here = (
        jnp.dot(flat_memory, w_value, preferred_element_type=jnp.float32) + b_value
    ).astype(jnp.bfloat16)

    def tail_rows(matrix):
        return lax.dynamic_slice_in_dim(matrix, last_image * padded_rows, padded_rows, 0)

    prior_image_keys, prior_image_values = shifted(
        (tail_rows(keys_here), tail_rows(values_here)), "dp", 1
    )
    all_keys = jnp.concatenate([keys_here, prior_image_keys], 0)
    all_values = jnp.concatenate([values_here, prior_image_values], 0)
    hidden_one, normed_one, inverse_one = layer_norm(start, ln1_gain, ln1_bias)
    hidden_one = hidden_one.astype(jnp.bfloat16)
    queries = (
        (jnp.dot(hidden_one, w_query, preferred_element_type=jnp.float32) + b_query) * scale
    ).astype(jnp.bfloat16)
    attended, log_totals = cross_forward(memory_rows, meta, queries, all_keys, all_values)
    branch = (
        core_sum(jnp.dot(attended, w_out, preferred_element_type=jnp.float32)) + b_out
    )
    middle = start + branch
    hidden_two, normed_two, inverse_two = layer_norm(middle, ln2_gain, ln2_bias)
    hidden_two = hidden_two.astype(jnp.bfloat16)
    up_value = jnp.dot(hidden_two, w_up, preferred_element_type=jnp.float32) + b_up
    activated = jax.nn.gelu(up_value, approximate=False).astype(jnp.bfloat16)
    down_sum = core_sum(jnp.dot(activated, w_down, preferred_element_type=jnp.float32))
    layer_out = (middle + down_sum + b_down).astype(jnp.bfloat16)
    grad_outer = cotangent.astype(jnp.float32)
    grad_down = jnp.einsum("tf,td->fd", activated, cotangent, preferred_element_type=jnp.float32)
    down_bias_grad = jnp.sum(grad_outer, axis=0)
    grad_act = jnp.einsum("td,fd->tf", cotangent, w_down, preferred_element_type=jnp.float32)
    unused_value, gelu_back = jax.vjp(lambda inner: jax.nn.gelu(inner, approximate=False), up_value)
    grad_upvalue = gelu_back(grad_act)[0].astype(jnp.bfloat16)
    grad_up = jnp.einsum("td,tf->df", hidden_two, grad_upvalue, preferred_element_type=jnp.float32)
    up_bias_grad = jnp.sum(grad_upvalue.astype(jnp.float32), axis=0)
    grad_hidden_two = core_sum(
        jnp.einsum("tf,df->td", grad_upvalue, w_up, preferred_element_type=jnp.float32)
    )
    back_two, gain_two_grad, bias_two_grad = norm_back(
        grad_hidden_two, normed_two, inverse_two, ln2_gain
    )
    grad_middle = grad_outer + back_two
    grad_branch = grad_middle.astype(jnp.bfloat16)
    grad_out = jnp.einsum("th,td->hd", attended, grad_branch, preferred_element_type=jnp.float32)
    out_bias_grad = jnp.sum(grad_branch.astype(jnp.float32), axis=0)
    grad_attended = jnp.einsum(
        "td,hd->th", grad_branch, w_out, preferred_element_type=jnp.float32
    ).astype(jnp.bfloat16)
    key_grads, value_grads, grad_queries = cross_back(
        memory_rows, meta, queries, grad_attended, attended, log_totals, all_keys, all_values
    )
    returned_keys, returned_values = (
        shifted(key_grads[own_rows:].astype(jnp.bfloat16), "dp", -1).astype(jnp.float32),
        shifted(value_grads[own_rows:].astype(jnp.bfloat16), "dp", -1).astype(jnp.float32),
    )

    def add_back(local_part, returned):
        begin = last_image * padded_rows
        current = lax.dynamic_slice_in_dim(local_part, begin, padded_rows, 0)
        return lax.dynamic_update_slice_in_dim(local_part, current + returned, begin, 0)

    key_total = add_back(key_grads[:own_rows].astype(jnp.float32), returned_keys).astype(jnp.bfloat16)
    value_total = add_back(value_grads[:own_rows].astype(jnp.float32), returned_values).astype(jnp.bfloat16)
    grad_key = jnp.einsum("md,me->de", flat_memory, key_total, preferred_element_type=jnp.float32)
    grad_value = jnp.einsum(
        "md,me->de", flat_memory, value_total, preferred_element_type=jnp.float32
    )
    value_bias_grad = jnp.sum(value_total.astype(jnp.float32), axis=0)
    memory_part = jnp.einsum(
        "me,de->md", key_total, w_key, preferred_element_type=jnp.float32
    ) + jnp.einsum("me,de->md", value_total, w_value, preferred_element_type=jnp.float32)
    grad_query_w = (
        jnp.einsum("td,th->dh", hidden_one, grad_queries, preferred_element_type=jnp.float32)
        * scale
    )
    query_bias_grad = jnp.sum(grad_queries.astype(jnp.float32), axis=0) * scale
    hidden_part = (
        jnp.einsum("th,dh->td", grad_queries, w_query, preferred_element_type=jnp.float32) * scale
    )
    grad_hidden_one, grad_memory = core_sum(hidden_part), core_sum(memory_part)
    back_one, gain_one_grad, bias_one_grad = norm_back(
        grad_hidden_one, normed_one, inverse_one, ln1_gain
    )
    grad_start = grad_middle + back_one
    d_memory = grad_memory.reshape(image_count, padded_rows, width)[:, :memory_rows].astype(jnp.bfloat16)
    grad_start_low = grad_start.astype(jnp.bfloat16)
    grad_self_out = jnp.einsum(
        "th,td->hd", self_attended, grad_start_low, preferred_element_type=jnp.float32
    )
    self_out_bias_grad = jnp.sum(grad_start_low.astype(jnp.float32), axis=0)
    grad_self_attended = jnp.einsum(
        "td,hd->th", grad_start_low, w_self_out, preferred_element_type=jnp.float32
    ).astype(jnp.bfloat16)
    prior_key_grads, prior_value_grads, prior_query_grads = self_prior_back(
        meta, self_queries, grad_self_attended, self_attended, self_logs, prior_keys, prior_values
    )
    later_keys, later_values = shifted((prior_key_grads, prior_value_grads), "dp", -1)
    self_key_grads, self_value_grads, grad_self_queries = self_own_back(
        meta,
        self_queries,
        grad_self_attended,
        self_attended,
        self_logs,
        self_key_rows,
        self_values,
        prior_query_grads,
    )
    self_key_total = (self_key_grads + later_keys.astype(jnp.float32)).astype(jnp.bfloat16)
    self_value_total = (self_value_grads + later_values.astype(jnp.float32)).astype(jnp.bfloat16)
    grad_self_query_w = (
        jnp.einsum("td,th->dh", hidden_zero, grad_self_queries, preferred_element_type=jnp.float32)
        * scale
    )
    self_query_bias_grad = jnp.sum(grad_self_queries.astype(jnp.float32), axis=0) * scale
    grad_self_key_w = jnp.einsum(
        "td,th->dh", hidden_zero, self_key_total, preferred_element_type=jnp.float32
    )
    grad_self_value_w = jnp.einsum(
        "td,th->dh", hidden_zero, self_value_total, preferred_element_type=jnp.float32
    )
    self_value_bias_grad = jnp.sum(self_value_total.astype(jnp.float32), axis=0)
    zero_part = (
        jnp.einsum("th,dh->td", grad_self_queries, w_self_query, preferred_element_type=jnp.float32)
        * scale
        + jnp.einsum("th,dh->td", self_key_total, w_self_key, preferred_element_type=jnp.float32)
        + jnp.einsum(
            "th,dh->td", self_value_total, w_self_value, preferred_element_type=jnp.float32
        )
    )
    grad_hidden_zero = core_sum(zero_part)
    back_zero, gain_zero_grad, bias_zero_grad = norm_back(
        grad_hidden_zero, self_normed_rows, inverse_zero, ln0_gain
    )
    d_tokens = (grad_start + back_zero).astype(jnp.bfloat16)
    (
        s_squery,
        self_key_spec,
        s_svalue,
        s_sout,
        summed_query,
        summed_key,
        summed_value,
        summed_out,
        summed_up,
        summed_down,
    ) = (
        scattered(grad_self_query_w, 0),
        scattered(grad_self_key_w, 0),
        scattered(grad_self_value_w, 0),
        scattered(grad_self_out, 1),
        scattered(grad_query_w, 0),
        scattered(grad_key, 0),
        scattered(grad_value, 0),
        scattered(grad_out, 1),
        scattered(grad_up, 0),
        scattered(grad_down, 1),
    )
    small_sums = butterfly_sum(
        (
            gain_zero_grad,
            bias_zero_grad,
            self_query_bias_grad,
            self_value_bias_grad,
            self_out_bias_grad,
            gain_one_grad,
            bias_one_grad,
            query_bias_grad,
            value_bias_grad,
            out_bias_grad,
            gain_two_grad,
            bias_two_grad,
            up_bias_grad,
            down_bias_grad,
        )
    )
    return (
        layer_out,
        d_tokens,
        d_memory,
        small_sums[0],
        small_sums[1],
        s_squery,
        small_sums[2],
        self_key_spec,
        s_svalue,
        small_sums[3],
        s_sout,
        small_sums[4],
        small_sums[5],
        small_sums[6],
        summed_query,
        small_sums[7],
        summed_key,
        summed_value,
        small_sums[8],
        summed_out,
        small_sums[9],
        small_sums[10],
        small_sums[11],
        summed_up,
        small_sums[12],
        summed_down,
        small_sums[13],
    )


def solution(mesh):
    in_specs = (
        P("dp", None),
        P("dp"),
        P("dp"),
        P("dp", None, None),
        P(),
        P(),
        P(None, "tensor"),
        P("tensor"),
        P(None, "tensor"),
        P(None, "tensor"),
        P("tensor"),
        P("tensor", None),
        P(),
        P(),
        P(),
        P(None, "tensor"),
        P("tensor"),
        P(None, "tensor"),
        P(None, "tensor"),
        P("tensor"),
        P("tensor", None),
        P(),
        P(),
        P(),
        P(None, "tensor"),
        P("tensor"),
        P("tensor", None),
        P(),
        P("dp", None),
    )
    out_specs = (
        P("dp", None),
        P("dp", None),
        P("dp", None, None),
        P(),
        P(),
        P("dp", "tensor"),
        P("tensor"),
        P("dp", "tensor"),
        P("dp", "tensor"),
        P("tensor"),
        P("tensor", "dp"),
        P(),
        P(),
        P(),
        P("dp", "tensor"),
        P("tensor"),
        P("dp", "tensor"),
        P("dp", "tensor"),
        P("tensor"),
        P("tensor", "dp"),
        P(),
        P(),
        P(),
        P("dp", "tensor"),
        P("tensor"),
        P("tensor", "dp"),
        P(),
    )
    return jax.shard_map(
        per_device, mesh=mesh, in_specs=in_specs, out_specs=out_specs, check_vma=False
    )
```

```python
import functools
import math

import jax
import jax.numpy as jnp
from jax import lax
from jax.experimental import pallas as pl
from jax.experimental.pallas import tpu as pltpu
from jax.sharding import PartitionSpec as P

HEAD_WIDTH = 64


EPSILON = 1e-05


def shifted(value, axis, steps):
    count = lax.axis_size(axis)
    initial, last = (max(0, -steps), min(count, count - steps))
    return lax.ppermute(value, axis, [(source, source + steps) for source in range(initial, last)])


def butterfly_sum(vectors):
    sizes = [vector.shape[0] for vector in vectors]
    total = jnp.concatenate(vectors).reshape(-1, 128)
    count = lax.axis_size("dp")
    bit = 1
    while bit < count:
        total = total + lax.ppermute(total, "dp", [(i, i ^ bit) for i in range(count)])
        bit *= 2
    flat = total.reshape(-1)
    pieces, at = [], 0
    for size in sizes:
        pieces.append(flat[at : at + size])
        at += size
    return pieces


def layer_norm(values, gain, bias):
    mean = jnp.mean(values, axis=-1, keepdims=True)
    centered = values - mean
    inverse = lax.rsqrt(jnp.mean(centered * centered, axis=-1, keepdims=True) + EPSILON)
    normed = centered * inverse
    return (normed * gain + bias, normed, inverse)


def norm_back(grad, normed, inverse, gain):
    scaled = grad * gain
    inner = (
        scaled
        - jnp.mean(scaled, axis=-1, keepdims=True)
        - normed * jnp.mean(scaled * normed, axis=-1, keepdims=True)
    )
    return (inner * inverse, jnp.sum(grad * normed, axis=0), jnp.sum(grad, axis=0))


BF = jnp.bfloat16
F32 = jnp.float32
NEG = -1e30
TILE = 256
HEAD_WIDTH = 64
PAIR = 2 * HEAD_WIDTH
VMEM_LIMIT = 60 * 1024 * 1024


def nt(left, right):
    return lax.dot_general(left, right, (((1,), (1,)), ((), ())), preferred_element_type=F32)


def nn(left, right):
    return lax.dot_general(left, right, (((1,), (0,)), ((), ())), preferred_element_type=F32)


def head_half(pair, half):
    lane = lax.broadcasted_iota(jnp.int32, pair.shape, 1)
    keep = lane < HEAD_WIDTH if half == 0 else lane >= HEAD_WIDTH
    return jnp.where(keep, pair, jnp.zeros_like(pair))


def span(index, size=TILE):
    return pl.ds(pl.multiple_of(index * size, size), size)


HEAD_ROWS = 80


def column_max(values):
    rows = values.shape[0]
    groups = max(1, rows // 64)
    step = -(-(rows // groups) // 8) * 8
    parts = []
    at = 0
    while at < rows:
        end = min(rows, at + step)
        parts.append(jnp.max(values[at:end], axis=0, keepdims=True))
        at = end
    while len(parts) > 1:
        parts = [jnp.maximum(*parts[i : i + 2]) if i + 1 < len(parts) else parts[i] for i in range(0, len(parts), 2)]
    return parts[0]


def extended(values, target, columns):
    turned = values.T
    extra = jnp.where(lax.broadcasted_iota(jnp.int32, (HEAD_ROWS - HEAD_WIDTH, turned.shape[1]), 0) == 0, 1.0, 0.0).astype(BF)
    for h in range(turned.shape[0] // HEAD_WIDTH):
        base = h * HEAD_ROWS
        target[base : base + HEAD_WIDTH, columns] = turned[h * HEAD_WIDTH : (h + 1) * HEAD_WIDTH, :]
        target[base + HEAD_WIDTH : base + HEAD_ROWS, columns] = extra


def lane_rows(i):
    return i * TILE + lax.broadcasted_iota(jnp.int32, (1, TILE), 1)


def self_forward_body(meta, q_ref, kp_ref, k_ref, vp_ref, v_ref, o_ref, log_ref,
                      vpt, vt, qm, bias, m_s, acc, done, scores):
    rows = q_ref.shape[0]
    pairs = q_ref.shape[1] // PAIR
    b1, b2, p0 = meta[0], meta[1], meta[2]
    tiles = rows // TILE
    offset = rows - kp_ref.shape[0]
    prior_tiles = kp_ref.shape[0] // TILE
    first_prior = (p0 - offset) // TILE
    prior_rows = (b1 + TILE - 1) // TILE

    def turn_own(j, c):
        extended(v_ref[span(j), :], vt, span(j))
        return c

    lax.fori_loop(0, tiles, turn_own, 0)

    def turn_prior(j, c):
        extended(vp_ref[span(j), :], vpt, span(j))
        return c

    lax.fori_loop(jnp.where(b1 > 0, first_prior, prior_tiles), prior_tiles, turn_prior, 0)

    def key_step(keys, values_t, j):
        for pair in range(pairs):
            key_pair = keys[span(j), pair * PAIR : pair * PAIR + PAIR]
            for half in range(2):
                scores[2 * pair + half] = nt(key_pair, qm[2 * pair + half])
        for pair in range(pairs):
            for half in range(2):
                h = 2 * pair + half
                heads = slice(h * HEAD_ROWS, (h + 1) * HEAD_ROWS)
                s = scores[h] + bias[...]
                m_old = m_s[h : h + 1, :]
                m_new = jnp.maximum(m_old, column_max(s))
                alpha = jnp.exp(m_old - m_new)
                e = jnp.exp(s - m_new)
                m_s[h : h + 1, :] = m_new
                acc[heads, :] = acc[heads, :] * alpha + nn(values_t[heads, span(j)], e.astype(BF))

    def row_tile(i, c):
        t = lane_rows(i)
        start = jnp.where(t < b1, 0, jnp.where(t < b2, b1, b2))
        for pair in range(pairs):
            q_pair = q_ref[span(i), pair * PAIR : pair * PAIR + PAIR]
            for half in range(2):
                qm[2 * pair + half] = head_half(q_pair, half)
        m_s[...] = jnp.full_like(m_s, NEG)
        acc[...] = jnp.zeros_like(acc)

        def prior(j, c2):
            r = offset + j * TILE + lax.broadcasted_iota(jnp.int32, (TILE, TILE), 0)
            bias[...] = jnp.where((r >= p0) & (t < b1), 0.0, NEG)
            key_step(kp_ref, vpt, j)
            return c2

        lax.fori_loop(jnp.where(i < prior_rows, first_prior, prior_tiles), prior_tiles, prior, 0)
        t_first = i * TILE
        lowest = jnp.where(t_first < b1, 0, jnp.where(t_first < b2, b1, b2))

        def own(j, c2):
            r = j * TILE + lax.broadcasted_iota(jnp.int32, (TILE, TILE), 0)
            bias[...] = jnp.where((r <= t) & (r >= start), 0.0, NEG)
            key_step(k_ref, vt, j)
            return c2

        lax.fori_loop(lowest // TILE, i + 1, own, 0)
        for h in range(2 * pairs):
            base = h * HEAD_ROWS
            total = acc[base + HEAD_WIDTH : base + HEAD_WIDTH + 1, :]
            log_ref[h : h + 1, span(i)] = m_s[h : h + 1, :] + jnp.log(total)
            done[h * HEAD_WIDTH : (h + 1) * HEAD_WIDTH, :] = acc[base : base + HEAD_WIDTH, :] * (1.0 / total)
        o_ref[span(i), :] = done[...].T.astype(BF)
        return c

    lax.fori_loop(0, tiles, row_tile, 0)


SMEM_SPEC = pl.BlockSpec(memory_space=pltpu.SMEM)
VMEM_SPEC = pl.BlockSpec(memory_space=pltpu.VMEM)


def self_forward(meta, q, k_prior, k, v_prior, v):
    rows, width = q.shape
    heads = width // HEAD_WIDTH
    return pl.pallas_call(
        self_forward_body,
        out_shape=(jax.ShapeDtypeStruct((rows, width), BF), jax.ShapeDtypeStruct((heads, rows), F32)),
        in_specs=[SMEM_SPEC] + [VMEM_SPEC] * 5,
        out_specs=(VMEM_SPEC, VMEM_SPEC),
        scratch_shapes=[
            pltpu.VMEM((heads * HEAD_ROWS, k_prior.shape[0]), BF),
            pltpu.VMEM((heads * HEAD_ROWS, rows), BF),
            pltpu.VMEM((heads, TILE, PAIR), BF),
            pltpu.VMEM((TILE, TILE), F32),
            pltpu.VMEM((heads, TILE), F32),
            pltpu.VMEM((heads * HEAD_ROWS, TILE), F32),
            pltpu.VMEM((width, TILE), F32),
            pltpu.VMEM((heads, TILE, TILE), F32),
        ],
        compiler_params=pltpu.CompilerParams(vmem_limit_bytes=VMEM_LIMIT),
        cost_estimate=pl.CostEstimate(flops=2 * 2 * rows * rows * width, bytes_accessed=8 * rows * width * 2, transcendentals=rows * rows * heads),
        name="self_forward",
    )(meta, q, k_prior, k, v_prior, v)


def grad_rows(do_ref, o_ref, i, width):
    heads = width // HEAD_WIDTH
    product = do_ref[span(i), :].astype(F32) * o_ref[span(i), :].astype(F32)
    high = product.astype(BF)
    low = (product - high.astype(F32)).astype(BF)
    head = lax.broadcasted_iota(jnp.int32, (heads, width), 0)
    column = lax.broadcasted_iota(jnp.int32, (heads, width), 1) // HEAD_WIDTH
    pick = jnp.where(head == column, 1.0, 0.0).astype(BF)
    return nt(pick, high) + nt(pick, low)


def halves(source, i, target, pairs):
    for pair in range(pairs):
        value = source[span(i), pair * PAIR : pair * PAIR + PAIR]
        for half in range(2):
            target[2 * pair + half] = head_half(value, half)


def grad_step(pairs, keys, values, keys_t, key_slice, key_lanes, qm, dom, shift, delta, bias, dk, dv, dqt, scores, grads):
    for pair in range(pairs):
        cols = slice(pair * PAIR, pair * PAIR + PAIR)
        key_pair = keys[key_slice, cols]
        value_pair = values[key_slice, cols]
        for half in range(2):
            h = 2 * pair + half
            scores[h] = nt(key_pair, qm[h])
            grads[h] = nt(value_pair, dom[h])
    for pair in range(pairs):
        cols = slice(pair * PAIR, pair * PAIR + PAIR)
        dv_pair = dv[key_slice, cols]
        dk_pair = dk[key_slice, cols]
        for half in range(2):
            h = 2 * pair + half
            heads = slice(h * HEAD_WIDTH, (h + 1) * HEAD_WIDTH)
            s = scores[h]
            if bias is not None:
                s = s + bias[...]
            p = jnp.exp(s - shift[h : h + 1, :])
            dp = grads[h]
            ds = (p * (dp - delta[h : h + 1, :])).astype(BF)
            dv_pair = dv_pair + nn(p.astype(BF), dom[h])
            dk_pair = dk_pair + nn(ds, qm[h])
            dqt[heads, :] = dqt[heads, :] + nn(keys_t[heads, key_lanes], ds)
        dv[key_slice, cols] = dv_pair
        dk[key_slice, cols] = dk_pair


def self_prior_back_body(meta, q_ref, do_ref, o_ref, log_ref, k_ref, v_ref, dk_ref, dv_ref, dq_ref,
                         kt, qm, dom, bias, delta, shift, dqt, dk, dv, scores, grads):
    rows, width = q_ref.shape
    pairs = width // PAIR
    b1, p0 = meta[0], meta[2]
    tiles = rows // TILE
    offset = rows - k_ref.shape[0]
    prior_tiles = k_ref.shape[0] // TILE
    first_prior = (p0 - offset) // TILE
    prior_rows = (b1 + TILE - 1) // TILE
    dk[...] = jnp.zeros_like(dk)
    dv[...] = jnp.zeros_like(dv)

    def turn(j, c):
        kt[:, span(j)] = k_ref[span(j), :].T
        return c

    lax.fori_loop(jnp.where(b1 > 0, first_prior, prior_tiles), prior_tiles, turn, 0)

    def row_tile(i, c):
        dqt[...] = jnp.zeros_like(dqt)
        t = lane_rows(i)

        @pl.when(i < prior_rows)
        def _():
            halves(q_ref, i, qm, pairs)
            halves(do_ref, i, dom, pairs)
            delta[...] = grad_rows(do_ref, o_ref, i, width)
            shift[...] = log_ref[:, span(i)]

        def prior(j, c2):
            r = offset + j * TILE + lax.broadcasted_iota(jnp.int32, (TILE, TILE), 0)
            bias[...] = jnp.where((r >= p0) & (t < b1), 0.0, NEG)
            grad_step(pairs, k_ref, v_ref, kt, span(j), span(j), qm, dom, shift, delta, bias, dk, dv, dqt, scores, grads)
            return c2

        lax.fori_loop(jnp.where(i < prior_rows, first_prior, prior_tiles), prior_tiles, prior, 0)
        dq_ref[span(i), :] = dqt[...].T
        return c

    lax.fori_loop(0, tiles, row_tile, 0)
    dk_ref[...] = dk[...].astype(BF)
    dv_ref[...] = dv[...].astype(BF)


def self_own_back_body(meta, q_ref, do_ref, o_ref, log_ref, k_ref, v_ref, dqp_ref, dk_ref, dv_ref, dq_ref,
                       kt, qm, dom, bias, delta, shift, dqt, dk, dv, scores, grads):
    rows, width = q_ref.shape
    pairs = width // PAIR
    b1, b2 = meta[0], meta[1]
    tiles = rows // TILE
    dk[...] = jnp.zeros_like(dk)
    dv[...] = jnp.zeros_like(dv)

    def turn(j, c):
        kt[:, span(j)] = k_ref[span(j), :].T
        return c

    lax.fori_loop(0, tiles, turn, 0)

    def row_tile(i, c):
        dqt[...] = jnp.zeros_like(dqt)
        t = lane_rows(i)
        start = jnp.where(t < b1, 0, jnp.where(t < b2, b1, b2))
        halves(q_ref, i, qm, pairs)
        halves(do_ref, i, dom, pairs)
        delta[...] = grad_rows(do_ref, o_ref, i, width)
        shift[...] = log_ref[:, span(i)]
        t_first = i * TILE
        lowest = jnp.where(t_first < b1, 0, jnp.where(t_first < b2, b1, b2))

        def own(j, c2):
            r = j * TILE + lax.broadcasted_iota(jnp.int32, (TILE, TILE), 0)
            bias[...] = jnp.where((r <= t) & (r >= start), 0.0, NEG)
            grad_step(pairs, k_ref, v_ref, kt, span(j), span(j), qm, dom, shift, delta, bias, dk, dv, dqt, scores, grads)
            return c2

        lax.fori_loop(lowest // TILE, i + 1, own, 0)
        dq_ref[span(i), :] = (dqp_ref[span(i), :] + dqt[...].T).astype(BF)
        return c

    lax.fori_loop(0, tiles, row_tile, 0)
    dk_ref[...] = dk[...].astype(BF)
    dv_ref[...] = dv[...].astype(BF)


def self_back_scratch(keys, width):
    heads = width // HEAD_WIDTH
    return [
        pltpu.VMEM((width, keys), BF),
        pltpu.VMEM((heads, TILE, PAIR), BF),
        pltpu.VMEM((heads, TILE, PAIR), BF),
        pltpu.VMEM((TILE, TILE), F32),
        pltpu.VMEM((heads, TILE), F32),
        pltpu.VMEM((heads, TILE), F32),
        pltpu.VMEM((width, TILE), F32),
        pltpu.VMEM((keys, width), F32),
        pltpu.VMEM((keys, width), F32),
        pltpu.VMEM((heads, TILE, TILE), F32),
        pltpu.VMEM((heads, TILE, TILE), F32),
    ]


def self_prior_back(meta, q, do, o, logs, k_prior, v_prior):
    rows, width = q.shape
    return pl.pallas_call(
        self_prior_back_body,
        out_shape=(jax.ShapeDtypeStruct(k_prior.shape, BF), jax.ShapeDtypeStruct(k_prior.shape, BF),
                   jax.ShapeDtypeStruct((rows, width), F32)),
        in_specs=[SMEM_SPEC] + [VMEM_SPEC] * 6,
        out_specs=(VMEM_SPEC,) * 3,
        scratch_shapes=self_back_scratch(k_prior.shape[0], width),
        compiler_params=pltpu.CompilerParams(vmem_limit_bytes=VMEM_LIMIT),
        cost_estimate=pl.CostEstimate(flops=3 * rows * rows * width, bytes_accessed=8 * rows * width * 2, transcendentals=rows * rows * 4),
        name="self_prior_back",
    )(meta, q, do, o, logs, k_prior, v_prior)


def self_own_back(meta, q, do, o, logs, k, v, dq_prior):
    rows, width = q.shape
    return pl.pallas_call(
        self_own_back_body,
        out_shape=(jax.ShapeDtypeStruct((rows, width), BF),) * 3,
        in_specs=[SMEM_SPEC] + [VMEM_SPEC] * 7,
        out_specs=(VMEM_SPEC,) * 3,
        scratch_shapes=self_back_scratch(rows, width),
        compiler_params=pltpu.CompilerParams(vmem_limit_bytes=VMEM_LIMIT),
        cost_estimate=pl.CostEstimate(flops=5 * rows * rows * width, bytes_accessed=8 * rows * width * 2, transcendentals=rows * rows * 4),
        name="self_own_back",
    )(meta, q, do, o, logs, k, v, dq_prior)


def segments(meta, rows):
    return ((0, meta[0], None), (meta[0], meta[1], meta[4]), (meta[1], rows, meta[5]))


def cross_forward_body(used, meta, q_ref, kp_ref, k_ref, vp_ref, v_ref, o_ref, log_ref, vpt, vt, qm, acc, scores):
    rows, width = q_ref.shape
    pairs = width // PAIR
    padded = kp_ref.shape[0]
    images = k_ref.shape[0] // padded
    for slot in range(images):
        extended(v_ref[slot * padded : (slot + 1) * padded, :], vt.at[slot], slice(None))
    extended(vp_ref[...], vpt, slice(None))
    for first, last, slot in segments(meta, rows):
        own = slot is not None
        keys = pl.ds(pl.multiple_of(slot * padded, 16), padded) if own else slice(None)
        key_table = k_ref if own else kp_ref
        value_table = vt.at[slot] if own else vpt

        def tile(i, c):
            halves(q_ref, i, qm, pairs)
            t = lane_rows(i)
            inside = (t >= first) & (t < last)
            for pair in range(pairs):
                key_pair = key_table[keys, pair * PAIR : pair * PAIR + PAIR]
                for half in range(2):
                    scores[2 * pair + half] = nt(key_pair, qm[2 * pair + half])
            for h in range(2 * pairs):
                heads = slice(h * HEAD_WIDTH, (h + 1) * HEAD_WIDTH)
                s = scores[h]
                if used < padded:
                    row = lax.broadcasted_iota(jnp.int32, s.shape, 0)
                    s = jnp.where(row < used, s, NEG)
                m = column_max(s)
                e = jnp.exp(s - m)
                mixed = nn(value_table[h * HEAD_ROWS : (h + 1) * HEAD_ROWS, :], e.astype(BF))
                total = mixed[HEAD_WIDTH : HEAD_WIDTH + 1, :]
                acc[heads, :] = mixed[:HEAD_WIDTH, :] * (1.0 / total)
                log_ref[h : h + 1, span(i)] = jnp.where(
                    inside, m + jnp.log(total), log_ref[h : h + 1, span(i)]
                )
            column = i * TILE + lax.broadcasted_iota(jnp.int32, (TILE, width), 0)
            keep = (column >= first) & (column < last)
            o_ref[span(i), :] = jnp.where(keep, acc[...].T, o_ref[span(i), :].astype(F32)).astype(BF)
            return c

        lax.fori_loop(first // TILE, jnp.where(last > first, (last + TILE - 1) // TILE, 0), tile, 0)


def cross_forward(used, meta, q, k_prior, k, v_prior, v):
    rows, width = q.shape
    heads = width // HEAD_WIDTH
    padded = k_prior.shape[0]
    return pl.pallas_call(
        functools.partial(cross_forward_body, used),
        out_shape=(jax.ShapeDtypeStruct((rows, width), BF), jax.ShapeDtypeStruct((heads, rows), F32)),
        in_specs=[SMEM_SPEC] + [VMEM_SPEC] * 5,
        out_specs=(VMEM_SPEC, VMEM_SPEC),
        scratch_shapes=[
            pltpu.VMEM((heads * HEAD_ROWS, padded), BF),
            pltpu.VMEM((k.shape[0] // padded, heads * HEAD_ROWS, padded), BF),
            pltpu.VMEM((heads, TILE, PAIR), BF),
            pltpu.VMEM((width, TILE), F32),
            pltpu.VMEM((heads, padded, TILE), F32),
        ],
        compiler_params=pltpu.CompilerParams(vmem_limit_bytes=VMEM_LIMIT),
        cost_estimate=pl.CostEstimate(flops=16 * rows * padded * width, bytes_accessed=8 * rows * width * 2, transcendentals=rows * padded * heads),
        name="cross_forward",
    )(meta, q, k_prior, k, v_prior, v)


def cross_back_body(used, meta, q_ref, do_ref, o_ref, log_ref, kp_ref, k_ref, vp_ref, v_ref, dkp_ref, dk_ref, dvp_ref, dv_ref,
                    dq_ref, kpt, kt, qm, dom, delta, shift, dqt, dkp, dk, dvp, dv, scores, grads):
    rows, width = q_ref.shape
    pairs = width // PAIR
    padded = kp_ref.shape[0]
    images = k_ref.shape[0] // padded
    for item in (dkp, dk, dvp, dv):
        item[...] = jnp.zeros_like(item)
    for slot in range(images):
        kt[slot] = k_ref[slot * padded : (slot + 1) * padded, :].T
    kpt[...] = kp_ref[...].T
    for first, last, slot in segments(meta, rows):
        own = slot is not None
        keys = pl.ds(pl.multiple_of(slot * padded, 16), padded) if own else slice(None)
        tables = (k_ref, v_ref, kt.at[slot]) if own else (kp_ref, vp_ref, kpt)
        sums = (dk, dv) if own else (dkp, dvp)

        def tile(i, c):
            halves(q_ref, i, qm, pairs)
            halves(do_ref, i, dom, pairs)
            t = lane_rows(i)
            inside = (t >= first) & (t < last)
            delta[...] = grad_rows(do_ref, o_ref, i, width)
            shift[...] = jnp.where(inside, log_ref[:, span(i)], -NEG)
            dqt[...] = jnp.zeros_like(dqt)
            grad_step(pairs, *tables, keys, slice(None), qm, dom, shift, delta, None, *sums, dqt, scores, grads)
            column = i * TILE + lax.broadcasted_iota(jnp.int32, (TILE, width), 0)
            keep = (column >= first) & (column < last)
            dq_ref[span(i), :] = jnp.where(keep, dqt[...].T, dq_ref[span(i), :].astype(F32)).astype(BF)
            return c

        lax.fori_loop(first // TILE, jnp.where(last > first, (last + TILE - 1) // TILE, 0), tile, 0)
    inner = lax.broadcasted_iota(jnp.int32, (padded, width), 0) < used
    for source, target in ((dkp, dkp_ref), (dk, dk_ref), (dvp, dvp_ref), (dv, dv_ref)):
        for slot in range(source.shape[0] // padded):
            part = slice(slot * padded, (slot + 1) * padded)
            target[part, :] = jnp.where(inner, source[part, :], 0.0).astype(BF)


def cross_back(used, meta, q, do, o, logs, k_prior, k, v_prior, v):
    rows, width = q.shape
    heads = width // HEAD_WIDTH
    padded = k_prior.shape[0]
    tables = (k_prior, k, v_prior, v)
    return pl.pallas_call(
        functools.partial(cross_back_body, used),
        out_shape=tuple(jax.ShapeDtypeStruct(table.shape, BF) for table in tables) + (jax.ShapeDtypeStruct((rows, width), BF),),
        in_specs=[SMEM_SPEC] + [VMEM_SPEC] * 8,
        out_specs=(VMEM_SPEC,) * 5,
        scratch_shapes=[
            pltpu.VMEM((width, padded), BF),
            pltpu.VMEM((k.shape[0] // padded, width, padded), BF),
            pltpu.VMEM((heads, TILE, PAIR), BF),
            pltpu.VMEM((heads, TILE, PAIR), BF),
            pltpu.VMEM((heads, TILE), F32),
            pltpu.VMEM((heads, TILE), F32),
            pltpu.VMEM((width, TILE), F32),
        ]
        + [pltpu.VMEM(table.shape, F32) for table in tables]
        + [pltpu.VMEM((heads, padded, TILE), F32)] * 2,
        compiler_params=pltpu.CompilerParams(vmem_limit_bytes=VMEM_LIMIT),
        cost_estimate=pl.CostEstimate(flops=40 * rows * padded * width, bytes_accessed=12 * rows * width * 2, transcendentals=rows * padded * heads),
        name="cross_back",
    )(meta, q, do, o, logs, *tables)


SQRT_HALF = 0.7071067811865476
GAUSS = 0.3989422804014327
ROW_CHUNK = 256


def error_function(x):
    x = jnp.clip(x, -4.0, 4.0)
    z = x * x
    top = -2.72614225801306e-10
    for term in (2.77068142495902e-08, -2.10102402082508e-06, -5.69250639462346e-05,
                 -7.34990630326855e-04, -2.95459980854025e-03, -1.60960333262415e-02):
        top = top * z + term
    low = -1.45660718464996e-05
    for term in (-2.13374055278905e-04, -1.68282697438203e-03, -7.37332916720468e-03, -1.42647390514189e-02):
        low = low * z + term
    return x * top / low


def row_norm(values):
    mean = jnp.mean(values, axis=-1, keepdims=True)
    centered = values - mean
    inverse = lax.rsqrt(jnp.mean(centered * centered, axis=-1, keepdims=True) + EPSILON)
    return centered * inverse, inverse


def chunk_place(index, inner, outer):
    return (index % inner) * outer + index // inner


def feed_forward_body(inner, outer, start_ref, own_ref, other_ref, b_out, gain, shift_in, dy_ref, w_up, b_up, w_down,
                      y1_ref, down_ref, dh_ref, grads_ref, db_ref,
                      h2, h2t, dyt, acc_down, acc_dh, u_s, da_s, g_s, du_s):
    step = pl.program_id(0)
    rows, width = dy_ref.shape
    tile = w_up.shape[1]
    chunks = rows // ROW_CHUNK

    @pl.when(step == 0)
    def _():
        for r in range(chunks):
            part = slice(r * ROW_CHUNK, (r + 1) * ROW_CHUNK)
            y1 = start_ref[part, :] + (own_ref[part, :].astype(F32) + other_ref[part, :].astype(F32)) + b_out[...]
            y1_ref[part, :] = y1
            normed, _ = row_norm(y1)
            low = (normed * gain[...] + shift_in[...]).astype(BF)
            h2[part, :] = low
            h2t[:, part] = low.T
            dyt[:, part] = dy_ref[part, :].T
        acc_down[...] = jnp.zeros_like(acc_down)
        acc_dh[...] = jnp.zeros_like(acc_dh)

    for r in range(chunks):
        part = slice(r * ROW_CHUNK, (r + 1) * ROW_CHUNK)
        u_s[part, :] = nn(h2[part, :], w_up[...]) + b_up[...]
        da_s[part, :] = nt(dy_ref[part, :], w_down[...])
    total = jnp.zeros((1, tile), F32)
    for r in range(chunks):
        part = slice(r * ROW_CHUNK, (r + 1) * ROW_CHUNK)
        u = u_s[part, :]
        half = 0.5 + 0.5 * error_function(u * SQRT_HALF)
        g = (u * half).astype(BF)
        slope = half + u * (GAUSS * jnp.exp(-0.5 * u * u))
        du = (da_s[part, :] * slope).astype(BF)
        g_s[part, :] = g
        du_s[part, :] = du
        total = total + jnp.sum(du.astype(F32), axis=0, keepdims=True)
        down = nn(g, w_down[...])
        dh = nt(du, w_up[...])
        acc_down[part, :] += down
        acc_dh[part, :] += dh

    db_ref[...] = total
    piece = width // (inner * outer)
    for source, turned, at in ((du_s, h2t, 0), (g_s, dyt, tile)):
        for r in range(width // ROW_CHUNK):
            part = slice(r * ROW_CHUNK, (r + 1) * ROW_CHUNK)
            product = nn(turned[part, :], source[...]).astype(BF)
            for c in range(ROW_CHUNK // piece):
                place = chunk_place(r * (ROW_CHUNK // piece) + c, inner, outer) * piece
                grads_ref[place : place + piece, at : at + tile] = product[c * piece : (c + 1) * piece, :]

    @pl.when(step == pl.num_programs(0) - 1)
    def _():
        down_ref[...] = acc_down[...].astype(BF)
        dh_ref[...] = acc_dh[...].astype(BF)


def feed_forward(inner, outer, tile, start, own, other, b_out, gain, shift_in, dy, w_up, b_up, w_down):
    rows, width = dy.shape
    hidden = w_up.shape[1]
    whole = lambda shape: pl.BlockSpec(shape, lambda k: (0, 0), pipeline_mode=pl.Buffered(1))
    row = whole((1, width))
    full = whole((rows, width))
    return pl.pallas_call(
        functools.partial(feed_forward_body, inner, outer),
        grid=(hidden // tile,),
        out_shape=(
            jax.ShapeDtypeStruct((rows, width), F32),
            jax.ShapeDtypeStruct((rows, width), BF),
            jax.ShapeDtypeStruct((rows, width), BF),
            jax.ShapeDtypeStruct((width, 2 * hidden), BF),
            jax.ShapeDtypeStruct((1, hidden), F32),
        ),
        in_specs=[full, full, full, row, row, row, full,
                  pl.BlockSpec((width, tile), lambda k: (0, k)),
                  pl.BlockSpec((1, tile), lambda k: (0, k)),
                  pl.BlockSpec((tile, width), lambda k: (k, 0))],
        out_specs=(full, full, full, pl.BlockSpec((width, 2 * tile), lambda k: (0, k)), pl.BlockSpec((1, tile), lambda k: (0, k))),
        scratch_shapes=[
            pltpu.VMEM((rows, width), BF),
            pltpu.VMEM((width, rows), BF),
            pltpu.VMEM((width, rows), BF),
            pltpu.VMEM((rows, width), F32),
            pltpu.VMEM((rows, width), F32),
            pltpu.VMEM((rows, tile), F32),
            pltpu.VMEM((rows, tile), F32),
            pltpu.VMEM((rows, tile), BF),
            pltpu.VMEM((rows, tile), BF),
        ],
        compiler_params=pltpu.CompilerParams(vmem_limit_bytes=VMEM_LIMIT),
        cost_estimate=pl.CostEstimate(flops=12 * rows * width * hidden, bytes_accessed=30 * rows * width, transcendentals=rows * hidden * 2),
        name="feed_forward",
    )(start, own, other, b_out.reshape(1, -1), gain.reshape(1, -1), shift_in.reshape(1, -1), dy, w_up, b_up.reshape(1, -1), w_down)


def bit_orders(count):
    bits = list(range(count.bit_length() - 1))
    return bits, [bits[1], bits[0]] + bits[2:]


def place_code(position, order):
    code = 0
    for rank, bit in enumerate(order):
        if position >> (len(order) - 1 - rank) & 1:
            code |= 1 << bit
    return code


def weight_grads_body(count, products, left_count, right_count, me, *refs):
    lefts, rights = refs[:left_count], refs[left_count : left_count + right_count]
    outs = refs[left_count + right_count : left_count + right_count + 4]
    turned = refs[left_count + right_count + 4 : -1]
    natural = refs[-1]
    width = lefts[0].shape[1]
    columns = rights[0].shape[1]
    piece = width // count
    orders = bit_orders(count)
    for left, target in zip(lefts, turned):
        for r in range(width // ROW_CHUNK):
            part = slice(r * ROW_CHUNK, (r + 1) * ROW_CHUNK)
            target[part, :] = left[:, part].T
    for number, (terms, factor) in enumerate(products):
        store = natural.at[number % 2]
        for r in range(width // ROW_CHUNK):
            part = slice(r * ROW_CHUNK, (r + 1) * ROW_CHUNK)
            total = None
            for left, right in terms:
                product = nn(turned[left][part, :], rights[right][...])
                total = product if total is None else total + product
            store[part, :] = (total * factor if factor != 1.0 else total).astype(BF)
        side = number // (len(products) // 2)
        at = number % (len(products) // 2) * columns
        keep, send = outs[2 * side], outs[2 * side + 1]
        for position in range(count):
            source = pl.multiple_of((me[0] ^ place_code(position, orders[side])) * piece, piece)
            target = keep if position < count // 2 else send
            row = position % (count // 2) * piece
            target[row : row + piece, at : at + columns] = store[pl.ds(source, piece), :]


def weight_grads(count, me, lefts, rights, products):
    width = lefts[0].shape[1]
    columns = rights[0].shape[1]
    half = jax.ShapeDtypeStruct((width // 2, columns * len(products) // 2), BF)
    flops = sum(2 * width * columns * lefts[left].shape[0] for terms, _ in products for left, _ in terms)
    return pl.pallas_call(
        functools.partial(weight_grads_body, count, products, len(lefts), len(rights)),
        out_shape=(half,) * 4,
        in_specs=[SMEM_SPEC] + [VMEM_SPEC] * (len(lefts) + len(rights)),
        out_specs=(VMEM_SPEC,) * 4,
        scratch_shapes=[pltpu.VMEM((width, left.shape[0]), BF) for left in lefts] + [pltpu.VMEM((2, width, columns), BF)],
        compiler_params=pltpu.CompilerParams(vmem_limit_bytes=VMEM_LIMIT),
        cost_estimate=pl.CostEstimate(flops=2 * flops, bytes_accessed=16 * width * width, transcendentals=0),
        name="weight_grads",
    )(me, *lefts, *rights)


def fold_body(joined, sides, *refs):
    ins, outs = refs[: 2 * sides], refs[2 * sides :]
    for side in range(sides):
        keep, got = ins[2 * side], ins[2 * side + 1]
        rows, columns = keep.shape
        total = keep[...].astype(F32) + got[...].astype(F32)
        if len(outs) == 1:
            outs[0][...] = total
            continue
        out_keep, out_send = (outs[0], outs[1]) if joined else (outs[2 * side], outs[2 * side + 1])
        at = side * columns if joined else 0
        out_keep[:, at : at + columns] = total[: rows // 2].astype(BF)
        out_send[:, at : at + columns] = total[rows // 2 :].astype(BF)


def fold(parts, joined, last):
    sides = len(parts) // 2
    rows, columns = parts[0].shape
    if last:
        shapes = (jax.ShapeDtypeStruct((rows, columns), F32),)
    elif joined:
        shapes = (jax.ShapeDtypeStruct((rows // 2, columns * sides), BF),) * 2
    else:
        shapes = (jax.ShapeDtypeStruct((rows // 2, columns), BF),) * (2 * sides)
    return pl.pallas_call(
        functools.partial(fold_body, joined, sides),
        out_shape=shapes,
        in_specs=[VMEM_SPEC] * len(parts),
        out_specs=(VMEM_SPEC,) * len(shapes),
        cost_estimate=pl.CostEstimate(flops=rows * columns * sides, bytes_accessed=6 * rows * columns * sides, transcendentals=0),
        compiler_params=pltpu.CompilerParams(vmem_limit_bytes=32 * 1024 * 1024),
        name="fold",
    )(*parts)


def exchanged(value, bit, count):
    return lax.ppermute(value, "dp", [(i, i ^ (1 << bit)) for i in range(count)])


def cube_sum(halves_in, count):
    keep_a, send_a, keep_b, send_b = halves_in
    first, second = bit_orders(count)
    levels = len(first)
    parts = (keep_a, exchanged(send_a, first[0], count), keep_b, exchanged(send_b, second[0], count))
    keep_a, send_a, keep_b, send_b = fold(parts, False, False)
    parts = (keep_a, exchanged(send_a, first[1], count), keep_b, exchanged(send_b, second[1], count))
    keep, send = fold(parts, True, False)
    for level in range(2, levels):
        result = fold((keep, exchanged(send, first[level], count)), False, level == levels - 1)
        if level < levels - 1:
            keep, send = result
    return result[0]


def padded_memory_body(source, target):
    rows = source.shape[1]
    target[...] = jnp.zeros_like(target)
    target[:rows, :] = source[0]


def padded_memory(memory, padded):
    images, rows, width = memory.shape
    return pl.pallas_call(
        padded_memory_body,
        grid=(images,),
        out_shape=jax.ShapeDtypeStruct((images * padded, width), memory.dtype),
        in_specs=[pl.BlockSpec((1, rows, width), lambda i: (i, 0, 0))],
        out_specs=pl.BlockSpec((padded, width), lambda i: (i, 0)),
        cost_estimate=pl.CostEstimate(flops=0, bytes_accessed=4 * images * padded * width, transcendentals=0),
        name="padded_memory",
    )(memory)


def memory_total_body(where, own, other, mine, theirs, target):
    image = pl.program_id(0)
    rows = target.shape[1]
    half = mine.shape[1]
    last = jnp.where(image == where[0], 1.0, 0.0)
    first_core = where[1] == 0
    target_rows = slice(0, rows)
    for side in range(2):
        columns = slice(side * half, (side + 1) * half)
        extra = jnp.where(first_core if side == 0 else jnp.logical_not(first_core), mine[...].astype(F32), theirs[...].astype(F32))
        total = own[:, columns].astype(F32) + other[:, columns].astype(F32) + last * extra
        target[0, target_rows, columns] = total[:rows].astype(BF)


def memory_total(rows, where, own, other, mine, theirs):
    padded = mine.shape[0]
    images, width = own.shape[0] // padded, own.shape[1]
    block = pl.BlockSpec((padded, width), lambda i: (i, 0))
    half = pl.BlockSpec(mine.shape, lambda i: (0, 0))
    return pl.pallas_call(
        memory_total_body,
        grid=(images,),
        out_shape=jax.ShapeDtypeStruct((images, rows, width), BF),
        in_specs=[SMEM_SPEC, block, block, half, half],
        out_specs=pl.BlockSpec((1, rows, width), lambda i: (i, 0, 0)),
        compiler_params=pltpu.CompilerParams(vmem_limit_bytes=32 * 1024 * 1024),
        cost_estimate=pl.CostEstimate(flops=0, bytes_accessed=8 * images * padded * width, transcendentals=0),
        name="memory_total",
    )(where, own, other, mine, theirs)


def core_swap(value):
    return lax.ppermute(value, "tensor", [(0, 1), (1, 0)])


def core_half(value, core):
    half = value.shape[1] // 2
    return jnp.where(core == 0, value[:, :half], value[:, half:])


def other_half(value, core):
    half = value.shape[1] // 2
    return jnp.where(core == 0, value[:, half:], value[:, :half])


def rejoined(mine, theirs, core):
    return jnp.concatenate([jnp.where(core == 0, mine, theirs), jnp.where(core == 0, theirs, mine)], 1)


def fetched(value, core):
    mine = shifted(core_half(value, core), "dp", 1)
    return rejoined(mine, core_swap(mine), core)


def given_back(partial, core):
    low = partial.astype(BF)
    total = core_half(low, core).astype(F32) + core_swap(other_half(low, core)).astype(F32)
    mine = shifted(total.astype(BF), "dp", -1)
    return mine, core_swap(mine)


def two_level_scatter(stacked, count):
    inner = min(4, count)
    outer = count // inner
    near = [[o * inner + i for i in range(inner)] for o in range(outer)]
    far = [[o * inner + i for o in range(outer)] for i in range(inner)]
    first = lax.psum_scatter(stacked, "dp", scatter_dimension=0, axis_index_groups=near, tiled=True)
    return lax.psum_scatter(first, "dp", scatter_dimension=0, axis_index_groups=far, tiled=True)


def per_device(
    tokens,
    page_ids,
    image_of_page,
    memory,
    ln0_gain,
    ln0_bias,
    w_self_query,
    b_self_query,
    w_self_key,
    w_self_value,
    b_self_value,
    w_self_out,
    b_self_out,
    ln1_gain,
    ln1_bias,
    w_query,
    b_query,
    w_key,
    w_value,
    b_value,
    w_out,
    b_out,
    ln2_gain,
    ln2_bias,
    w_up,
    b_up,
    w_down,
    b_down,
    cotangent,
):
    count = lax.axis_size("dp")
    me = lax.axis_index("dp")
    core = lax.axis_index("tensor")
    row_count, width = tokens.shape
    image_count, memory_rows = (memory.shape[0], memory.shape[1])
    scale = 1.0 / math.sqrt(HEAD_WIDTH)
    padded_rows = -(-memory_rows // 16) * 16
    first_page = me * image_count
    local_page = page_ids - first_page
    begins = [jnp.sum((local_page < page).astype(jnp.int32)) for page in range(image_count)]
    prior_begin = shifted(jnp.full((128,), begins[1], jnp.int32), "dp", 1)[0]
    slots = [jnp.int32(image_count)] + [image_of_page[page] - first_page for page in range(image_count)]
    meta = jnp.stack(begins + [prior_begin] + slots).astype(jnp.int32)
    last_image = image_of_page[image_count - 1] - first_page
    skipped = row_count // 4
    prior_tokens = fetched(tokens[skipped:], core)
    flat_memory = padded_memory(memory, padded_rows)
    prior_memory = fetched(
        lax.dynamic_slice_in_dim(flat_memory, last_image * padded_rows, padded_rows, 0), core
    )

    def project(rows, weight, bias=None):
        product = jnp.dot(rows, weight, preferred_element_type=F32)
        return (product if bias is None else product + bias).astype(BF)

    def back(grads, weight):
        return jnp.einsum("th,dh->td", grads, weight, preferred_element_type=F32)

    input_values = tokens.astype(F32)
    hidden_zero, self_normed_rows, inverse_zero = layer_norm(input_values, ln0_gain, ln0_bias)
    hidden_zero = hidden_zero.astype(BF)
    self_queries = (
        (jnp.dot(hidden_zero, w_self_query, preferred_element_type=F32) + b_self_query) * scale
    ).astype(BF)
    self_key_rows = project(hidden_zero, w_self_key)
    self_values = project(hidden_zero, w_self_value, b_self_value)
    keys_here = project(flat_memory, w_key)
    values_here = project(flat_memory, w_value, b_value)
    prior_hidden = layer_norm(prior_tokens.astype(F32), ln0_gain, ln0_bias)[0].astype(BF)
    prior_keys = project(prior_hidden, w_self_key)
    prior_values = project(prior_hidden, w_self_value, b_self_value)
    self_attended, self_logs = self_forward(
        meta, self_queries, prior_keys, self_key_rows, prior_values, self_values
    )
    self_part = project(self_attended, w_self_out)
    self_other = core_swap(self_part)
    prior_image_keys = project(prior_memory, w_key)
    prior_image_values = project(prior_memory, w_value, b_value)
    start = input_values + (self_part.astype(F32) + self_other.astype(F32)) + b_self_out
    hidden_one, normed_one, inverse_one = layer_norm(start, ln1_gain, ln1_bias)
    hidden_one = hidden_one.astype(BF)
    queries = (
        (jnp.dot(hidden_one, w_query, preferred_element_type=F32) + b_query) * scale
    ).astype(BF)
    attended, log_totals = cross_forward(
        memory_rows, meta, queries, prior_image_keys, keys_here, prior_image_values, values_here
    )
    cross_part = project(attended, w_out)
    cross_other = core_swap(cross_part)
    inner = min(4, count)
    tile = 512
    middle, down_part, grad_part, forward_grads, up_bias_grad = feed_forward(
        inner, count // inner, tile, start, cross_part, cross_other, b_out, ln2_gain, ln2_bias, cotangent, w_up, b_up, w_down
    )
    grad_other = core_swap(grad_part)
    forward_sums = two_level_scatter(forward_grads, count).astype(F32)
    down_other = core_swap(down_part)
    layer_out = (middle + (down_part.astype(F32) + down_other.astype(F32)) + b_down).astype(BF)
    grad_outer = cotangent.astype(F32)
    down_bias_grad = jnp.sum(grad_outer, axis=0)
    unused_hidden, normed_two, inverse_two = layer_norm(middle, ln2_gain, ln2_bias)
    back_two, gain_two_grad, bias_two_grad = norm_back(
        grad_part.astype(F32) + grad_other.astype(F32), normed_two, inverse_two, ln2_gain
    )
    grad_middle = grad_outer + back_two
    grad_branch = grad_middle.astype(BF)
    out_bias_grad = jnp.sum(grad_branch.astype(F32), axis=0)
    grad_attended = jnp.einsum("td,hd->th", grad_branch, w_out, preferred_element_type=F32).astype(BF)
    prior_image_key_grads, key_grads, prior_image_value_grads, value_grads, grad_queries = cross_back(
        memory_rows,
        meta,
        queries,
        grad_attended,
        attended,
        log_totals,
        prior_image_keys,
        keys_here,
        prior_image_values,
        values_here,
    )
    hidden_part = (back(grad_queries, w_query) * scale).astype(BF)
    hidden_other = core_swap(hidden_part)
    me_list = jnp.full((1,), me, jnp.int32)
    cross_sums = cube_sum(
        weight_grads(
            count,
            me_list,
            (hidden_one, flat_memory, prior_memory, grad_branch),
            (grad_queries, key_grads, prior_image_key_grads, value_grads, prior_image_value_grads, attended),
            (
                (((0, 0),), scale),
                (((1, 1), (2, 2)), 1.0),
                (((1, 3), (2, 4)), 1.0),
                (((3, 5),), 1.0),
            ),
        ),
        count,
    )
    memory_back = given_back(back(prior_image_key_grads, w_key) + back(prior_image_value_grads, w_value), core)
    memory_part = (back(key_grads, w_key) + back(value_grads, w_value)).astype(BF)
    memory_other = core_swap(memory_part)
    value_bias_grad = jnp.sum(value_grads.astype(F32), axis=0) + jnp.sum(prior_image_value_grads.astype(F32), axis=0)
    query_bias_grad = jnp.sum(grad_queries.astype(F32), axis=0) * scale
    back_one, gain_one_grad, bias_one_grad = norm_back(
        hidden_part.astype(F32) + hidden_other.astype(F32), normed_one, inverse_one, ln1_gain
    )
    grad_start = grad_middle + back_one
    d_memory = memory_total(memory_rows, jnp.stack([last_image, core]), memory_part, memory_other, *memory_back)
    grad_start_low = grad_start.astype(BF)
    self_out_bias_grad = jnp.sum(grad_start_low.astype(F32), axis=0)
    grad_self_attended = jnp.einsum(
        "td,hd->th", grad_start_low, w_self_out, preferred_element_type=F32
    ).astype(BF)
    prior_key_grads, prior_value_grads, prior_query_grads = self_prior_back(
        meta, self_queries, grad_self_attended, self_attended, self_logs, prior_keys, prior_values
    )
    zero_back = given_back(back(prior_key_grads, w_self_key) + back(prior_value_grads, w_self_value), core)
    self_key_grads, self_value_grads, grad_self_queries = self_own_back(
        meta,
        self_queries,
        grad_self_attended,
        self_attended,
        self_logs,
        self_key_rows,
        self_values,
        prior_query_grads,
    )
    zero_part = (
        back(grad_self_queries, w_self_query) * scale
        + back(self_key_grads, w_self_key)
        + back(self_value_grads, w_self_value)
    ).astype(BF)
    zero_other = core_swap(zero_part)
    self_sums = cube_sum(
        weight_grads(
            count,
            me_list,
            (hidden_zero, prior_hidden, grad_start_low),
            (grad_self_queries, self_key_grads, prior_key_grads, self_value_grads, prior_value_grads, self_attended),
            (
                (((0, 0),), scale),
                (((0, 1), (1, 2)), 1.0),
                (((0, 3), (1, 4)), 1.0),
                (((2, 5),), 1.0),
            ),
        ),
        count,
    )
    self_query_bias_grad = jnp.sum(grad_self_queries.astype(F32), axis=0) * scale
    self_value_bias_grad = jnp.sum(self_value_grads.astype(F32), axis=0) + jnp.sum(prior_value_grads.astype(F32), axis=0)
    returned_rows = jnp.pad(rejoined(*zero_back, core), ((skipped, 0), (0, 0)))
    grad_hidden_zero = zero_part.astype(F32) + zero_other.astype(F32) + returned_rows.astype(F32)
    back_zero, gain_zero_grad, bias_zero_grad = norm_back(
        grad_hidden_zero, self_normed_rows, inverse_zero, ln0_gain
    )
    d_tokens = (grad_start + back_zero).astype(BF)
    small_sums = butterfly_sum(
        (
            gain_zero_grad,
            bias_zero_grad,
            self_query_bias_grad,
            self_value_bias_grad,
            self_out_bias_grad,
            gain_one_grad,
            bias_one_grad,
            query_bias_grad,
            value_bias_grad,
            out_bias_grad,
            gain_two_grad,
            bias_two_grad,
            up_bias_grad[0],
            down_bias_grad,
        )
    )
    local = w_query.shape[1]

    def cut(table, number):
        return table[:, number * local : (number + 1) * local]

    pieces = forward_sums.reshape(forward_sums.shape[0], -1, 2, tile)
    summed_up = pieces[:, :, 0].reshape(forward_sums.shape[0], -1)
    summed_down = pieces[:, :, 1].reshape(forward_sums.shape[0], -1).T
    return (
        layer_out,
        d_tokens,
        d_memory,
        small_sums[0],
        small_sums[1],
        cut(self_sums, 0),
        small_sums[2],
        cut(self_sums, 1),
        cut(self_sums, 2),
        small_sums[3],
        cut(self_sums, 3).T,
        small_sums[4],
        small_sums[5],
        small_sums[6],
        cut(cross_sums, 0),
        small_sums[7],
        cut(cross_sums, 1),
        cut(cross_sums, 2),
        small_sums[8],
        cut(cross_sums, 3).T,
        small_sums[9],
        small_sums[10],
        small_sums[11],
        summed_up,
        small_sums[12],
        summed_down,
        small_sums[13],
    )


def solution(mesh):
    in_specs = (
        P("dp", None),
        P("dp"),
        P("dp"),
        P("dp", None, None),
        P(),
        P(),
        P(None, "tensor"),
        P("tensor"),
        P(None, "tensor"),
        P(None, "tensor"),
        P("tensor"),
        P("tensor", None),
        P(),
        P(),
        P(),
        P(None, "tensor"),
        P("tensor"),
        P(None, "tensor"),
        P(None, "tensor"),
        P("tensor"),
        P("tensor", None),
        P(),
        P(),
        P(),
        P(None, "tensor"),
        P("tensor"),
        P("tensor", None),
        P(),
        P("dp", None),
    )
    out_specs = (
        P("dp", None),
        P("dp", None),
        P("dp", None, None),
        P(),
        P(),
        P("dp", "tensor"),
        P("tensor"),
        P("dp", "tensor"),
        P("dp", "tensor"),
        P("tensor"),
        P("tensor", "dp"),
        P(),
        P(),
        P(),
        P("dp", "tensor"),
        P("tensor"),
        P("dp", "tensor"),
        P("dp", "tensor"),
        P("tensor"),
        P("tensor", "dp"),
        P(),
        P(),
        P(),
        P("dp", "tensor"),
        P("tensor"),
        P("tensor", "dp"),
        P(),
    )
    return jax.shard_map(
        per_device, mesh=mesh, in_specs=in_specs, out_specs=out_specs, check_vma=False
    )
```

```python
import functools
import math

import jax
import jax.numpy as jnp
from jax import lax
from jax.experimental import pallas as pl
from jax.experimental.pallas import tpu as pltpu
from jax.sharding import PartitionSpec as P

HEAD_WIDTH = 64


EPSILON = 1e-05


def shifted(value, axis, steps):
    count = lax.axis_size(axis)
    initial, last = (max(0, -steps), min(count, count - steps))
    return lax.ppermute(value, axis, [(source, source + steps) for source in range(initial, last)])


def butterfly_sum(vectors):
    sizes = [vector.shape[0] for vector in vectors]
    total = jnp.concatenate(vectors).reshape(-1, 128)
    count = lax.axis_size("dp")
    bit = 1
    while bit < count:
        total = total + lax.ppermute(total, "dp", [(i, i ^ bit) for i in range(count)])
        bit *= 2
    flat = total.reshape(-1)
    pieces, at = [], 0
    for size in sizes:
        pieces.append(flat[at : at + size])
        at += size
    return pieces


BF = jnp.bfloat16
F32 = jnp.float32
NEG = -1e30
TILE = 256
HEAD_WIDTH = 64
PAIR = 2 * HEAD_WIDTH
MIB = 1024 * 1024


def nt(left, right):
    return lax.dot_general(left, right, (((1,), (1,)), ((), ())), preferred_element_type=F32)


def nn(left, right):
    return lax.dot_general(left, right, (((1,), (0,)), ((), ())), preferred_element_type=F32)


def head_half(pair, half):
    lane = lax.broadcasted_iota(jnp.int32, pair.shape, 1)
    keep = lane < HEAD_WIDTH if half == 0 else lane >= HEAD_WIDTH
    return jnp.where(keep, pair, jnp.zeros_like(pair))


def span(index, size=TILE):
    return pl.ds(pl.multiple_of(index * size, size), size)


HEAD_ROWS = 80


def column_max(values):
    rows = values.shape[0]
    groups = max(1, rows // 64)
    step = -(-(rows // groups) // 8) * 8
    parts = []
    at = 0
    while at < rows:
        end = min(rows, at + step)
        parts.append(jnp.max(values[at:end], axis=0, keepdims=True))
        at = end
    while len(parts) > 1:
        parts = [jnp.maximum(*parts[i : i + 2]) if i + 1 < len(parts) else parts[i] for i in range(0, len(parts), 2)]
    return parts[0]


def extended(values, target, columns):
    turned = values.T
    extra = jnp.where(lax.broadcasted_iota(jnp.int32, (HEAD_ROWS - HEAD_WIDTH, turned.shape[1]), 0) == 0, 1.0, 0.0).astype(BF)
    for h in range(turned.shape[0] // HEAD_WIDTH):
        base = h * HEAD_ROWS
        target[base : base + HEAD_WIDTH, columns] = turned[h * HEAD_WIDTH : (h + 1) * HEAD_WIDTH, :]
        target[base + HEAD_WIDTH : base + HEAD_ROWS, columns] = extra


def lane_rows(i):
    return i * TILE + lax.broadcasted_iota(jnp.int32, (1, TILE), 1)


def self_forward_body(meta, q_ref, kp_ref, k_ref, vp_ref, v_ref, o_ref, log_ref,
                      vpt, vt, qm, bias, m_s, acc, done, scores):
    rows = q_ref.shape[0]
    pairs = q_ref.shape[1] // PAIR
    b1, b2, p0 = meta[0], meta[1], meta[2]
    tiles = rows // TILE
    offset = rows - kp_ref.shape[0]
    prior_tiles = kp_ref.shape[0] // TILE
    first_prior = (p0 - offset) // TILE
    prior_rows = (b1 + TILE - 1) // TILE

    def turn_own(j, c):
        extended(v_ref[span(j), :], vt, span(j))
        return c

    lax.fori_loop(0, tiles, turn_own, 0)

    def turn_prior(j, c):
        extended(vp_ref[span(j), :], vpt, span(j))
        return c

    lax.fori_loop(jnp.where(b1 > 0, first_prior, prior_tiles), prior_tiles, turn_prior, 0)

    def key_step(keys, values_t, j):
        for pair in range(pairs):
            key_pair = keys[span(j), pair * PAIR : pair * PAIR + PAIR]
            for half in range(2):
                scores[2 * pair + half] = nt(key_pair, qm[2 * pair + half])
        for pair in range(pairs):
            for half in range(2):
                h = 2 * pair + half
                heads = slice(h * HEAD_ROWS, (h + 1) * HEAD_ROWS)
                s = scores[h] + bias[...]
                m_old = m_s[h : h + 1, :]
                m_new = jnp.maximum(m_old, column_max(s))
                alpha = jnp.exp(m_old - m_new)
                e = jnp.exp(s - m_new)
                m_s[h : h + 1, :] = m_new
                acc[heads, :] = acc[heads, :] * alpha + nn(values_t[heads, span(j)], e.astype(BF))

    def row_tile(i, c):
        t = lane_rows(i)
        start = jnp.where(t < b1, 0, jnp.where(t < b2, b1, b2))
        for pair in range(pairs):
            q_pair = q_ref[span(i), pair * PAIR : pair * PAIR + PAIR]
            for half in range(2):
                qm[2 * pair + half] = head_half(q_pair, half)
        m_s[...] = jnp.full_like(m_s, NEG)
        acc[...] = jnp.zeros_like(acc)

        def prior(j, c2):
            r = offset + j * TILE + lax.broadcasted_iota(jnp.int32, (TILE, TILE), 0)
            bias[...] = jnp.where((r >= p0) & (t < b1), 0.0, NEG)
            key_step(kp_ref, vpt, j)
            return c2

        lax.fori_loop(jnp.where(i < prior_rows, first_prior, prior_tiles), prior_tiles, prior, 0)
        t_first = i * TILE
        lowest = jnp.where(t_first < b1, 0, jnp.where(t_first < b2, b1, b2))

        def own(j, c2):
            r = j * TILE + lax.broadcasted_iota(jnp.int32, (TILE, TILE), 0)
            bias[...] = jnp.where((r <= t) & (r >= start), 0.0, NEG)
            key_step(k_ref, vt, j)
            return c2

        lax.fori_loop(lowest // TILE, i + 1, own, 0)
        for h in range(2 * pairs):
            base = h * HEAD_ROWS
            total = acc[base + HEAD_WIDTH : base + HEAD_WIDTH + 1, :]
            log_ref[h : h + 1, span(i)] = m_s[h : h + 1, :] + jnp.log(total)
            done[h * HEAD_WIDTH : (h + 1) * HEAD_WIDTH, :] = acc[base : base + HEAD_WIDTH, :] * (1.0 / total)
        o_ref[span(i), :] = done[...].T.astype(BF)
        return c

    lax.fori_loop(0, tiles, row_tile, 0)


SMEM_SPEC = pl.BlockSpec(memory_space=pltpu.SMEM)
VMEM_SPEC = pl.BlockSpec(memory_space=pltpu.VMEM)


def self_forward(meta, q, k_prior, k, v_prior, v):
    rows, width = q.shape
    heads = width // HEAD_WIDTH
    return pl.pallas_call(
        self_forward_body,
        out_shape=(jax.ShapeDtypeStruct((rows, width), BF), jax.ShapeDtypeStruct((heads, rows), F32)),
        in_specs=[SMEM_SPEC] + [VMEM_SPEC] * 5,
        out_specs=(VMEM_SPEC, VMEM_SPEC),
        scratch_shapes=[
            pltpu.VMEM((heads * HEAD_ROWS, k_prior.shape[0]), BF),
            pltpu.VMEM((heads * HEAD_ROWS, rows), BF),
            pltpu.VMEM((heads, TILE, PAIR), BF),
            pltpu.VMEM((TILE, TILE), F32),
            pltpu.VMEM((heads, TILE), F32),
            pltpu.VMEM((heads * HEAD_ROWS, TILE), F32),
            pltpu.VMEM((width, TILE), F32),
            pltpu.VMEM((heads, TILE, TILE), F32),
        ],
        compiler_params=pltpu.CompilerParams(vmem_limit_bytes=16 * MIB),
        cost_estimate=pl.CostEstimate(flops=2 * 2 * rows * rows * width, bytes_accessed=8 * rows * width * 2, transcendentals=rows * rows * heads),
        name="self_forward",
    )(meta, q, k_prior, k, v_prior, v)


def grad_rows(do_ref, o_ref, i, width):
    heads = width // HEAD_WIDTH
    product = do_ref[span(i), :].astype(F32) * o_ref[span(i), :].astype(F32)
    high = product.astype(BF)
    low = (product - high.astype(F32)).astype(BF)
    head = lax.broadcasted_iota(jnp.int32, (heads, width), 0)
    column = lax.broadcasted_iota(jnp.int32, (heads, width), 1) // HEAD_WIDTH
    pick = jnp.where(head == column, 1.0, 0.0).astype(BF)
    return nt(pick, high) + nt(pick, low)


def halves(source, i, target, pairs):
    for pair in range(pairs):
        value = source[span(i), pair * PAIR : pair * PAIR + PAIR]
        for half in range(2):
            target[2 * pair + half] = head_half(value, half)


def grad_step(pairs, keys, values, keys_t, key_slice, key_lanes, qm, dom, shift, delta, bias, dk, dv, dqt, scores, grads):
    for pair in range(pairs):
        cols = slice(pair * PAIR, pair * PAIR + PAIR)
        key_pair = keys[key_slice, cols]
        value_pair = values[key_slice, cols]
        for half in range(2):
            h = 2 * pair + half
            scores[h] = nt(key_pair, qm[h])
            grads[h] = nt(value_pair, dom[h])
    for pair in range(pairs):
        cols = slice(pair * PAIR, pair * PAIR + PAIR)
        dv_pair = dv[key_slice, cols]
        dk_pair = dk[key_slice, cols]
        for half in range(2):
            h = 2 * pair + half
            heads = slice(h * HEAD_WIDTH, (h + 1) * HEAD_WIDTH)
            s = scores[h]
            if bias is not None:
                s = s + bias[...]
            p = jnp.exp(s - shift[h : h + 1, :])
            dp = grads[h]
            ds = (p * (dp - delta[h : h + 1, :])).astype(BF)
            dv_pair = dv_pair + nn(p.astype(BF), dom[h])
            dk_pair = dk_pair + nn(ds, qm[h])
            dqt[heads, :] = dqt[heads, :] + nn(keys_t[heads, key_lanes], ds)
        dv[key_slice, cols] = dv_pair
        dk[key_slice, cols] = dk_pair


def self_prior_back_body(meta, q_ref, do_ref, o_ref, log_ref, k_ref, v_ref, dk_ref, dv_ref, dq_ref,
                         kt, qm, dom, bias, delta, shift, dqt, dk, dv, scores, grads):
    rows, width = q_ref.shape
    pairs = width // PAIR
    b1, p0 = meta[0], meta[2]
    tiles = rows // TILE
    offset = rows - k_ref.shape[0]
    prior_tiles = k_ref.shape[0] // TILE
    first_prior = (p0 - offset) // TILE
    prior_rows = (b1 + TILE - 1) // TILE
    dk[...] = jnp.zeros_like(dk)
    dv[...] = jnp.zeros_like(dv)

    def turn(j, c):
        kt[:, span(j)] = k_ref[span(j), :].T
        return c

    lax.fori_loop(jnp.where(b1 > 0, first_prior, prior_tiles), prior_tiles, turn, 0)

    def row_tile(i, c):
        dqt[...] = jnp.zeros_like(dqt)
        t = lane_rows(i)

        @pl.when(i < prior_rows)
        def _():
            halves(q_ref, i, qm, pairs)
            halves(do_ref, i, dom, pairs)
            delta[...] = grad_rows(do_ref, o_ref, i, width)
            shift[...] = log_ref[:, span(i)]

        def prior(j, c2):
            r = offset + j * TILE + lax.broadcasted_iota(jnp.int32, (TILE, TILE), 0)
            bias[...] = jnp.where((r >= p0) & (t < b1), 0.0, NEG)
            grad_step(pairs, k_ref, v_ref, kt, span(j), span(j), qm, dom, shift, delta, bias, dk, dv, dqt, scores, grads)
            return c2

        lax.fori_loop(jnp.where(i < prior_rows, first_prior, prior_tiles), prior_tiles, prior, 0)
        dq_ref[span(i), :] = dqt[...].T
        return c

    lax.fori_loop(0, tiles, row_tile, 0)
    dk_ref[...] = dk[...].astype(BF)
    dv_ref[...] = dv[...].astype(BF)


def self_own_back_body(meta, q_ref, do_ref, o_ref, log_ref, k_ref, v_ref, dqp_ref, dk_ref, dv_ref, dq_ref,
                       kt, qm, dom, bias, delta, shift, dqt, dk, dv, scores, grads):
    rows, width = q_ref.shape
    pairs = width // PAIR
    b1, b2 = meta[0], meta[1]
    tiles = rows // TILE
    dk[...] = jnp.zeros_like(dk)
    dv[...] = jnp.zeros_like(dv)

    def turn(j, c):
        kt[:, span(j)] = k_ref[span(j), :].T
        return c

    lax.fori_loop(0, tiles, turn, 0)

    def row_tile(i, c):
        dqt[...] = jnp.zeros_like(dqt)
        t = lane_rows(i)
        start = jnp.where(t < b1, 0, jnp.where(t < b2, b1, b2))
        halves(q_ref, i, qm, pairs)
        halves(do_ref, i, dom, pairs)
        delta[...] = grad_rows(do_ref, o_ref, i, width)
        shift[...] = log_ref[:, span(i)]
        t_first = i * TILE
        lowest = jnp.where(t_first < b1, 0, jnp.where(t_first < b2, b1, b2))

        def own(j, c2):
            r = j * TILE + lax.broadcasted_iota(jnp.int32, (TILE, TILE), 0)
            bias[...] = jnp.where((r <= t) & (r >= start), 0.0, NEG)
            grad_step(pairs, k_ref, v_ref, kt, span(j), span(j), qm, dom, shift, delta, bias, dk, dv, dqt, scores, grads)
            return c2

        lax.fori_loop(lowest // TILE, i + 1, own, 0)
        dq_ref[span(i), :] = (dqp_ref[span(i), :] + dqt[...].T).astype(BF)
        return c

    lax.fori_loop(0, tiles, row_tile, 0)
    dk_ref[...] = dk[...].astype(BF)
    dv_ref[...] = dv[...].astype(BF)


def self_back_scratch(keys, width):
    heads = width // HEAD_WIDTH
    return [
        pltpu.VMEM((width, keys), BF),
        pltpu.VMEM((heads, TILE, PAIR), BF),
        pltpu.VMEM((heads, TILE, PAIR), BF),
        pltpu.VMEM((TILE, TILE), F32),
        pltpu.VMEM((heads, TILE), F32),
        pltpu.VMEM((heads, TILE), F32),
        pltpu.VMEM((width, TILE), F32),
        pltpu.VMEM((keys, width), F32),
        pltpu.VMEM((keys, width), F32),
        pltpu.VMEM((heads, TILE, TILE), F32),
        pltpu.VMEM((heads, TILE, TILE), F32),
    ]


def self_prior_back(meta, q, do, o, logs, k_prior, v_prior):
    rows, width = q.shape
    return pl.pallas_call(
        self_prior_back_body,
        out_shape=(jax.ShapeDtypeStruct(k_prior.shape, BF), jax.ShapeDtypeStruct(k_prior.shape, BF),
                   jax.ShapeDtypeStruct((rows, width), F32)),
        in_specs=[SMEM_SPEC] + [VMEM_SPEC] * 6,
        out_specs=(VMEM_SPEC,) * 3,
        scratch_shapes=self_back_scratch(k_prior.shape[0], width),
        compiler_params=pltpu.CompilerParams(vmem_limit_bytes=22 * MIB),
        cost_estimate=pl.CostEstimate(flops=3 * rows * rows * width, bytes_accessed=8 * rows * width * 2, transcendentals=rows * rows * 4),
        name="self_prior_back",
    )(meta, q, do, o, logs, k_prior, v_prior)


def self_own_back(meta, q, do, o, logs, k, v, dq_prior):
    rows, width = q.shape
    return pl.pallas_call(
        self_own_back_body,
        out_shape=(jax.ShapeDtypeStruct((rows, width), BF),) * 3,
        in_specs=[SMEM_SPEC] + [VMEM_SPEC] * 7,
        out_specs=(VMEM_SPEC,) * 3,
        scratch_shapes=self_back_scratch(rows, width),
        compiler_params=pltpu.CompilerParams(vmem_limit_bytes=26 * MIB),
        cost_estimate=pl.CostEstimate(flops=5 * rows * rows * width, bytes_accessed=8 * rows * width * 2, transcendentals=rows * rows * 4),
        name="self_own_back",
    )(meta, q, do, o, logs, k, v, dq_prior)


def segments(meta, rows):
    return ((0, meta[0], None), (meta[0], meta[1], meta[4]), (meta[1], rows, meta[5]))


def cross_forward_body(used, meta, q_ref, kp_ref, k_ref, vp_ref, v_ref, o_ref, log_ref, vpt, vt, qm, acc, scores):
    rows, width = q_ref.shape
    pairs = width // PAIR
    padded = kp_ref.shape[0]
    images = k_ref.shape[0] // padded
    for slot in range(images):
        extended(v_ref[slot * padded : (slot + 1) * padded, :], vt.at[slot], slice(None))
    extended(vp_ref[...], vpt, slice(None))
    for first, last, slot in segments(meta, rows):
        own = slot is not None
        keys = pl.ds(pl.multiple_of(slot * padded, 16), padded) if own else slice(None)
        key_table = k_ref if own else kp_ref
        value_table = vt.at[slot] if own else vpt

        def tile(i, c):
            halves(q_ref, i, qm, pairs)
            t = lane_rows(i)
            inside = (t >= first) & (t < last)
            for pair in range(pairs):
                key_pair = key_table[keys, pair * PAIR : pair * PAIR + PAIR]
                for half in range(2):
                    scores[2 * pair + half] = nt(key_pair, qm[2 * pair + half])
            for h in range(2 * pairs):
                heads = slice(h * HEAD_WIDTH, (h + 1) * HEAD_WIDTH)
                s = scores[h]
                if used < padded:
                    row = lax.broadcasted_iota(jnp.int32, s.shape, 0)
                    s = jnp.where(row < used, s, NEG)
                m = column_max(s)
                e = jnp.exp(s - m)
                mixed = nn(value_table[h * HEAD_ROWS : (h + 1) * HEAD_ROWS, :], e.astype(BF))
                total = mixed[HEAD_WIDTH : HEAD_WIDTH + 1, :]
                acc[heads, :] = mixed[:HEAD_WIDTH, :] * (1.0 / total)
                log_ref[h : h + 1, span(i)] = jnp.where(
                    inside, m + jnp.log(total), log_ref[h : h + 1, span(i)]
                )
            column = i * TILE + lax.broadcasted_iota(jnp.int32, (TILE, width), 0)
            keep = (column >= first) & (column < last)
            o_ref[span(i), :] = jnp.where(keep, acc[...].T, o_ref[span(i), :].astype(F32)).astype(BF)
            return c

        lax.fori_loop(first // TILE, jnp.where(last > first, (last + TILE - 1) // TILE, 0), tile, 0)


def cross_forward(used, meta, q, k_prior, k, v_prior, v):
    rows, width = q.shape
    heads = width // HEAD_WIDTH
    padded = k_prior.shape[0]
    return pl.pallas_call(
        functools.partial(cross_forward_body, used),
        out_shape=(jax.ShapeDtypeStruct((rows, width), BF), jax.ShapeDtypeStruct((heads, rows), F32)),
        in_specs=[SMEM_SPEC] + [VMEM_SPEC] * 5,
        out_specs=(VMEM_SPEC, VMEM_SPEC),
        scratch_shapes=[
            pltpu.VMEM((heads * HEAD_ROWS, padded), BF),
            pltpu.VMEM((k.shape[0] // padded, heads * HEAD_ROWS, padded), BF),
            pltpu.VMEM((heads, TILE, PAIR), BF),
            pltpu.VMEM((width, TILE), F32),
            pltpu.VMEM((heads, padded, TILE), F32),
        ],
        compiler_params=pltpu.CompilerParams(vmem_limit_bytes=20 * MIB),
        cost_estimate=pl.CostEstimate(flops=16 * rows * padded * width, bytes_accessed=8 * rows * width * 2, transcendentals=rows * padded * heads),
        name="cross_forward",
    )(meta, q, k_prior, k, v_prior, v)


def cross_back_body(used, meta, q_ref, do_ref, o_ref, log_ref, kp_ref, k_ref, vp_ref, v_ref, dkp_ref, dk_ref, dvp_ref, dv_ref,
                    dq_ref, kpt, kt, qm, dom, delta, shift, dqt, dkp, dk, dvp, dv, scores, grads):
    rows, width = q_ref.shape
    pairs = width // PAIR
    padded = kp_ref.shape[0]
    images = k_ref.shape[0] // padded
    for item in (dkp, dk, dvp, dv):
        item[...] = jnp.zeros_like(item)
    for slot in range(images):
        kt[slot] = k_ref[slot * padded : (slot + 1) * padded, :].T
    kpt[...] = kp_ref[...].T
    for first, last, slot in segments(meta, rows):
        own = slot is not None
        keys = pl.ds(pl.multiple_of(slot * padded, 16), padded) if own else slice(None)
        tables = (k_ref, v_ref, kt.at[slot]) if own else (kp_ref, vp_ref, kpt)
        sums = (dk, dv) if own else (dkp, dvp)

        def tile(i, c):
            halves(q_ref, i, qm, pairs)
            halves(do_ref, i, dom, pairs)
            t = lane_rows(i)
            inside = (t >= first) & (t < last)
            delta[...] = grad_rows(do_ref, o_ref, i, width)
            shift[...] = jnp.where(inside, log_ref[:, span(i)], -NEG)
            dqt[...] = jnp.zeros_like(dqt)
            grad_step(pairs, *tables, keys, slice(None), qm, dom, shift, delta, None, *sums, dqt, scores, grads)
            column = i * TILE + lax.broadcasted_iota(jnp.int32, (TILE, width), 0)
            keep = (column >= first) & (column < last)
            dq_ref[span(i), :] = jnp.where(keep, dqt[...].T, dq_ref[span(i), :].astype(F32)).astype(BF)
            return c

        lax.fori_loop(first // TILE, jnp.where(last > first, (last + TILE - 1) // TILE, 0), tile, 0)
    inner = lax.broadcasted_iota(jnp.int32, (padded, width), 0) < used
    for source, target in ((dkp, dkp_ref), (dk, dk_ref), (dvp, dvp_ref), (dv, dv_ref)):
        for slot in range(source.shape[0] // padded):
            part = slice(slot * padded, (slot + 1) * padded)
            target[part, :] = jnp.where(inner, source[part, :], 0.0).astype(BF)


def cross_back(used, meta, q, do, o, logs, k_prior, k, v_prior, v):
    rows, width = q.shape
    heads = width // HEAD_WIDTH
    padded = k_prior.shape[0]
    tables = (k_prior, k, v_prior, v)
    return pl.pallas_call(
        functools.partial(cross_back_body, used),
        out_shape=tuple(jax.ShapeDtypeStruct(table.shape, BF) for table in tables) + (jax.ShapeDtypeStruct((rows, width), BF),),
        in_specs=[SMEM_SPEC] + [VMEM_SPEC] * 8,
        out_specs=(VMEM_SPEC,) * 5,
        scratch_shapes=[
            pltpu.VMEM((width, padded), BF),
            pltpu.VMEM((k.shape[0] // padded, width, padded), BF),
            pltpu.VMEM((heads, TILE, PAIR), BF),
            pltpu.VMEM((heads, TILE, PAIR), BF),
            pltpu.VMEM((heads, TILE), F32),
            pltpu.VMEM((heads, TILE), F32),
            pltpu.VMEM((width, TILE), F32),
        ]
        + [pltpu.VMEM(table.shape, F32) for table in tables]
        + [pltpu.VMEM((heads, padded, TILE), F32)] * 2,
        compiler_params=pltpu.CompilerParams(vmem_limit_bytes=42 * MIB),
        cost_estimate=pl.CostEstimate(flops=40 * rows * padded * width, bytes_accessed=12 * rows * width * 2, transcendentals=rows * padded * heads),
        name="cross_back",
    )(meta, q, do, o, logs, *tables)


SQRT_HALF = 0.7071067811865476
GAUSS = 0.3989422804014327
ROW_CHUNK = 256


def error_function(x):
    x = jnp.clip(x, -4.0, 4.0)
    z = x * x
    top = -2.72614225801306e-10
    for term in (2.77068142495902e-08, -2.10102402082508e-06, -5.69250639462346e-05,
                 -7.34990630326855e-04, -2.95459980854025e-03, -1.60960333262415e-02):
        top = top * z + term
    low = -1.45660718464996e-05
    for term in (-2.13374055278905e-04, -1.68282697438203e-03, -7.37332916720468e-03, -1.42647390514189e-02):
        low = low * z + term
    return x * top / low


def row_norm(values):
    mean = jnp.mean(values, axis=-1, keepdims=True)
    centered = values - mean
    inverse = lax.rsqrt(jnp.mean(centered * centered, axis=-1, keepdims=True) + EPSILON)
    return centered * inverse, inverse


def chunk_place(index, inner, outer):
    return (index % inner) * outer + index // inner


def feed_forward_body(inner, outer, start_ref, own_ref, other_ref, b_out, gain, shift_in, dy_ref, w_up, b_up, w_down,
                      y1_ref, down_ref, dh_ref, grads_ref, db_ref,
                      h2, h2t, dyt, acc_down, acc_dh, u_s, da_s, g_s, du_s):
    step = pl.program_id(0)
    rows, width = dy_ref.shape
    tile = w_up.shape[1]
    chunks = rows // ROW_CHUNK

    @pl.when(step == 0)
    def _():
        for r in range(chunks):
            part = slice(r * ROW_CHUNK, (r + 1) * ROW_CHUNK)
            y1 = start_ref[part, :] + (own_ref[part, :].astype(F32) + other_ref[part, :].astype(F32)) + b_out[...]
            y1_ref[part, :] = y1
            normed, _ = row_norm(y1)
            low = (normed * gain[...] + shift_in[...]).astype(BF)
            h2[part, :] = low
            h2t[:, part] = low.T
            dyt[:, part] = dy_ref[part, :].T
        acc_down[...] = jnp.zeros_like(acc_down)
        acc_dh[...] = jnp.zeros_like(acc_dh)

    for r in range(chunks):
        part = slice(r * ROW_CHUNK, (r + 1) * ROW_CHUNK)
        u_s[part, :] = nn(h2[part, :], w_up[...]) + b_up[...]
        da_s[part, :] = nt(dy_ref[part, :], w_down[...])
    total = jnp.zeros((1, tile), F32)
    for r in range(chunks):
        part = slice(r * ROW_CHUNK, (r + 1) * ROW_CHUNK)
        u = u_s[part, :]
        half = 0.5 + 0.5 * error_function(u * SQRT_HALF)
        g = (u * half).astype(BF)
        slope = half + u * (GAUSS * jnp.exp(-0.5 * u * u))
        du = (da_s[part, :] * slope).astype(BF)
        g_s[part, :] = g
        du_s[part, :] = du
        total = total + jnp.sum(du.astype(F32), axis=0, keepdims=True)
        down = nn(g, w_down[...])
        dh = nt(du, w_up[...])
        acc_down[part, :] += down
        acc_dh[part, :] += dh

    db_ref[...] = total
    piece = width // (inner * outer)
    for source, turned, at in ((du_s, h2t, 0), (g_s, dyt, tile)):
        for r in range(width // ROW_CHUNK):
            part = slice(r * ROW_CHUNK, (r + 1) * ROW_CHUNK)
            product = nn(turned[part, :], source[...]).astype(BF)
            for c in range(ROW_CHUNK // piece):
                place = chunk_place(r * (ROW_CHUNK // piece) + c, inner, outer) * piece
                grads_ref[place : place + piece, at : at + tile] = product[c * piece : (c + 1) * piece, :]

    @pl.when(step == pl.num_programs(0) - 1)
    def _():
        down_ref[...] = acc_down[...].astype(BF)
        dh_ref[...] = acc_dh[...].astype(BF)


def feed_forward(inner, outer, tile, start, own, other, b_out, gain, shift_in, dy, w_up, b_up, w_down):
    rows, width = dy.shape
    hidden = w_up.shape[1]
    whole = lambda shape: pl.BlockSpec(shape, lambda k: (0, 0), pipeline_mode=pl.Buffered(1))
    row = whole((1, width))
    full = whole((rows, width))
    return pl.pallas_call(
        functools.partial(feed_forward_body, inner, outer),
        grid=(hidden // tile,),
        out_shape=(
            jax.ShapeDtypeStruct((rows, width), F32),
            jax.ShapeDtypeStruct((rows, width), BF),
            jax.ShapeDtypeStruct((rows, width), BF),
            jax.ShapeDtypeStruct((width, 2 * hidden), BF),
            jax.ShapeDtypeStruct((1, hidden), F32),
        ),
        in_specs=[full, full, full, row, row, row, full,
                  pl.BlockSpec((width, tile), lambda k: (0, k)),
                  pl.BlockSpec((1, tile), lambda k: (0, k)),
                  pl.BlockSpec((tile, width), lambda k: (k, 0))],
        out_specs=(full, full, full, pl.BlockSpec((width, 2 * tile), lambda k: (0, k)), pl.BlockSpec((1, tile), lambda k: (0, k))),
        scratch_shapes=[
            pltpu.VMEM((rows, width), BF),
            pltpu.VMEM((width, rows), BF),
            pltpu.VMEM((width, rows), BF),
            pltpu.VMEM((rows, width), F32),
            pltpu.VMEM((rows, width), F32),
            pltpu.VMEM((rows, tile), F32),
            pltpu.VMEM((rows, tile), F32),
            pltpu.VMEM((rows, tile), BF),
            pltpu.VMEM((rows, tile), BF),
        ],
        compiler_params=pltpu.CompilerParams(vmem_limit_bytes=54 * MIB),
        cost_estimate=pl.CostEstimate(flops=12 * rows * width * hidden, bytes_accessed=30 * rows * width, transcendentals=rows * hidden * 2),
        name="feed_forward",
    )(start, own, other, b_out.reshape(1, -1), gain.reshape(1, -1), shift_in.reshape(1, -1), dy, w_up, b_up.reshape(1, -1), w_down)

def norm_project_body(flags, weight_flags, *refs):
    has_extra, emit_base, emit_hidden = flags
    refs = list(refs)
    values = refs.pop(0)[...].astype(F32)
    if has_extra:
        own, other, offset = refs.pop(0), refs.pop(0), refs.pop(0)
        values = values + (own[...].astype(F32) + other[...].astype(F32)) + offset[...]
    gain, shift_in = refs.pop(0), refs.pop(0)
    weights = []
    for has_bias, factor in weight_flags:
        weight = refs.pop(0)
        weights.append((weight, refs.pop(0) if has_bias else None, factor))
    if emit_base:
        refs.pop(0)[...] = values
    normed, _ = row_norm(values)
    hidden = (normed * gain[...] + shift_in[...]).astype(BF)
    if emit_hidden:
        refs.pop(0)[...] = hidden
    for weight, offset, factor in weights:
        product = nn(hidden, weight[...])
        if offset is not None:
            product = product + offset[...]
        if factor != 1.0:
            product = product * factor
        refs.pop(0)[...] = product.astype(BF)


def norm_project(base, extra, gain, shift_in, weights, emit_base, emit_hidden):
    rows, width = base.shape
    tile = ROW_CHUNK
    block = pl.BlockSpec((tile, width), lambda i: (i, 0))
    fixed = lambda shape: pl.BlockSpec(shape, lambda i: (0, 0), pipeline_mode=pl.Buffered(1))
    operands, specs = [base], [block]
    if extra is not None:
        own, other, offset = extra
        operands += [own, other, offset.reshape(1, -1)]
        specs += [block, block, fixed((1, width))]
    operands += [gain.reshape(1, -1), shift_in.reshape(1, -1)]
    specs += [fixed((1, width))] * 2
    shapes, outs = [], []
    if emit_base:
        shapes.append(jax.ShapeDtypeStruct((rows, width), F32))
        outs.append(block)
    if emit_hidden:
        shapes.append(jax.ShapeDtypeStruct((rows, width), BF))
        outs.append(block)
    for weight, offset, _ in weights:
        operands.append(weight)
        specs.append(fixed(weight.shape))
        if offset is not None:
            operands.append(offset.reshape(1, -1))
            specs.append(fixed((1, weight.shape[1])))
        shapes.append(jax.ShapeDtypeStruct((rows, weight.shape[1]), BF))
        outs.append(pl.BlockSpec((tile, weight.shape[1]), lambda i: (i, 0)))
    flops = sum(2 * rows * width * weight.shape[1] for weight, _, _ in weights)
    return pl.pallas_call(
        functools.partial(norm_project_body, (extra is not None, emit_base, emit_hidden),
                          tuple((offset is not None, factor) for _, offset, factor in weights)),
        grid=(rows // tile,),
        out_shape=tuple(shapes),
        in_specs=specs,
        out_specs=tuple(outs),
        compiler_params=pltpu.CompilerParams(vmem_limit_bytes=12 * MIB),
        cost_estimate=pl.CostEstimate(flops=2 * flops, bytes_accessed=10 * rows * width, transcendentals=0),
        name="norm_project",
    )(*operands)


def norm_back_body(flags, *refs):
    skip, has_back, has_weight, emit_wide = flags
    refs = list(refs)
    core = refs.pop(0)
    own, other, base, grad, gain = (refs.pop(0) for _ in range(5))
    step = pl.program_id(0)
    total = own[...].astype(F32) + other[...].astype(F32)
    if has_back:
        mine, theirs = refs.pop(0)[...].astype(F32), refs.pop(0)[...].astype(F32)
        first = core[0] == 0
        back = jnp.concatenate([jnp.where(first, mine, theirs), jnp.where(first, theirs, mine)], 1)
        total = total + jnp.where(step >= skip, back, 0.0)
    if has_weight:
        weight = refs.pop(0)
    normed, inverse = row_norm(base[...].astype(F32))
    scaled = total * gain[...]
    inner = (
        scaled
        - jnp.mean(scaled, axis=-1, keepdims=True)
        - normed * jnp.mean(scaled * normed, axis=-1, keepdims=True)
    )
    result = grad[...].astype(F32) + inner * inverse
    if emit_wide:
        refs.pop(0)[...] = result
    low = result.astype(BF)
    refs.pop(0)[...] = low
    if has_weight:
        refs.pop(0)[...] = nt(low, weight[...]).astype(BF)
    sums = refs.pop(0)

    @pl.when(step == 0)
    def _():
        sums[...] = jnp.zeros_like(sums)

    sums[0:1, :] += jnp.sum(total * normed, axis=0, keepdims=True)
    sums[1:2, :] += jnp.sum(total, axis=0, keepdims=True)
    if has_weight:
        sums[2:3, :] += jnp.sum(low.astype(F32), axis=0, keepdims=True)
        if grad.dtype == BF:
            sums[3:4, :] += jnp.sum(grad[...].astype(F32), axis=0, keepdims=True)


def norm_back(core, own, other, base, grad, gain, returned, weight, emit_wide):
    rows, width = own.shape
    tile = ROW_CHUNK
    block = pl.BlockSpec((tile, width), lambda i: (i, 0))
    fixed = lambda shape: pl.BlockSpec(shape, lambda i: (0, 0), pipeline_mode=pl.Buffered(1))
    operands = [core, own, other, base, grad, gain.reshape(1, -1)]
    specs = [SMEM_SPEC, block, block, block, block, fixed((1, width))]
    skip = 0
    if returned is not None:
        skip = (rows - returned[0].shape[0]) // tile
        operands += list(returned)
        specs += [pl.BlockSpec((tile, width // 2), lambda i: (jnp.maximum(i - skip, 0), 0))] * 2
    shapes, outs = [], []
    if weight is not None:
        operands.append(weight)
        specs.append(fixed(weight.shape))
    if emit_wide:
        shapes.append(jax.ShapeDtypeStruct((rows, width), F32))
        outs.append(block)
    shapes.append(jax.ShapeDtypeStruct((rows, width), BF))
    outs.append(block)
    if weight is not None:
        shapes.append(jax.ShapeDtypeStruct((rows, weight.shape[0]), BF))
        outs.append(pl.BlockSpec((tile, weight.shape[0]), lambda i: (i, 0)))
    shapes.append(jax.ShapeDtypeStruct((8, width), F32))
    outs.append(pl.BlockSpec((8, width), lambda i: (0, 0)))
    return pl.pallas_call(
        functools.partial(norm_back_body, (skip, returned is not None, weight is not None, emit_wide)),
        grid=(rows // tile,),
        out_shape=tuple(shapes),
        in_specs=specs,
        out_specs=tuple(outs),
        compiler_params=pltpu.CompilerParams(vmem_limit_bytes=18 * MIB),
        cost_estimate=pl.CostEstimate(flops=4 * rows * width * 512, bytes_accessed=16 * rows * width, transcendentals=0),
        name="norm_back",
    )(*operands)


def memory_project_body(memory, w_key, w_value, offset, padded, keys, values):
    rows = memory.shape[1]
    padded[rows // 16 * 16 :, :] = jnp.zeros((padded.shape[0] - rows // 16 * 16, padded.shape[1]), BF)
    padded[:rows, :] = memory[0]
    low = padded[...]
    keys[...] = nn(low, w_key[...]).astype(BF)
    values[...] = (nn(low, w_value[...]) + offset[...]).astype(BF)


def memory_project(memory, padded, w_key, w_value, offset):
    images, rows, width = memory.shape
    half = w_key.shape[1]
    fixed = lambda shape: pl.BlockSpec(shape, lambda i: (0, 0), pipeline_mode=pl.Buffered(1))
    return pl.pallas_call(
        memory_project_body,
        grid=(images,),
        out_shape=(
            jax.ShapeDtypeStruct((images * padded, width), BF),
            jax.ShapeDtypeStruct((images * padded, half), BF),
            jax.ShapeDtypeStruct((images * padded, half), BF),
        ),
        in_specs=[pl.BlockSpec((1, rows, width), lambda i: (i, 0, 0)), fixed(w_key.shape), fixed(w_value.shape), fixed((1, half))],
        out_specs=(
            pl.BlockSpec((padded, width), lambda i: (i, 0)),
            pl.BlockSpec((padded, half), lambda i: (i, 0)),
            pl.BlockSpec((padded, half), lambda i: (i, 0)),
        ),
        compiler_params=pltpu.CompilerParams(vmem_limit_bytes=14 * MIB),
        cost_estimate=pl.CostEstimate(flops=4 * images * padded * width * half, bytes_accessed=6 * images * padded * width, transcendentals=0),
        name="memory_project",
    )(memory, w_key, w_value, offset.reshape(1, -1))


def back_sum_body(factors, *refs):
    count = len(factors)
    total = None
    for at, factor in enumerate(factors):
        product = nt(refs[at][...], refs[count + at][...])
        if factor != 1.0:
            product = product * factor
        total = product if total is None else total + product
    refs[2 * count][...] = total.astype(BF)


def back_sum(grads, weights, factors, tile):
    rows, inner = grads[0].shape
    width = weights[0].shape[0]
    return pl.pallas_call(
        functools.partial(back_sum_body, factors),
        grid=(rows // tile,),
        out_shape=jax.ShapeDtypeStruct((rows, width), BF),
        in_specs=[pl.BlockSpec((tile, inner), lambda i: (i, 0))] * len(grads)
        + [pl.BlockSpec(weight.shape, lambda i: (0, 0), pipeline_mode=pl.Buffered(1)) for weight in weights],
        out_specs=pl.BlockSpec((tile, width), lambda i: (i, 0)),
        compiler_params=pltpu.CompilerParams(vmem_limit_bytes=10 * MIB),
        cost_estimate=pl.CostEstimate(flops=4 * rows * inner * width * len(grads), bytes_accessed=4 * rows * inner * len(grads), transcendentals=0),
        name="back_sum",
    )(*grads, *weights)


def bit_orders(count, turns):
    bits = list(range(count.bit_length() - 1))
    return tuple(tuple(bits[turn:turns] + bits[:turn] + bits[turns:]) for turn in range(turns))


def place_code(position, order):
    code = 0
    for rank, bit in enumerate(order):
        if position >> (len(order) - 1 - rank) & 1:
            code |= 1 << bit
    return code


def weight_grads_body(count, sides, left_count, right_count, me, *refs):
    lefts, rights = refs[:left_count], refs[left_count : left_count + right_count]
    outs = refs[left_count + right_count : left_count + right_count + 2 * len(sides)]
    turned = refs[left_count + right_count + 2 * len(sides) : -1]
    natural = refs[-1]
    width = lefts[0].shape[1]
    columns = rights[0].shape[1]
    piece = width // count
    for left, target in zip(lefts, turned):
        for r in range(width // ROW_CHUNK):
            part = slice(r * ROW_CHUNK, (r + 1) * ROW_CHUNK)
            target[part, :] = left[:, part].T
    number = 0
    for side, (order, products) in enumerate(sides):
        keep, send = outs[2 * side], outs[2 * side + 1]
        for at, (terms, factor) in enumerate(products):
            store = natural.at[number % 2]
            number += 1
            for r in range(width // ROW_CHUNK):
                part = slice(r * ROW_CHUNK, (r + 1) * ROW_CHUNK)
                total = None
                for left, right in terms:
                    product = nn(turned[left][part, :], rights[right][...])
                    total = product if total is None else total + product
                store[part, :] = (total * factor if factor != 1.0 else total).astype(BF)
            place = slice(at * columns, (at + 1) * columns)
            for position in range(count):
                source = pl.multiple_of((me[0] ^ place_code(position, order)) * piece, piece)
                target = keep if position < count // 2 else send
                row = position % (count // 2) * piece
                target[row : row + piece, place] = store[pl.ds(source, piece), :]


def weight_grads(count, me, lefts, rights, sides):
    width = lefts[0].shape[1]
    columns = rights[0].shape[1]
    shapes = []
    flops = 0
    for _, products in sides:
        shapes += [jax.ShapeDtypeStruct((width // 2, columns * len(products)), BF)] * 2
        flops += sum(2 * width * columns * lefts[left].shape[0] for terms, _ in products for left, _ in terms)
    return pl.pallas_call(
        functools.partial(weight_grads_body, count, sides, len(lefts), len(rights)),
        out_shape=tuple(shapes),
        in_specs=[SMEM_SPEC] + [VMEM_SPEC] * (len(lefts) + len(rights)),
        out_specs=(VMEM_SPEC,) * len(shapes),
        scratch_shapes=[pltpu.VMEM((width, left.shape[0]), BF) for left in lefts] + [pltpu.VMEM((2, width, columns), BF)],
        compiler_params=pltpu.CompilerParams(vmem_limit_bytes=24 * MIB),
        cost_estimate=pl.CostEstimate(flops=2 * flops, bytes_accessed=16 * width * width, transcendentals=0),
        name="weight_grads",
    )(me, *lefts, *rights)


def fold_body(joined, sides, *refs):
    ins, outs = refs[: 2 * sides], refs[2 * sides :]
    at = 0
    for side in range(sides):
        keep, got = ins[2 * side], ins[2 * side + 1]
        rows, columns = keep.shape
        total = keep[...].astype(F32) + got[...].astype(F32)
        if len(outs) == 1:
            outs[0][...] = total
            continue
        out_keep, out_send = (outs[0], outs[1]) if joined else (outs[2 * side], outs[2 * side + 1])
        out_keep[:, at : at + columns] = total[: rows // 2].astype(BF)
        out_send[:, at : at + columns] = total[rows // 2 :].astype(BF)
        at += columns if joined else 0


def fold(parts, joined, last):
    sides = len(parts) // 2
    rows = parts[0].shape[0]
    widths = [part.shape[1] for part in parts[::2]]
    columns = sum(widths)
    if last:
        shapes = (jax.ShapeDtypeStruct((rows, columns), F32),)
    elif joined:
        shapes = (jax.ShapeDtypeStruct((rows // 2, columns), BF),) * 2
    else:
        shapes = tuple(jax.ShapeDtypeStruct((rows // 2, wide), BF) for wide in widths for _ in range(2))
    return pl.pallas_call(
        functools.partial(fold_body, joined, sides),
        out_shape=shapes,
        in_specs=[VMEM_SPEC] * len(parts),
        out_specs=(VMEM_SPEC,) * len(shapes),
        cost_estimate=pl.CostEstimate(flops=rows * columns, bytes_accessed=6 * rows * columns, transcendentals=0),
        compiler_params=pltpu.CompilerParams(vmem_limit_bytes=11 * MIB),
        name="fold",
    )(*parts)


def tied(values, *tokens):
    return lax.optimization_barrier(tuple(values) + tokens)[: len(values)]


def exchanged(value, bit, count):
    return lax.ppermute(value, "dp", [(i, i ^ (1 << bit)) for i in range(count)])


class CubeSum:
    def __init__(self, count, orders):
        self.count, self.level = count, 0
        self.orders = orders
        self.held, self.parts = (), []

    def add(self, parts):
        first = len(self.held) // 2
        self.held += tuple(parts)
        for side in range(len(parts) // 2):
            bit = self.orders[first + side][self.level]
            self.parts += [parts[2 * side], exchanged(parts[2 * side + 1], bit, self.count)]

    def advance(self, *tokens):
        levels = len(self.orders[0])
        last = self.level == levels - 1
        parts = tied(self.parts, *tokens) if tokens else self.parts
        result = fold(tuple(parts), self.level + 1 == len(self.orders), last)
        self.level += 1
        if last:
            return result[0]
        self.held, self.parts = (), []
        self.add(result)
        return None

    def finish(self):
        while True:
            result = self.advance()
            if result is not None:
                return result


def memory_total_body(where, own, other, mine, theirs, target):
    image = pl.program_id(0)
    rows = target.shape[1]
    half = mine.shape[1]
    last = jnp.where(image == where[0], 1.0, 0.0)
    first_core = where[1] == 0
    target_rows = slice(0, rows)
    for side in range(2):
        columns = slice(side * half, (side + 1) * half)
        extra = jnp.where(first_core if side == 0 else jnp.logical_not(first_core), mine[...].astype(F32), theirs[...].astype(F32))
        total = own[:, columns].astype(F32) + other[:, columns].astype(F32) + last * extra
        target[0, target_rows, columns] = total[:rows].astype(BF)


def memory_total(rows, where, own, other, mine, theirs):
    padded = mine.shape[0]
    images, width = own.shape[0] // padded, own.shape[1]
    block = pl.BlockSpec((padded, width), lambda i: (i, 0))
    half = pl.BlockSpec(mine.shape, lambda i: (0, 0))
    return pl.pallas_call(
        memory_total_body,
        grid=(images,),
        out_shape=jax.ShapeDtypeStruct((images, rows, width), BF),
        in_specs=[SMEM_SPEC, block, block, half, half],
        out_specs=pl.BlockSpec((1, rows, width), lambda i: (i, 0, 0)),
        compiler_params=pltpu.CompilerParams(vmem_limit_bytes=12 * MIB),
        cost_estimate=pl.CostEstimate(flops=0, bytes_accessed=8 * images * padded * width, transcendentals=0),
        name="memory_total",
    )(where, own, other, mine, theirs)


def core_swap(value):
    return lax.ppermute(value, "tensor", [(0, 1), (1, 0)])


def core_half(value, core):
    half = value.shape[1] // 2
    return jnp.where(core == 0, value[:, :half], value[:, half:])


def other_half(value, core):
    half = value.shape[1] // 2
    return jnp.where(core == 0, value[:, half:], value[:, :half])


def rejoined(mine, theirs, core):
    return jnp.concatenate([jnp.where(core == 0, mine, theirs), jnp.where(core == 0, theirs, mine)], 1)


def fetched(value, core):
    mine = shifted(core_half(value, core), "dp", 1)
    return rejoined(mine, core_swap(mine), core)


def given_start(partial, core):
    low = partial.astype(BF)
    return core_half(low, core), core_swap(other_half(low, core))


def given_send(halves_in):
    mine, other = halves_in
    return shifted((mine.astype(F32) + other.astype(F32)).astype(BF), "dp", -1)


def two_level_scatter(stacked, count):
    inner = min(4, count)
    outer = count // inner
    near = [[o * inner + i for i in range(inner)] for o in range(outer)]
    far = [[o * inner + i for o in range(outer)] for i in range(inner)]
    first = lax.psum_scatter(stacked, "dp", scatter_dimension=0, axis_index_groups=near, tiled=True)

    def second(held):
        return lax.psum_scatter(held, "dp", scatter_dimension=0, axis_index_groups=far, tiled=True)

    return first, second


def per_device(
    tokens,
    page_ids,
    image_of_page,
    memory,
    ln0_gain,
    ln0_bias,
    w_self_query,
    b_self_query,
    w_self_key,
    w_self_value,
    b_self_value,
    w_self_out,
    b_self_out,
    ln1_gain,
    ln1_bias,
    w_query,
    b_query,
    w_key,
    w_value,
    b_value,
    w_out,
    b_out,
    ln2_gain,
    ln2_bias,
    w_up,
    b_up,
    w_down,
    b_down,
    cotangent,
):
    count = lax.axis_size("dp")
    me = lax.axis_index("dp")
    core = lax.axis_index("tensor")
    row_count, width = tokens.shape
    image_count, memory_rows = (memory.shape[0], memory.shape[1])
    scale = 1.0 / math.sqrt(HEAD_WIDTH)
    padded_rows = -(-memory_rows // 16) * 16
    first_page = me * image_count
    local_page = page_ids - first_page
    begins = [jnp.sum((local_page < page).astype(jnp.int32)) for page in range(image_count)]
    prior_begin = shifted(jnp.full((128,), begins[1], jnp.int32), "dp", 1)[0]
    slots = [jnp.int32(image_count)] + [image_of_page[page] - first_page for page in range(image_count)]
    meta = jnp.stack(begins + [prior_begin] + slots).astype(jnp.int32)
    last_image = image_of_page[image_count - 1] - first_page
    skipped = row_count // 4
    last_memory = lax.dynamic_index_in_dim(memory, last_image, 0, keepdims=False)
    last_memory = jnp.pad(last_memory, ((0, padded_rows - memory_rows), (0, 0)))
    tokens_mine = shifted(core_half(tokens[skipped:], core), "dp", 1)
    memory_mine_in = shifted(core_half(last_memory, core), "dp", 1)

    def project(rows, weight, bias=None):
        product = jnp.dot(rows, weight, preferred_element_type=F32)
        return (product if bias is None else product + bias).astype(BF)

    hidden_zero, self_queries, self_key_rows, self_values = norm_project(
        tokens,
        None,
        ln0_gain,
        ln0_bias,
        ((w_self_query, b_self_query, scale), (w_self_key, None, 1.0), (w_self_value, b_self_value, 1.0)),
        False,
        True,
    )
    flat_memory, keys_here, values_here = memory_project(memory, padded_rows, w_key, w_value, b_value)
    (tokens_mine,) = tied((tokens_mine,), self_queries, keys_here)
    prior_tokens = rejoined(tokens_mine, core_swap(tokens_mine), core)
    prior_hidden, prior_keys, prior_values = norm_project(
        prior_tokens,
        None,
        ln0_gain,
        ln0_bias,
        ((w_self_key, None, 1.0), (w_self_value, b_self_value, 1.0)),
        False,
        True,
    )
    memory_mine_in, prior_keys = tied((memory_mine_in, prior_keys))
    prior_memory = rejoined(memory_mine_in, core_swap(memory_mine_in), core)
    self_attended, self_logs = self_forward(
        meta, self_queries, prior_keys, self_key_rows, prior_values, self_values
    )
    self_part = project(self_attended, w_self_out)
    self_other = core_swap(self_part)
    prior_image_keys = project(prior_memory, w_key)
    prior_image_values = project(prior_memory, w_value, b_value)
    start, hidden_one, queries = norm_project(
        tokens, (self_part, self_other, b_self_out), ln1_gain, ln1_bias, ((w_query, b_query, scale),), True, True
    )
    attended, log_totals = cross_forward(
        memory_rows, meta, queries, prior_image_keys, keys_here, prior_image_values, values_here
    )
    cross_part = project(attended, w_out)
    cross_other = core_swap(cross_part)
    inner = min(4, count)
    tile = 512
    middle, down_part, grad_part, forward_grads, up_bias_grad = feed_forward(
        inner, count // inner, tile, start, cross_part, cross_other, b_out, ln2_gain, ln2_bias, cotangent, w_up, b_up, w_down
    )
    grad_other = core_swap(grad_part)
    forward_first, forward_second = two_level_scatter(forward_grads, count)
    down_other = core_swap(down_part)
    core_list = jnp.full((1,), core, jnp.int32)
    me_list = jnp.full((1,), me, jnp.int32)
    grad_middle, grad_branch, grad_attended, sums_two = norm_back(
        core_list, grad_part, grad_other, middle, cotangent, ln2_gain, None, w_out, True
    )
    (grad_attended,) = tied((grad_attended,), down_other)
    prior_image_key_grads, key_grads, prior_image_value_grads, value_grads, grad_queries = cross_back(
        memory_rows,
        meta,
        queries,
        grad_attended,
        attended,
        log_totals,
        prior_image_keys,
        keys_here,
        prior_image_values,
        values_here,
    )
    hidden_part = back_sum((grad_queries,), (w_query,), (scale,), 256)
    hidden_other = core_swap(hidden_part)
    (grad_queries,) = tied((grad_queries,), hidden_part)
    pair, thirds = bit_orders(count, 2), bit_orders(count, 3)
    cross_parts = weight_grads(
        count,
        me_list,
        (hidden_one, flat_memory, prior_memory),
        (grad_queries, key_grads, prior_image_key_grads, value_grads, prior_image_value_grads),
        ((pair[0], ((((0, 0),), scale), (((1, 1), (2, 2)), 1.0), (((1, 3), (2, 4)), 1.0))),),
    )
    cross_cube = CubeSum(count, pair)
    cross_cube.add(cross_parts)
    memory_start = given_start(
        back_sum((prior_image_key_grads, prior_image_value_grads), (w_key, w_value), (1.0, 1.0), padded_rows), core
    )
    memory_part = back_sum((key_grads, value_grads), (w_key, w_value), (1.0, 1.0), padded_rows)
    memory_other = core_swap(memory_part)
    value_bias_grad = jnp.sum(value_grads.astype(F32), axis=0) + jnp.sum(prior_image_value_grads.astype(F32), axis=0)
    query_bias_grad = jnp.sum(grad_queries.astype(F32), axis=0) * scale
    hidden_other, memory_mine = tied((hidden_other, memory_start[0]), memory_part, *cross_parts)
    memory_mine = given_send((memory_mine, memory_start[1]))
    grad_start, grad_start_low, grad_self_attended, sums_one = norm_back(
        core_list, hidden_part, hidden_other, start, grad_middle, ln1_gain, None, w_self_out, True
    )
    out_parts = weight_grads(
        count,
        me_list,
        (grad_branch, grad_start_low),
        (attended, self_attended),
        ((pair[1], ((((0, 0),), 1.0), (((1, 1),), 1.0))),),
    )
    cross_cube.add(out_parts)
    grad_self_attended, forward_first = tied((grad_self_attended, forward_first), memory_other, *out_parts)
    forward_sums = forward_second(forward_first)
    prior_key_grads, prior_value_grads, prior_query_grads = self_prior_back(
        meta, self_queries, grad_self_attended, self_attended, self_logs, prior_keys, prior_values
    )
    zero_start = given_start(
        back_sum((prior_key_grads, prior_value_grads), (w_self_key, w_self_value), (1.0, 1.0), 256), core
    )
    cross_cube.advance(prior_query_grads)
    prior_query_grads, memory_mine = tied((prior_query_grads, memory_mine), *cross_cube.held)
    zero_mine = given_send(zero_start)
    memory_theirs = core_swap(memory_mine)
    self_key_grads, self_value_grads, grad_self_queries = self_own_back(
        meta,
        self_queries,
        grad_self_attended,
        self_attended,
        self_logs,
        self_key_rows,
        self_values,
        prior_query_grads,
    )
    cross_cube.advance(grad_self_queries)
    grad_self_queries, zero_mine, forward_sums = tied((grad_self_queries, zero_mine, forward_sums), *cross_cube.held)
    zero_theirs = core_swap(zero_mine)
    self_parts = weight_grads(
        count,
        me_list,
        (hidden_zero, prior_hidden),
        (grad_self_queries, self_key_grads, prior_key_grads, self_value_grads, prior_value_grads),
        (
            (thirds[0], ((((0, 0),), scale),)),
            (thirds[1], ((((0, 1), (1, 2)), 1.0),)),
            (thirds[2], ((((0, 3), (1, 4)), 1.0),)),
        ),
    )
    self_cube = CubeSum(count, thirds)
    self_cube.add(self_parts)
    (grad_self_queries,) = tied((grad_self_queries,), memory_theirs, zero_theirs, *self_parts)
    zero_part = back_sum(
        (grad_self_queries, self_key_grads, self_value_grads),
        (w_self_query, w_self_key, w_self_value),
        (scale, 1.0, 1.0),
        256,
    )
    zero_other = core_swap(zero_part)
    cross_cube.advance(zero_part)
    self_cube.advance(*cross_cube.held)
    self_query_bias_grad = jnp.sum(grad_self_queries.astype(F32), axis=0) * scale
    self_value_bias_grad = jnp.sum(self_value_grads.astype(F32), axis=0) + jnp.sum(prior_value_grads.astype(F32), axis=0)
    zero_other, zero_theirs = tied((zero_other, zero_theirs), *self_cube.held)
    d_tokens, sums_zero = norm_back(
        core_list, zero_part, zero_other, tokens, grad_start, ln0_gain, (zero_mine, zero_theirs), None, False
    )
    self_cube.advance(sums_zero)
    (down_other,) = tied((down_other,), *self_cube.held)
    layer_out = (middle + (down_part.astype(F32) + down_other.astype(F32)) + b_down).astype(BF)
    self_cube.advance(layer_out)
    (memory_theirs,) = tied((memory_theirs,), *self_cube.held)
    d_memory = memory_total(
        memory_rows, jnp.stack([last_image, core]), memory_part, memory_other, memory_mine, memory_theirs
    )
    cross_sums = cross_cube.finish()
    self_sums = self_cube.finish()
    small_sums = butterfly_sum(
        (
            sums_zero[0],
            sums_zero[1],
            self_query_bias_grad,
            self_value_bias_grad,
            sums_one[2],
            sums_one[0],
            sums_one[1],
            query_bias_grad,
            value_bias_grad,
            sums_two[2],
            sums_two[0],
            sums_two[1],
            up_bias_grad[0],
            sums_two[3],
        )
    )
    local = w_query.shape[1]

    def cut(table, number):
        return table[:, number * local : (number + 1) * local]

    pieces = forward_sums.astype(F32).reshape(forward_sums.shape[0], -1, 2, tile)
    summed_up = pieces[:, :, 0].reshape(forward_sums.shape[0], -1)
    summed_down = pieces[:, :, 1].reshape(forward_sums.shape[0], -1).T
    return (
        layer_out,
        d_tokens,
        d_memory,
        small_sums[0],
        small_sums[1],
        cut(self_sums, 0),
        small_sums[2],
        cut(self_sums, 1),
        cut(self_sums, 2),
        small_sums[3],
        cut(cross_sums, 4).T,
        small_sums[4],
        small_sums[5],
        small_sums[6],
        cut(cross_sums, 0),
        small_sums[7],
        cut(cross_sums, 1),
        cut(cross_sums, 2),
        small_sums[8],
        cut(cross_sums, 3).T,
        small_sums[9],
        small_sums[10],
        small_sums[11],
        summed_up,
        small_sums[12],
        summed_down,
        small_sums[13],
    )


def solution(mesh):
    in_specs = (
        P("dp", None),
        P("dp"),
        P("dp"),
        P("dp", None, None),
        P(),
        P(),
        P(None, "tensor"),
        P("tensor"),
        P(None, "tensor"),
        P(None, "tensor"),
        P("tensor"),
        P("tensor", None),
        P(),
        P(),
        P(),
        P(None, "tensor"),
        P("tensor"),
        P(None, "tensor"),
        P(None, "tensor"),
        P("tensor"),
        P("tensor", None),
        P(),
        P(),
        P(),
        P(None, "tensor"),
        P("tensor"),
        P("tensor", None),
        P(),
        P("dp", None),
    )
    out_specs = (
        P("dp", None),
        P("dp", None),
        P("dp", None, None),
        P(),
        P(),
        P("dp", "tensor"),
        P("tensor"),
        P("dp", "tensor"),
        P("dp", "tensor"),
        P("tensor"),
        P("tensor", "dp"),
        P(),
        P(),
        P(),
        P("dp", "tensor"),
        P("tensor"),
        P("dp", "tensor"),
        P("dp", "tensor"),
        P("tensor"),
        P("tensor", "dp"),
        P(),
        P(),
        P(),
        P("dp", "tensor"),
        P("tensor"),
        P("tensor", "dp"),
        P(),
    )
    return jax.shard_map(
        per_device, mesh=mesh, in_specs=in_specs, out_specs=out_specs, check_vma=False
    )
```

```python
import functools
import math

import jax
import jax.numpy as jnp
from jax import lax
from jax.experimental import pallas as pl
from jax.experimental.pallas import tpu as pltpu
from jax.sharding import PartitionSpec as P

HEAD_WIDTH = 64


EPSILON = 1e-05


def shifted(value, axis, steps):
    count = lax.axis_size(axis)
    initial, last = (max(0, -steps), min(count, count - steps))
    return lax.ppermute(value, axis, [(source, source + steps) for source in range(initial, last)])


class ButterflySum:
    def __init__(self, vectors):
        self.sizes = [vector.shape[0] for vector in vectors]
        self.total = jnp.concatenate(vectors).reshape(-1, 128)
        self.count = lax.axis_size("dp")
        self.bit = 1

    def step(self):
        pairs = [(i, i ^ self.bit) for i in range(self.count)]
        self.total = self.total + lax.ppermute(self.total, "dp", pairs)
        self.bit *= 2

    def finish(self):
        while self.bit < self.count:
            self.step()
        flat = self.total.reshape(-1)
        pieces, at = [], 0
        for size in self.sizes:
            pieces.append(flat[at : at + size])
            at += size
        return pieces


BF = jnp.bfloat16
F32 = jnp.float32
NEG = -1e30
TILE = 256
HEAD_WIDTH = 64
PAIR = 2 * HEAD_WIDTH
MIB = 1024 * 1024


def nt(left, right):
    return lax.dot_general(left, right, (((1,), (1,)), ((), ())), preferred_element_type=F32)


def nn(left, right):
    return lax.dot_general(left, right, (((1,), (0,)), ((), ())), preferred_element_type=F32)


def head_half(pair, half):
    lane = lax.broadcasted_iota(jnp.int32, pair.shape, 1)
    keep = lane < HEAD_WIDTH if half == 0 else lane >= HEAD_WIDTH
    return jnp.where(keep, pair, jnp.zeros_like(pair))


def span(index, size=TILE):
    return pl.ds(pl.multiple_of(index * size, size), size)


HEAD_ROWS = 80


def column_max(values):
    rows = values.shape[0]
    groups = max(1, rows // 64)
    step = -(-(rows // groups) // 8) * 8
    parts = []
    at = 0
    while at < rows:
        end = min(rows, at + step)
        parts.append(jnp.max(values[at:end], axis=0, keepdims=True))
        at = end
    while len(parts) > 1:
        parts = [jnp.maximum(*parts[i : i + 2]) if i + 1 < len(parts) else parts[i] for i in range(0, len(parts), 2)]
    return parts[0]


def extended(values, target, columns):
    turned = values.T
    extra = jnp.where(lax.broadcasted_iota(jnp.int32, (HEAD_ROWS - HEAD_WIDTH, turned.shape[1]), 0) == 0, 1.0, 0.0).astype(BF)
    for h in range(turned.shape[0] // HEAD_WIDTH):
        base = h * HEAD_ROWS
        target[base : base + HEAD_WIDTH, columns] = turned[h * HEAD_WIDTH : (h + 1) * HEAD_WIDTH, :]
        target[base + HEAD_WIDTH : base + HEAD_ROWS, columns] = extra


def lane_rows(i):
    return i * TILE + lax.broadcasted_iota(jnp.int32, (1, TILE), 1)


def self_forward_body(meta, q_ref, kp_ref, k_ref, vp_ref, v_ref, o_ref, log_ref,
                      vpt, vt, qm, bias, m_s, acc, done, scores):
    rows = q_ref.shape[0]
    pairs = q_ref.shape[1] // PAIR
    b1, b2, p0 = meta[0], meta[1], meta[2]
    tiles = rows // TILE
    offset = rows - kp_ref.shape[0]
    prior_tiles = kp_ref.shape[0] // TILE
    first_prior = (p0 - offset) // TILE
    prior_rows = (b1 + TILE - 1) // TILE

    def turn_own(j, c):
        extended(v_ref[span(j), :], vt, span(j))
        return c

    lax.fori_loop(0, tiles, turn_own, 0)

    def turn_prior(j, c):
        extended(vp_ref[span(j), :], vpt, span(j))
        return c

    lax.fori_loop(jnp.where(b1 > 0, first_prior, prior_tiles), prior_tiles, turn_prior, 0)

    def key_step(keys, values_t, j):
        for pair in range(pairs):
            key_pair = keys[span(j), pair * PAIR : pair * PAIR + PAIR]
            for half in range(2):
                scores[2 * pair + half] = nt(key_pair, qm[2 * pair + half])
        for pair in range(pairs):
            for half in range(2):
                h = 2 * pair + half
                heads = slice(h * HEAD_ROWS, (h + 1) * HEAD_ROWS)
                s = scores[h] + bias[...]
                m_old = m_s[h : h + 1, :]
                m_new = jnp.maximum(m_old, column_max(s))
                alpha = jnp.exp(m_old - m_new)
                e = jnp.exp(s - m_new)
                m_s[h : h + 1, :] = m_new
                acc[heads, :] = acc[heads, :] * alpha + nn(values_t[heads, span(j)], e.astype(BF))

    def row_tile(i, c):
        t = lane_rows(i)
        start = jnp.where(t < b1, 0, jnp.where(t < b2, b1, b2))
        for pair in range(pairs):
            q_pair = q_ref[span(i), pair * PAIR : pair * PAIR + PAIR]
            for half in range(2):
                qm[2 * pair + half] = head_half(q_pair, half)
        m_s[...] = jnp.full_like(m_s, NEG)
        acc[...] = jnp.zeros_like(acc)

        def prior(j, c2):
            r = offset + j * TILE + lax.broadcasted_iota(jnp.int32, (TILE, TILE), 0)
            bias[...] = jnp.where((r >= p0) & (t < b1), 0.0, NEG)
            key_step(kp_ref, vpt, j)
            return c2

        lax.fori_loop(jnp.where(i < prior_rows, first_prior, prior_tiles), prior_tiles, prior, 0)
        t_first = i * TILE
        lowest = jnp.where(t_first < b1, 0, jnp.where(t_first < b2, b1, b2))

        def own(j, c2):
            r = j * TILE + lax.broadcasted_iota(jnp.int32, (TILE, TILE), 0)
            bias[...] = jnp.where((r <= t) & (r >= start), 0.0, NEG)
            key_step(k_ref, vt, j)
            return c2

        lax.fori_loop(lowest // TILE, i + 1, own, 0)
        for h in range(2 * pairs):
            base = h * HEAD_ROWS
            total = acc[base + HEAD_WIDTH : base + HEAD_WIDTH + 1, :]
            log_ref[h : h + 1, span(i)] = m_s[h : h + 1, :] + jnp.log(total)
            done[h * HEAD_WIDTH : (h + 1) * HEAD_WIDTH, :] = acc[base : base + HEAD_WIDTH, :] * (1.0 / total)
        o_ref[span(i), :] = done[...].T.astype(BF)
        return c

    lax.fori_loop(0, tiles, row_tile, 0)


SMEM_SPEC = pl.BlockSpec(memory_space=pltpu.SMEM)
VMEM_SPEC = pl.BlockSpec(memory_space=pltpu.VMEM)


def self_forward(meta, q, k_prior, k, v_prior, v):
    rows, width = q.shape
    heads = width // HEAD_WIDTH
    return pl.pallas_call(
        self_forward_body,
        out_shape=(jax.ShapeDtypeStruct((rows, width), BF), jax.ShapeDtypeStruct((heads, rows), F32)),
        in_specs=[SMEM_SPEC] + [VMEM_SPEC] * 5,
        out_specs=(VMEM_SPEC, VMEM_SPEC),
        scratch_shapes=[
            pltpu.VMEM((heads * HEAD_ROWS, k_prior.shape[0]), BF),
            pltpu.VMEM((heads * HEAD_ROWS, rows), BF),
            pltpu.VMEM((heads, TILE, PAIR), BF),
            pltpu.VMEM((TILE, TILE), F32),
            pltpu.VMEM((heads, TILE), F32),
            pltpu.VMEM((heads * HEAD_ROWS, TILE), F32),
            pltpu.VMEM((width, TILE), F32),
            pltpu.VMEM((heads, TILE, TILE), F32),
        ],
        compiler_params=pltpu.CompilerParams(vmem_limit_bytes=16 * MIB),
        cost_estimate=pl.CostEstimate(flops=2 * 2 * rows * rows * width, bytes_accessed=8 * rows * width * 2, transcendentals=rows * rows * heads),
        name="self_forward",
    )(meta, q, k_prior, k, v_prior, v)


def grad_rows(do_ref, o_ref, i, width):
    heads = width // HEAD_WIDTH
    product = do_ref[span(i), :].astype(F32) * o_ref[span(i), :].astype(F32)
    high = product.astype(BF)
    low = (product - high.astype(F32)).astype(BF)
    head = lax.broadcasted_iota(jnp.int32, (heads, width), 0)
    column = lax.broadcasted_iota(jnp.int32, (heads, width), 1) // HEAD_WIDTH
    pick = jnp.where(head == column, 1.0, 0.0).astype(BF)
    return nt(pick, high) + nt(pick, low)


def halves(source, i, target, pairs):
    for pair in range(pairs):
        value = source[span(i), pair * PAIR : pair * PAIR + PAIR]
        for half in range(2):
            target[2 * pair + half] = head_half(value, half)


def grad_step(pairs, keys, values, keys_t, key_slice, key_lanes, qm, dom, shift, delta, bias, dk, dv, dqt, scores, grads):
    for pair in range(pairs):
        cols = slice(pair * PAIR, pair * PAIR + PAIR)
        key_pair = keys[key_slice, cols]
        value_pair = values[key_slice, cols]
        for half in range(2):
            h = 2 * pair + half
            scores[h] = nt(key_pair, qm[h])
            grads[h] = nt(value_pair, dom[h])
    for pair in range(pairs):
        cols = slice(pair * PAIR, pair * PAIR + PAIR)
        dv_pair = dv[key_slice, cols]
        dk_pair = dk[key_slice, cols]
        for half in range(2):
            h = 2 * pair + half
            heads = slice(h * HEAD_WIDTH, (h + 1) * HEAD_WIDTH)
            s = scores[h]
            if bias is not None:
                s = s + bias[...]
            p = jnp.exp(s - shift[h : h + 1, :])
            dp = grads[h]
            ds = (p * (dp - delta[h : h + 1, :])).astype(BF)
            dv_pair = dv_pair + nn(p.astype(BF), dom[h])
            dk_pair = dk_pair + nn(ds, qm[h])
            dqt[heads, :] = dqt[heads, :] + nn(keys_t[heads, key_lanes], ds)
        dv[key_slice, cols] = dv_pair
        dk[key_slice, cols] = dk_pair


def self_prior_back_body(meta, q_ref, do_ref, o_ref, log_ref, k_ref, v_ref, dk_ref, dv_ref, dq_ref,
                         kt, qm, dom, bias, delta, shift, dqt, dk, dv, scores, grads):
    rows, width = q_ref.shape
    pairs = width // PAIR
    b1, p0 = meta[0], meta[2]
    tiles = rows // TILE
    offset = rows - k_ref.shape[0]
    prior_tiles = k_ref.shape[0] // TILE
    first_prior = (p0 - offset) // TILE
    prior_rows = (b1 + TILE - 1) // TILE
    dk[...] = jnp.zeros_like(dk)
    dv[...] = jnp.zeros_like(dv)

    def turn(j, c):
        kt[:, span(j)] = k_ref[span(j), :].T
        return c

    lax.fori_loop(jnp.where(b1 > 0, first_prior, prior_tiles), prior_tiles, turn, 0)

    def row_tile(i, c):
        dqt[...] = jnp.zeros_like(dqt)
        t = lane_rows(i)

        @pl.when(i < prior_rows)
        def _():
            halves(q_ref, i, qm, pairs)
            halves(do_ref, i, dom, pairs)
            delta[...] = grad_rows(do_ref, o_ref, i, width)
            shift[...] = log_ref[:, span(i)]

        def prior(j, c2):
            r = offset + j * TILE + lax.broadcasted_iota(jnp.int32, (TILE, TILE), 0)
            bias[...] = jnp.where((r >= p0) & (t < b1), 0.0, NEG)
            grad_step(pairs, k_ref, v_ref, kt, span(j), span(j), qm, dom, shift, delta, bias, dk, dv, dqt, scores, grads)
            return c2

        lax.fori_loop(jnp.where(i < prior_rows, first_prior, prior_tiles), prior_tiles, prior, 0)
        dq_ref[span(i), :] = dqt[...].T
        return c

    lax.fori_loop(0, tiles, row_tile, 0)
    dk_ref[...] = dk[...].astype(BF)
    dv_ref[...] = dv[...].astype(BF)


def self_own_back_body(meta, q_ref, do_ref, o_ref, log_ref, k_ref, v_ref, dqp_ref, dk_ref, dv_ref, dq_ref,
                       kt, qm, dom, bias, delta, shift, dqt, dk, dv, scores, grads):
    rows, width = q_ref.shape
    pairs = width // PAIR
    b1, b2 = meta[0], meta[1]
    tiles = rows // TILE
    dk[...] = jnp.zeros_like(dk)
    dv[...] = jnp.zeros_like(dv)

    def turn(j, c):
        kt[:, span(j)] = k_ref[span(j), :].T
        return c

    lax.fori_loop(0, tiles, turn, 0)

    def row_tile(i, c):
        dqt[...] = jnp.zeros_like(dqt)
        t = lane_rows(i)
        start = jnp.where(t < b1, 0, jnp.where(t < b2, b1, b2))
        halves(q_ref, i, qm, pairs)
        halves(do_ref, i, dom, pairs)
        delta[...] = grad_rows(do_ref, o_ref, i, width)
        shift[...] = log_ref[:, span(i)]
        t_first = i * TILE
        lowest = jnp.where(t_first < b1, 0, jnp.where(t_first < b2, b1, b2))

        def own(j, c2):
            r = j * TILE + lax.broadcasted_iota(jnp.int32, (TILE, TILE), 0)
            bias[...] = jnp.where((r <= t) & (r >= start), 0.0, NEG)
            grad_step(pairs, k_ref, v_ref, kt, span(j), span(j), qm, dom, shift, delta, bias, dk, dv, dqt, scores, grads)
            return c2

        lax.fori_loop(lowest // TILE, i + 1, own, 0)
        dq_ref[span(i), :] = (dqp_ref[span(i), :] + dqt[...].T).astype(BF)
        return c

    lax.fori_loop(0, tiles, row_tile, 0)
    dk_ref[...] = dk[...].astype(BF)
    dv_ref[...] = dv[...].astype(BF)


def self_back_scratch(keys, width):
    heads = width // HEAD_WIDTH
    return [
        pltpu.VMEM((width, keys), BF),
        pltpu.VMEM((heads, TILE, PAIR), BF),
        pltpu.VMEM((heads, TILE, PAIR), BF),
        pltpu.VMEM((TILE, TILE), F32),
        pltpu.VMEM((heads, TILE), F32),
        pltpu.VMEM((heads, TILE), F32),
        pltpu.VMEM((width, TILE), F32),
        pltpu.VMEM((keys, width), F32),
        pltpu.VMEM((keys, width), F32),
        pltpu.VMEM((heads, TILE, TILE), F32),
        pltpu.VMEM((heads, TILE, TILE), F32),
    ]


def self_prior_back(meta, q, do, o, logs, k_prior, v_prior):
    rows, width = q.shape
    return pl.pallas_call(
        self_prior_back_body,
        out_shape=(jax.ShapeDtypeStruct(k_prior.shape, BF), jax.ShapeDtypeStruct(k_prior.shape, BF),
                   jax.ShapeDtypeStruct((rows, width), F32)),
        in_specs=[SMEM_SPEC] + [VMEM_SPEC] * 6,
        out_specs=(VMEM_SPEC,) * 3,
        scratch_shapes=self_back_scratch(k_prior.shape[0], width),
        compiler_params=pltpu.CompilerParams(vmem_limit_bytes=22 * MIB),
        cost_estimate=pl.CostEstimate(flops=3 * rows * rows * width, bytes_accessed=8 * rows * width * 2, transcendentals=rows * rows * 4),
        name="self_prior_back",
    )(meta, q, do, o, logs, k_prior, v_prior)


def self_own_back(meta, q, do, o, logs, k, v, dq_prior):
    rows, width = q.shape
    return pl.pallas_call(
        self_own_back_body,
        out_shape=(jax.ShapeDtypeStruct((rows, width), BF),) * 3,
        in_specs=[SMEM_SPEC] + [VMEM_SPEC] * 7,
        out_specs=(VMEM_SPEC,) * 3,
        scratch_shapes=self_back_scratch(rows, width),
        compiler_params=pltpu.CompilerParams(vmem_limit_bytes=26 * MIB),
        cost_estimate=pl.CostEstimate(flops=5 * rows * rows * width, bytes_accessed=8 * rows * width * 2, transcendentals=rows * rows * 4),
        name="self_own_back",
    )(meta, q, do, o, logs, k, v, dq_prior)


def segment(meta, index, rows):
    first = jnp.where(index == 0, 0, jnp.where(index == 1, meta[0], meta[1]))
    last = jnp.where(index == 0, meta[0], jnp.where(index == 1, meta[1], rows))
    return first, last, meta[3 + index]


def gather_tables(kp_ref, k_ref, vp_ref, v_ref, k_all, v_all, sems):
    own = k_ref.shape[0]
    copies = [
        pltpu.make_async_copy(k_ref, k_all.at[:own, :], sems.at[0]),
        pltpu.make_async_copy(v_ref, v_all.at[:own, :], sems.at[1]),
        pltpu.make_async_copy(kp_ref, k_all.at[own:, :], sems.at[2]),
        pltpu.make_async_copy(vp_ref, v_all.at[own:, :], sems.at[3]),
    ]
    for copy in copies:
        copy.start()
    for copy in copies:
        copy.wait()


def cross_forward_body(used, meta, q_ref, kp_ref, k_ref, vp_ref, v_ref, o_ref, log_ref, k_all, v_all, vt, qm, acc, scores, sems):
    rows, width = q_ref.shape
    pairs = width // PAIR
    padded = kp_ref.shape[0]
    images = k_all.shape[0] // padded
    gather_tables(kp_ref, k_ref, vp_ref, v_ref, k_all, v_all, sems)

    def turn(slot, c):
        extended(v_all[pl.ds(pl.multiple_of(slot * padded, 16), padded), :], vt.at[slot], slice(None))
        return c

    lax.fori_loop(0, images, turn, 0)

    def one(index, c0):
        first, last, slot = segment(meta, index, rows)
        keys = pl.ds(pl.multiple_of(slot * padded, 16), padded)

        def tile(i, c):
            halves(q_ref, i, qm, pairs)
            t = lane_rows(i)
            inside = (t >= first) & (t < last)
            for pair in range(pairs):
                key_pair = k_all[keys, pair * PAIR : pair * PAIR + PAIR]
                for half in range(2):
                    scores[2 * pair + half] = nt(key_pair, qm[2 * pair + half])
            for h in range(2 * pairs):
                heads = slice(h * HEAD_WIDTH, (h + 1) * HEAD_WIDTH)
                s = scores[h]
                if used < padded:
                    row = lax.broadcasted_iota(jnp.int32, s.shape, 0)
                    s = jnp.where(row < used, s, NEG)
                m = column_max(s)
                e = jnp.exp(s - m)
                mixed = nn(vt[slot, h * HEAD_ROWS : (h + 1) * HEAD_ROWS, :], e.astype(BF))
                total = mixed[HEAD_WIDTH : HEAD_WIDTH + 1, :]
                acc[heads, :] = mixed[:HEAD_WIDTH, :] * (1.0 / total)
                log_ref[h : h + 1, span(i)] = jnp.where(
                    inside, m + jnp.log(total), log_ref[h : h + 1, span(i)]
                )
            column = i * TILE + lax.broadcasted_iota(jnp.int32, (TILE, width), 0)
            keep = (column >= first) & (column < last)
            o_ref[span(i), :] = jnp.where(keep, acc[...].T, o_ref[span(i), :].astype(F32)).astype(BF)
            return c

        lax.fori_loop(first // TILE, jnp.where(last > first, (last + TILE - 1) // TILE, 0), tile, 0)
        return c0

    lax.fori_loop(0, 3, one, 0)


ANY_SPEC = pl.BlockSpec(memory_space=pl.ANY)


def cross_forward(used, meta, q, k_prior, k, v_prior, v):
    rows, width = q.shape
    heads = width // HEAD_WIDTH
    padded = k_prior.shape[0]
    every = padded + k.shape[0]
    return pl.pallas_call(
        functools.partial(cross_forward_body, used),
        out_shape=(jax.ShapeDtypeStruct((rows, width), BF), jax.ShapeDtypeStruct((heads, rows), F32)),
        in_specs=[SMEM_SPEC, VMEM_SPEC] + [ANY_SPEC] * 4,
        out_specs=(VMEM_SPEC, VMEM_SPEC),
        scratch_shapes=[
            pltpu.VMEM((every, width), BF),
            pltpu.VMEM((every, width), BF),
            pltpu.VMEM((every // padded, heads * HEAD_ROWS, padded), BF),
            pltpu.VMEM((heads, TILE, PAIR), BF),
            pltpu.VMEM((width, TILE), F32),
            pltpu.VMEM((heads, padded, TILE), F32),
            pltpu.SemaphoreType.DMA((4,)),
        ],
        compiler_params=pltpu.CompilerParams(vmem_limit_bytes=22 * MIB),
        cost_estimate=pl.CostEstimate(flops=16 * rows * padded * width, bytes_accessed=8 * rows * width * 2, transcendentals=rows * padded * heads),
        name="cross_forward",
    )(meta, q, k_prior, k, v_prior, v)


def cross_back_body(used, meta, q_ref, do_ref, o_ref, log_ref, kp_ref, k_ref, vp_ref, v_ref, dkp_ref, dk_ref, dvp_ref, dv_ref,
                    dq_ref, k_all, v_all, kt, qm, dom, delta, shift, dqt, dk, dv, scores, grads, sems):
    rows, width = q_ref.shape
    pairs = width // PAIR
    padded = kp_ref.shape[0]
    images = k_all.shape[0] // padded
    gather_tables(kp_ref, k_ref, vp_ref, v_ref, k_all, v_all, sems)
    for item in (dk, dv):
        item[...] = jnp.zeros_like(item)

    def turn(slot, c):
        kt[slot] = k_all[pl.ds(pl.multiple_of(slot * padded, 16), padded), :].T
        return c

    lax.fori_loop(0, images, turn, 0)

    def one(index, c0):
        first, last, slot = segment(meta, index, rows)
        keys = pl.ds(pl.multiple_of(slot * padded, 16), padded)

        def tile(i, c):
            halves(q_ref, i, qm, pairs)
            halves(do_ref, i, dom, pairs)
            t = lane_rows(i)
            inside = (t >= first) & (t < last)
            delta[...] = grad_rows(do_ref, o_ref, i, width)
            shift[...] = jnp.where(inside, log_ref[:, span(i)], -NEG)
            dqt[...] = jnp.zeros_like(dqt)
            grad_step(pairs, k_all, v_all, kt.at[slot], keys, slice(None), qm, dom, shift, delta, None, dk, dv, dqt, scores, grads)
            column = i * TILE + lax.broadcasted_iota(jnp.int32, (TILE, width), 0)
            keep = (column >= first) & (column < last)
            dq_ref[span(i), :] = jnp.where(keep, dqt[...].T, dq_ref[span(i), :].astype(F32)).astype(BF)
            return c

        lax.fori_loop(first // TILE, jnp.where(last > first, (last + TILE - 1) // TILE, 0), tile, 0)
        return c0

    lax.fori_loop(0, 3, one, 0)
    inner = lax.broadcasted_iota(jnp.int32, (padded, width), 0) < used
    for source, own_target, prior_target in ((dk, dk_ref, dkp_ref), (dv, dv_ref, dvp_ref)):
        for slot in range(images):
            part = slice(slot * padded, (slot + 1) * padded)
            value = jnp.where(inner, source[part, :], 0.0).astype(BF)
            if slot < images - 1:
                own_target[part, :] = value
            else:
                prior_target[...] = value


def cross_back(used, meta, q, do, o, logs, k_prior, k, v_prior, v):
    rows, width = q.shape
    heads = width // HEAD_WIDTH
    padded = k_prior.shape[0]
    every = padded + k.shape[0]
    tables = (k_prior, k, v_prior, v)
    return pl.pallas_call(
        functools.partial(cross_back_body, used),
        out_shape=tuple(jax.ShapeDtypeStruct(table.shape, BF) for table in tables) + (jax.ShapeDtypeStruct((rows, width), BF),),
        in_specs=[SMEM_SPEC] + [VMEM_SPEC] * 4 + [ANY_SPEC] * 4,
        out_specs=(VMEM_SPEC,) * 5,
        scratch_shapes=[
            pltpu.VMEM((every, width), BF),
            pltpu.VMEM((every, width), BF),
            pltpu.VMEM((every // padded, width, padded), BF),
            pltpu.VMEM((heads, TILE, PAIR), BF),
            pltpu.VMEM((heads, TILE, PAIR), BF),
            pltpu.VMEM((heads, TILE), F32),
            pltpu.VMEM((heads, TILE), F32),
            pltpu.VMEM((width, TILE), F32),
            pltpu.VMEM((every, width), F32),
            pltpu.VMEM((every, width), F32),
            pltpu.VMEM((heads, padded, TILE), F32),
            pltpu.VMEM((heads, padded, TILE), F32),
            pltpu.SemaphoreType.DMA((4,)),
        ],
        compiler_params=pltpu.CompilerParams(vmem_limit_bytes=44 * MIB),
        cost_estimate=pl.CostEstimate(flops=40 * rows * padded * width, bytes_accessed=12 * rows * width * 2, transcendentals=rows * padded * heads),
        name="cross_back",
    )(meta, q, do, o, logs, *tables)


SQRT_HALF = 0.7071067811865476
GAUSS = 0.3989422804014327
ROW_CHUNK = 256


def error_function(x):
    x = jnp.clip(x, -4.0, 4.0)
    z = x * x
    top = -2.72614225801306e-10
    for term in (2.77068142495902e-08, -2.10102402082508e-06, -5.69250639462346e-05,
                 -7.34990630326855e-04, -2.95459980854025e-03, -1.60960333262415e-02):
        top = top * z + term
    low = -1.45660718464996e-05
    for term in (-2.13374055278905e-04, -1.68282697438203e-03, -7.37332916720468e-03, -1.42647390514189e-02):
        low = low * z + term
    return x * top / low


def row_norm(values):
    mean = jnp.mean(values, axis=-1, keepdims=True)
    centered = values - mean
    inverse = lax.rsqrt(jnp.mean(centered * centered, axis=-1, keepdims=True) + EPSILON)
    return centered * inverse, inverse


def chunk_place(index, inner, outer):
    return (index % inner) * outer + index // inner


def feed_forward_body(inner, outer, start_ref, own_ref, other_ref, b_out, gain, shift_in, dy_ref, w_up, b_up, w_down,
                      y1_ref, down_ref, dh_ref, grads_ref, db_ref,
                      h2, h2t, dyt, acc_down, acc_dh, u_s, da_s, g_s, du_s):
    step = pl.program_id(0)
    rows, width = dy_ref.shape
    tile = w_up.shape[1]
    chunks = rows // ROW_CHUNK

    @pl.when(step == 0)
    def _():
        for r in range(chunks):
            part = slice(r * ROW_CHUNK, (r + 1) * ROW_CHUNK)
            y1 = start_ref[part, :].astype(F32) + (own_ref[part, :].astype(F32) + other_ref[part, :].astype(F32)) + b_out[...]
            y1_ref[part, :] = y1.astype(BF)
            normed, _ = row_norm(y1)
            low = (normed * gain[...] + shift_in[...]).astype(BF)
            h2[part, :] = low
            h2t[:, part] = low.T
            dyt[:, part] = dy_ref[part, :].T
        acc_down[...] = jnp.zeros_like(acc_down)
        acc_dh[...] = jnp.zeros_like(acc_dh)

    for r in range(chunks):
        part = slice(r * ROW_CHUNK, (r + 1) * ROW_CHUNK)
        u_s[part, :] = nn(h2[part, :], w_up[...]) + b_up[...]
        da_s[part, :] = nt(dy_ref[part, :], w_down[...])
    total = jnp.zeros((1, tile), F32)
    for r in range(chunks):
        part = slice(r * ROW_CHUNK, (r + 1) * ROW_CHUNK)
        u = u_s[part, :]
        half = 0.5 + 0.5 * error_function(u * SQRT_HALF)
        g = (u * half).astype(BF)
        slope = half + u * (GAUSS * jnp.exp(-0.5 * u * u))
        du = (da_s[part, :] * slope).astype(BF)
        g_s[part, :] = g
        du_s[part, :] = du
        total = total + jnp.sum(du.astype(F32), axis=0, keepdims=True)
        down = nn(g, w_down[...])
        dh = nt(du, w_up[...])
        acc_down[part, :] += down
        acc_dh[part, :] += dh

    db_ref[...] = total
    piece = width // (inner * outer)
    for source, turned, at in ((du_s, h2t, 0), (g_s, dyt, tile)):
        for r in range(width // ROW_CHUNK):
            part = slice(r * ROW_CHUNK, (r + 1) * ROW_CHUNK)
            product = nn(turned[part, :], source[...]).astype(BF)
            for c in range(ROW_CHUNK // piece):
                place = chunk_place(r * (ROW_CHUNK // piece) + c, inner, outer) * piece
                grads_ref[place : place + piece, at : at + tile] = product[c * piece : (c + 1) * piece, :]

    @pl.when(step == pl.num_programs(0) - 1)
    def _():
        down_ref[...] = acc_down[...].astype(BF)
        dh_ref[...] = acc_dh[...].astype(BF)


def feed_forward(inner, outer, tile, start, own, other, b_out, gain, shift_in, dy, w_up, b_up, w_down):
    rows, width = dy.shape
    hidden = w_up.shape[1]
    whole = lambda shape: pl.BlockSpec(shape, lambda k: (0, 0), pipeline_mode=pl.Buffered(1))
    row = whole((1, width))
    full = whole((rows, width))
    return pl.pallas_call(
        functools.partial(feed_forward_body, inner, outer),
        grid=(hidden // tile,),
        out_shape=(
            jax.ShapeDtypeStruct((rows, width), BF),
            jax.ShapeDtypeStruct((rows, width), BF),
            jax.ShapeDtypeStruct((rows, width), BF),
            jax.ShapeDtypeStruct((width, 2 * hidden), BF),
            jax.ShapeDtypeStruct((1, hidden), F32),
        ),
        in_specs=[full, full, full, row, row, row, full,
                  pl.BlockSpec((width, tile), lambda k: (0, k)),
                  pl.BlockSpec((1, tile), lambda k: (0, k)),
                  pl.BlockSpec((tile, width), lambda k: (k, 0))],
        out_specs=(full, full, full, pl.BlockSpec((width, 2 * tile), lambda k: (0, k)), pl.BlockSpec((1, tile), lambda k: (0, k))),
        scratch_shapes=[
            pltpu.VMEM((rows, width), BF),
            pltpu.VMEM((width, rows), BF),
            pltpu.VMEM((width, rows), BF),
            pltpu.VMEM((rows, width), F32),
            pltpu.VMEM((rows, width), F32),
            pltpu.VMEM((rows, tile), F32),
            pltpu.VMEM((rows, tile), F32),
            pltpu.VMEM((rows, tile), BF),
            pltpu.VMEM((rows, tile), BF),
        ],
        compiler_params=pltpu.CompilerParams(vmem_limit_bytes=54 * MIB),
        cost_estimate=pl.CostEstimate(flops=12 * rows * width * hidden, bytes_accessed=30 * rows * width, transcendentals=rows * hidden * 2),
        name="feed_forward",
    )(start, own, other, b_out.reshape(1, -1), gain.reshape(1, -1), shift_in.reshape(1, -1), dy, w_up, b_up.reshape(1, -1), w_down)

def norm_project_body(flags, weight_flags, *refs):
    has_extra, emit_base, emit_hidden = flags
    refs = list(refs)
    values = refs.pop(0)[...].astype(F32)
    if has_extra:
        own, other, offset = refs.pop(0), refs.pop(0), refs.pop(0)
        values = values + (own[...].astype(F32) + other[...].astype(F32)) + offset[...]
    gain, shift_in = refs.pop(0), refs.pop(0)
    weights = []
    for has_bias, factor in weight_flags:
        weight = refs.pop(0)
        weights.append((weight, refs.pop(0) if has_bias else None, factor))
    if emit_base:
        refs.pop(0)[...] = values.astype(BF)
    normed, _ = row_norm(values)
    hidden = (normed * gain[...] + shift_in[...]).astype(BF)
    if emit_hidden:
        refs.pop(0)[...] = hidden
    for weight, offset, factor in weights:
        product = nn(hidden, weight[...])
        if offset is not None:
            product = product + offset[...]
        if factor != 1.0:
            product = product * factor
        refs.pop(0)[...] = product.astype(BF)


def norm_project(base, extra, gain, shift_in, weights, emit_base, emit_hidden):
    rows, width = base.shape
    tile = ROW_CHUNK
    block = pl.BlockSpec((tile, width), lambda i: (i, 0))
    fixed = lambda shape: pl.BlockSpec(shape, lambda i: (0, 0), pipeline_mode=pl.Buffered(1))
    operands, specs = [base], [block]
    if extra is not None:
        own, other, offset = extra
        operands += [own, other, offset.reshape(1, -1)]
        specs += [block, block, fixed((1, width))]
    operands += [gain.reshape(1, -1), shift_in.reshape(1, -1)]
    specs += [fixed((1, width))] * 2
    shapes, outs = [], []
    if emit_base:
        shapes.append(jax.ShapeDtypeStruct((rows, width), BF))
        outs.append(block)
    if emit_hidden:
        shapes.append(jax.ShapeDtypeStruct((rows, width), BF))
        outs.append(block)
    for weight, offset, _ in weights:
        operands.append(weight)
        specs.append(fixed(weight.shape))
        if offset is not None:
            operands.append(offset.reshape(1, -1))
            specs.append(fixed((1, weight.shape[1])))
        shapes.append(jax.ShapeDtypeStruct((rows, weight.shape[1]), BF))
        outs.append(pl.BlockSpec((tile, weight.shape[1]), lambda i: (i, 0)))
    flops = sum(2 * rows * width * weight.shape[1] for weight, _, _ in weights)
    return pl.pallas_call(
        functools.partial(norm_project_body, (extra is not None, emit_base, emit_hidden),
                          tuple((offset is not None, factor) for _, offset, factor in weights)),
        grid=(rows // tile,),
        out_shape=tuple(shapes),
        in_specs=specs,
        out_specs=tuple(outs),
        compiler_params=pltpu.CompilerParams(vmem_limit_bytes=12 * MIB),
        cost_estimate=pl.CostEstimate(flops=2 * flops, bytes_accessed=10 * rows * width, transcendentals=0),
        name="norm_project",
    )(*operands)


def norm_back_body(flags, *refs):
    skip, has_back, has_weight, grad_sum = flags
    refs = list(refs)
    core = refs.pop(0)
    own, other, base, grad, gain = (refs.pop(0) for _ in range(5))
    step = pl.program_id(0)
    total = own[...].astype(F32) + other[...].astype(F32)
    if has_back:
        mine, theirs = refs.pop(0)[...].astype(F32), refs.pop(0)[...].astype(F32)
        first = core[0] == 0
        back = jnp.concatenate([jnp.where(first, mine, theirs), jnp.where(first, theirs, mine)], 1)
        total = total + jnp.where(step >= skip, back, 0.0)
    if has_weight:
        weight = refs.pop(0)
    normed, inverse = row_norm(base[...].astype(F32))
    scaled = total * gain[...]
    inner = (
        scaled
        - jnp.mean(scaled, axis=-1, keepdims=True)
        - normed * jnp.mean(scaled * normed, axis=-1, keepdims=True)
    )
    result = grad[...].astype(F32) + inner * inverse
    low = result.astype(BF)
    refs.pop(0)[...] = low
    if has_weight:
        refs.pop(0)[...] = nt(low, weight[...]).astype(BF)
    sums = refs.pop(0)

    @pl.when(step == 0)
    def _():
        sums[...] = jnp.zeros_like(sums)

    sums[0:1, :] += jnp.sum(total * normed, axis=0, keepdims=True)
    sums[1:2, :] += jnp.sum(total, axis=0, keepdims=True)
    if has_weight:
        sums[2:3, :] += jnp.sum(low.astype(F32), axis=0, keepdims=True)
        if grad_sum:
            sums[3:4, :] += jnp.sum(grad[...].astype(F32), axis=0, keepdims=True)


def norm_back(core, own, other, base, grad, gain, returned, weight, grad_sum):
    rows, width = own.shape
    tile = ROW_CHUNK
    block = pl.BlockSpec((tile, width), lambda i: (i, 0))
    fixed = lambda shape: pl.BlockSpec(shape, lambda i: (0, 0), pipeline_mode=pl.Buffered(1))
    operands = [core, own, other, base, grad, gain.reshape(1, -1)]
    specs = [SMEM_SPEC, block, block, block, block, fixed((1, width))]
    skip = 0
    if returned is not None:
        skip = (rows - returned[2]) // tile
        operands += list(returned[:2])
        specs += [pl.BlockSpec((tile, width // 2), lambda i: (jnp.maximum(i - skip, 0), 0))] * 2
    shapes, outs = [], []
    if weight is not None:
        operands.append(weight)
        specs.append(fixed(weight.shape))
    shapes.append(jax.ShapeDtypeStruct((rows, width), BF))
    outs.append(block)
    if weight is not None:
        shapes.append(jax.ShapeDtypeStruct((rows, weight.shape[0]), BF))
        outs.append(pl.BlockSpec((tile, weight.shape[0]), lambda i: (i, 0)))
    shapes.append(jax.ShapeDtypeStruct((8, width), F32))
    outs.append(pl.BlockSpec((8, width), lambda i: (0, 0)))
    return pl.pallas_call(
        functools.partial(norm_back_body, (skip, returned is not None, weight is not None, grad_sum)),
        grid=(rows // tile,),
        out_shape=tuple(shapes),
        in_specs=specs,
        out_specs=tuple(outs),
        compiler_params=pltpu.CompilerParams(vmem_limit_bytes=18 * MIB),
        cost_estimate=pl.CostEstimate(flops=4 * rows * width * 512, bytes_accessed=16 * rows * width, transcendentals=0),
        name="norm_back",
    )(*operands)


def memory_project_body(memory, w_key, w_value, offset, padded, keys, values):
    rows = memory.shape[1]
    padded[rows // 16 * 16 :, :] = jnp.zeros((padded.shape[0] - rows // 16 * 16, padded.shape[1]), BF)
    padded[:rows, :] = memory[0]
    low = padded[...]
    keys[...] = nn(low, w_key[...]).astype(BF)
    values[...] = (nn(low, w_value[...]) + offset[...]).astype(BF)


def memory_project(memory, padded, w_key, w_value, offset):
    images, rows, width = memory.shape
    half = w_key.shape[1]
    fixed = lambda shape: pl.BlockSpec(shape, lambda i: (0, 0), pipeline_mode=pl.Buffered(1))
    return pl.pallas_call(
        memory_project_body,
        grid=(images,),
        out_shape=(
            jax.ShapeDtypeStruct((images * padded, width), BF),
            jax.ShapeDtypeStruct((images * padded, half), BF),
            jax.ShapeDtypeStruct((images * padded, half), BF),
        ),
        in_specs=[pl.BlockSpec((1, rows, width), lambda i: (i, 0, 0)), fixed(w_key.shape), fixed(w_value.shape), fixed((1, half))],
        out_specs=(
            pl.BlockSpec((padded, width), lambda i: (i, 0)),
            pl.BlockSpec((padded, half), lambda i: (i, 0)),
            pl.BlockSpec((padded, half), lambda i: (i, 0)),
        ),
        compiler_params=pltpu.CompilerParams(vmem_limit_bytes=14 * MIB),
        cost_estimate=pl.CostEstimate(flops=4 * images * padded * width * half, bytes_accessed=6 * images * padded * width, transcendentals=0),
        name="memory_project",
    )(memory, w_key, w_value, offset.reshape(1, -1))


def back_sum_body(factors, *refs):
    count = len(factors)
    total = None
    for at, factor in enumerate(factors):
        product = nt(refs[at][...], refs[count + at][...])
        if factor != 1.0:
            product = product * factor
        total = product if total is None else total + product
    refs[2 * count][...] = total.astype(BF)


def back_sum(grads, weights, factors, tile):
    rows, inner = grads[0].shape
    width = weights[0].shape[0]
    return pl.pallas_call(
        functools.partial(back_sum_body, factors),
        grid=(rows // tile,),
        out_shape=jax.ShapeDtypeStruct((rows, width), BF),
        in_specs=[pl.BlockSpec((tile, inner), lambda i: (i, 0))] * len(grads)
        + [pl.BlockSpec(weight.shape, lambda i: (0, 0), pipeline_mode=pl.Buffered(1)) for weight in weights],
        out_specs=pl.BlockSpec((tile, width), lambda i: (i, 0)),
        compiler_params=pltpu.CompilerParams(vmem_limit_bytes=10 * MIB),
        cost_estimate=pl.CostEstimate(flops=4 * rows * inner * width * len(grads), bytes_accessed=4 * rows * inner * len(grads), transcendentals=0),
        name="back_sum",
    )(*grads, *weights)


def bit_orders(count, turns):
    bits = list(range(count.bit_length() - 1))
    return tuple(tuple(bits[turn:turns] + bits[:turn] + bits[turns:]) for turn in range(turns))


def place_code(position, order):
    code = 0
    for rank, bit in enumerate(order):
        if position >> (len(order) - 1 - rank) & 1:
            code |= 1 << bit
    return code


def weight_grads_body(count, sides, left_count, right_count, me, *refs):
    lefts, rights = refs[:left_count], refs[left_count : left_count + right_count]
    outs = refs[left_count + right_count : left_count + right_count + 2 * len(sides)]
    turned = refs[left_count + right_count + 2 * len(sides) : -1]
    natural = refs[-1]
    width = lefts[0].shape[1]
    columns = rights[0].shape[1]
    piece = width // count
    for left, target in zip(lefts, turned):
        for r in range(width // ROW_CHUNK):
            part = slice(r * ROW_CHUNK, (r + 1) * ROW_CHUNK)
            target[part, :] = left[:, part].T
    number = 0
    for side, (order, products) in enumerate(sides):
        keep, send = outs[2 * side], outs[2 * side + 1]
        for at, (terms, factor) in enumerate(products):
            store = natural.at[number % 2]
            number += 1
            for r in range(width // ROW_CHUNK):
                part = slice(r * ROW_CHUNK, (r + 1) * ROW_CHUNK)
                total = None
                for left, right in terms:
                    product = nn(turned[left][part, :], rights[right][...])
                    total = product if total is None else total + product
                store[part, :] = (total * factor if factor != 1.0 else total).astype(BF)
            place = slice(at * columns, (at + 1) * columns)
            for position in range(count):
                source = pl.multiple_of((me[0] ^ place_code(position, order)) * piece, piece)
                target = keep if position < count // 2 else send
                row = position % (count // 2) * piece
                target[row : row + piece, place] = store[pl.ds(source, piece), :]


def placed_grads_body(inner, outer, products, left_count, right_count, *refs):
    lefts, rights = refs[:left_count], refs[left_count : left_count + right_count]
    target = refs[left_count + right_count]
    turned = refs[left_count + right_count + 1 :]
    width = lefts[0].shape[1]
    columns = rights[0].shape[1]
    piece = width // (inner * outer)
    for left, store in zip(lefts, turned):
        for r in range(width // ROW_CHUNK):
            part = slice(r * ROW_CHUNK, (r + 1) * ROW_CHUNK)
            store[part, :] = left[:, part].T
    for at, (terms, factor) in enumerate(products):
        for r in range(width // ROW_CHUNK):
            part = slice(r * ROW_CHUNK, (r + 1) * ROW_CHUNK)
            total = None
            for left, right in terms:
                product = nn(turned[left][part, :], rights[right][...])
                total = product if total is None else total + product
            low = (total * factor if factor != 1.0 else total).astype(BF)
            for c in range(ROW_CHUNK // piece):
                place = chunk_place(r * (ROW_CHUNK // piece) + c, inner, outer) * piece
                target[place : place + piece, at * columns : (at + 1) * columns] = low[c * piece : (c + 1) * piece, :]


def placed_grads(inner, outer, lefts, rights, products):
    width = lefts[0].shape[1]
    columns = rights[0].shape[1]
    flops = sum(2 * width * columns * lefts[left].shape[0] for terms, _ in products for left, _ in terms)
    return pl.pallas_call(
        functools.partial(placed_grads_body, inner, outer, products, len(lefts), len(rights)),
        out_shape=jax.ShapeDtypeStruct((width, columns * len(products)), BF),
        in_specs=[VMEM_SPEC] * (len(lefts) + len(rights)),
        out_specs=VMEM_SPEC,
        scratch_shapes=[pltpu.VMEM((width, left.shape[0]), BF) for left in lefts],
        compiler_params=pltpu.CompilerParams(vmem_limit_bytes=34 * MIB),
        cost_estimate=pl.CostEstimate(flops=flops, bytes_accessed=16 * width * width, transcendentals=0),
        name="placed_grads",
    )(*lefts, *rights)


def weight_grads(count, me, lefts, rights, sides, limit):
    width = lefts[0].shape[1]
    columns = rights[0].shape[1]
    shapes = []
    flops = 0
    for _, products in sides:
        shapes += [jax.ShapeDtypeStruct((width // 2, columns * len(products)), BF)] * 2
        flops += sum(2 * width * columns * lefts[left].shape[0] for terms, _ in products for left, _ in terms)
    return pl.pallas_call(
        functools.partial(weight_grads_body, count, sides, len(lefts), len(rights)),
        out_shape=tuple(shapes),
        in_specs=[SMEM_SPEC] + [VMEM_SPEC] * (len(lefts) + len(rights)),
        out_specs=(VMEM_SPEC,) * len(shapes),
        scratch_shapes=[pltpu.VMEM((width, left.shape[0]), BF) for left in lefts] + [pltpu.VMEM((2, width, columns), BF)],
        compiler_params=pltpu.CompilerParams(vmem_limit_bytes=limit * MIB),
        cost_estimate=pl.CostEstimate(flops=2 * flops, bytes_accessed=16 * width * width, transcendentals=0),
        name="weight_grads",
    )(me, *lefts, *rights)


def fold_body(joined, sides, *refs):
    ins, outs = refs[: 2 * sides], refs[2 * sides :]
    at = 0
    for side in range(sides):
        keep, got = ins[2 * side], ins[2 * side + 1]
        rows, columns = keep.shape
        total = keep[...].astype(F32) + got[...].astype(F32)
        if len(outs) == 1:
            outs[0][...] = total
            continue
        out_keep, out_send = (outs[0], outs[1]) if joined else (outs[2 * side], outs[2 * side + 1])
        out_keep[:, at : at + columns] = total[: rows // 2].astype(BF)
        out_send[:, at : at + columns] = total[rows // 2 :].astype(BF)
        at += columns if joined else 0


def fold(parts, joined, last):
    sides = len(parts) // 2
    rows = parts[0].shape[0]
    widths = [part.shape[1] for part in parts[::2]]
    columns = sum(widths)
    if last:
        shapes = (jax.ShapeDtypeStruct((rows, columns), F32),)
    elif joined:
        shapes = (jax.ShapeDtypeStruct((rows // 2, columns), BF),) * 2
    else:
        shapes = tuple(jax.ShapeDtypeStruct((rows // 2, wide), BF) for wide in widths for _ in range(2))
    return pl.pallas_call(
        functools.partial(fold_body, joined, sides),
        out_shape=shapes,
        in_specs=[VMEM_SPEC] * len(parts),
        out_specs=(VMEM_SPEC,) * len(shapes),
        cost_estimate=pl.CostEstimate(flops=rows * columns, bytes_accessed=6 * rows * columns, transcendentals=0),
        compiler_params=pltpu.CompilerParams(vmem_limit_bytes=11 * MIB),
        name="fold",
    )(*parts)


def tied(values, *tokens):
    return lax.optimization_barrier(tuple(values) + tokens)[: len(values)]


def exchanged(value, bit, count):
    return lax.ppermute(value, "dp", [(i, i ^ (1 << bit)) for i in range(count)])


class CubeSum:
    def __init__(self, count, orders):
        self.count, self.level = count, 0
        self.orders = orders
        self.held, self.parts = (), []

    def add(self, parts):
        first = len(self.held) // 2
        self.held += tuple(parts)
        for side in range(len(parts) // 2):
            bit = self.orders[first + side][self.level]
            self.parts += [parts[2 * side], exchanged(parts[2 * side + 1], bit, self.count)]

    def advance(self, *tokens):
        levels = len(self.orders[0])
        last = self.level == levels - 1
        parts = tied(self.parts, *tokens) if tokens else self.parts
        result = fold(tuple(parts), self.level + 1 == len(self.orders), last)
        self.level += 1
        if last:
            return result[0]
        self.held, self.parts = (), []
        self.add(result)
        return None

    def finish(self):
        while True:
            result = self.advance()
            if result is not None:
                return result


def memory_total_body(where, own, other, mine, theirs, target):
    image = pl.program_id(0)
    rows = target.shape[1]
    half = mine.shape[1]
    last = jnp.where(image == where[0], 1.0, 0.0)
    first_core = where[1] == 0
    target_rows = slice(0, rows)
    for side in range(2):
        columns = slice(side * half, (side + 1) * half)
        extra = jnp.where(first_core if side == 0 else jnp.logical_not(first_core), mine[...].astype(F32), theirs[...].astype(F32))
        total = own[:, columns].astype(F32) + other[:, columns].astype(F32) + last * extra
        target[0, target_rows, columns] = total[:rows].astype(BF)


def memory_total(rows, where, own, other, mine, theirs):
    padded = mine.shape[0]
    images, width = own.shape[0] // padded, own.shape[1]
    block = pl.BlockSpec((padded, width), lambda i: (i, 0))
    half = pl.BlockSpec(mine.shape, lambda i: (0, 0))
    return pl.pallas_call(
        memory_total_body,
        grid=(images,),
        out_shape=jax.ShapeDtypeStruct((images, rows, width), BF),
        in_specs=[SMEM_SPEC, block, block, half, half],
        out_specs=pl.BlockSpec((1, rows, width), lambda i: (i, 0, 0)),
        compiler_params=pltpu.CompilerParams(vmem_limit_bytes=12 * MIB),
        cost_estimate=pl.CostEstimate(flops=0, bytes_accessed=8 * images * padded * width, transcendentals=0),
        name="memory_total",
    )(where, own, other, mine, theirs)


def core_swap(value):
    return lax.ppermute(value, "tensor", [(0, 1), (1, 0)])


def core_half(value, core):
    half = value.shape[1] // 2
    return jnp.where(core == 0, value[:, :half], value[:, half:])


def other_half(value, core):
    half = value.shape[1] // 2
    return jnp.where(core == 0, value[:, half:], value[:, :half])


def rejoined(mine, theirs, core):
    return jnp.concatenate([jnp.where(core == 0, mine, theirs), jnp.where(core == 0, theirs, mine)], 1)


def fetched(value, core):
    mine = shifted(core_half(value, core), "dp", 1)
    return rejoined(mine, core_swap(mine), core)


def given_start(partial, core):
    low = partial.astype(BF)
    return core_half(low, core), core_swap(other_half(low, core))


def given_total(halves_in):
    mine, other = halves_in
    return (mine.astype(F32) + other.astype(F32)).astype(BF)


def outer_split(inner, outer, me, source):
    rows, columns = source.shape
    piece = rows // outer
    order = tuple(range(outer.bit_length() - 1))

    def body(me_ref, source_ref, keep, send):
        mine = me_ref[0] // inner
        for position in range(outer):
            at = pl.multiple_of((mine ^ place_code(position, order)) * piece, piece)
            target = keep if position < outer // 2 else send
            row = position % (outer // 2) * piece
            target[row : row + piece, :] = source_ref[pl.ds(at, piece), :]

    half = jax.ShapeDtypeStruct((rows // 2, columns), source.dtype)
    return pl.pallas_call(
        body,
        out_shape=(half, half),
        in_specs=[SMEM_SPEC, VMEM_SPEC],
        out_specs=(VMEM_SPEC, VMEM_SPEC),
        compiler_params=pltpu.CompilerParams(vmem_limit_bytes=14 * MIB),
        cost_estimate=pl.CostEstimate(flops=0, bytes_accessed=4 * rows * columns, transcendentals=0),
        name="outer_split",
    )(me, source)


def two_level_scatter(stacked, count):
    inner = min(4, count)
    outer = count // inner
    near = [[o * inner + i for i in range(inner)] for o in range(outer)]
    far = [[o * inner + i for o in range(outer)] for i in range(inner)]
    first = lax.psum_scatter(stacked, "dp", scatter_dimension=0, axis_index_groups=near, tiled=True)

    def second(held):
        return lax.psum_scatter(held, "dp", scatter_dimension=0, axis_index_groups=far, tiled=True)

    return first, second


def per_device(
    tokens,
    page_ids,
    image_of_page,
    memory,
    ln0_gain,
    ln0_bias,
    w_self_query,
    b_self_query,
    w_self_key,
    w_self_value,
    b_self_value,
    w_self_out,
    b_self_out,
    ln1_gain,
    ln1_bias,
    w_query,
    b_query,
    w_key,
    w_value,
    b_value,
    w_out,
    b_out,
    ln2_gain,
    ln2_bias,
    w_up,
    b_up,
    w_down,
    b_down,
    cotangent,
):
    count = lax.axis_size("dp")
    me = lax.axis_index("dp")
    core = lax.axis_index("tensor")
    row_count, width = tokens.shape
    image_count, memory_rows = (memory.shape[0], memory.shape[1])
    scale = 1.0 / math.sqrt(HEAD_WIDTH)
    padded_rows = -(-memory_rows // 16) * 16
    first_page = me * image_count
    local_page = page_ids - first_page
    begins = [jnp.sum((local_page < page).astype(jnp.int32)) for page in range(image_count)]
    prior_begin = shifted(jnp.full((128,), begins[1], jnp.int32), "dp", 1)[0]
    slots = [jnp.int32(image_count)] + [image_of_page[page] - first_page for page in range(image_count)]
    meta = jnp.stack(begins + [prior_begin] + slots).astype(jnp.int32)
    last_image = image_of_page[image_count - 1] - first_page
    skipped = row_count // 4
    last_memory = lax.dynamic_index_in_dim(memory, last_image, 0, keepdims=False)
    last_memory = jnp.pad(last_memory, ((0, padded_rows - memory_rows), (0, 0)))
    tokens_mine = shifted(core_half(tokens[skipped:], core), "dp", 1)
    memory_mine_in = shifted(core_half(last_memory, core), "dp", 1)

    def project(rows, weight, bias=None):
        product = jnp.dot(rows, weight, preferred_element_type=F32)
        return (product if bias is None else product + bias).astype(BF)

    hidden_zero, self_queries, self_key_rows, self_values = norm_project(
        tokens,
        None,
        ln0_gain,
        ln0_bias,
        ((w_self_query, b_self_query, scale), (w_self_key, None, 1.0), (w_self_value, b_self_value, 1.0)),
        False,
        True,
    )
    flat_memory, keys_here, values_here = memory_project(memory, padded_rows, w_key, w_value, b_value)
    (tokens_mine,) = tied((tokens_mine,), self_queries, keys_here)
    prior_tokens = rejoined(tokens_mine, core_swap(tokens_mine), core)
    prior_hidden, prior_keys, prior_values = norm_project(
        prior_tokens,
        None,
        ln0_gain,
        ln0_bias,
        ((w_self_key, None, 1.0), (w_self_value, b_self_value, 1.0)),
        False,
        True,
    )
    self_attended, self_logs = self_forward(
        meta, self_queries, prior_keys, self_key_rows, prior_values, self_values
    )
    self_attended, memory_mine_in = tied((self_attended, memory_mine_in))
    prior_memory = rejoined(memory_mine_in, core_swap(memory_mine_in), core)
    self_part = project(self_attended, w_self_out)
    self_other = core_swap(self_part)
    prior_image_keys = project(prior_memory, w_key)
    prior_image_values = project(prior_memory, w_value, b_value)
    start, hidden_one, queries = norm_project(
        tokens, (self_part, self_other, b_self_out), ln1_gain, ln1_bias, ((w_query, b_query, scale),), True, True
    )
    attended, log_totals = cross_forward(
        memory_rows, meta, queries, prior_image_keys, keys_here, prior_image_values, values_here
    )
    cross_part = project(attended, w_out)
    cross_other = core_swap(cross_part)
    inner = min(4, count)
    tile = 512
    middle, down_part, grad_part, forward_grads, up_bias_grad = feed_forward(
        inner, count // inner, tile, start, cross_part, cross_other, b_out, ln2_gain, ln2_bias, cotangent, w_up, b_up, w_down
    )
    grad_other = core_swap(grad_part)
    forward_first, _ = two_level_scatter(forward_grads, count)
    down_other = core_swap(down_part)
    core_list = jnp.full((1,), core, jnp.int32)
    me_list = jnp.full((1,), me, jnp.int32)
    grad_branch, grad_attended, sums_two = norm_back(
        core_list, grad_part, grad_other, middle, cotangent, ln2_gain, None, w_out, True
    )
    (grad_attended,) = tied((grad_attended,), down_other)
    prior_image_key_grads, key_grads, prior_image_value_grads, value_grads, grad_queries = cross_back(
        memory_rows,
        meta,
        queries,
        grad_attended,
        attended,
        log_totals,
        prior_image_keys,
        keys_here,
        prior_image_values,
        values_here,
    )
    hidden_part = back_sum((grad_queries,), (w_query,), (scale,), 256)
    hidden_other = core_swap(hidden_part)
    (grad_queries,) = tied((grad_queries,), hidden_part)
    pair, thirds = bit_orders(count, 2), bit_orders(count, 3)
    thirds = bit_orders(count, 3)
    memory_start = given_start(
        back_sum((prior_image_key_grads, prior_image_value_grads), (w_key, w_value), (1.0, 1.0), padded_rows), core
    )
    memory_part = back_sum((key_grads, value_grads), (w_key, w_value), (1.0, 1.0), padded_rows)
    memory_other = core_swap(memory_part)
    value_bias_grad = jnp.sum(value_grads.astype(F32), axis=0) + jnp.sum(prior_image_value_grads.astype(F32), axis=0)
    query_bias_grad = jnp.sum(grad_queries.astype(F32), axis=0) * scale
    (hidden_other,) = tied((hidden_other,), memory_part)
    memory_half = given_total(memory_start)
    grad_start_low, grad_self_attended, sums_one = norm_back(
        core_list, hidden_part, hidden_other, start, grad_branch, ln1_gain, None, w_self_out, False
    )
    cross_grads = placed_grads(
        inner,
        count // inner,
        (hidden_one, flat_memory, prior_memory, grad_branch, grad_start_low),
        (grad_queries, key_grads, prior_image_key_grads, value_grads, prior_image_value_grads, attended, self_attended),
        (
            (((0, 0),), scale),
            (((1, 1), (2, 2)), 1.0),
            (((1, 3), (2, 4)), 1.0),
            (((3, 5),), 1.0),
            (((4, 6),), 1.0),
        ),
    )
    cross_first, both_second = two_level_scatter(cross_grads, count)
    (grad_self_attended,) = tied((grad_self_attended,), memory_other, cross_grads)
    prior_key_grads, prior_value_grads, prior_query_grads = self_prior_back(
        meta, self_queries, grad_self_attended, self_attended, self_logs, prior_keys, prior_values
    )
    zero_start = given_start(
        back_sum((prior_key_grads, prior_value_grads), (w_self_key, w_self_value), (1.0, 1.0), 256), core
    )
    (forward_first,) = tied((forward_first,), zero_start[0])
    outer_bits = tuple(range(inner.bit_length() - 1, count.bit_length() - 1))
    forward_cube = CubeSum(count, (outer_bits,))
    forward_cube.add(outer_split(inner, count // inner, me_list, forward_first))
    returned_sent = jnp.concatenate([given_total(zero_start), memory_half], 0)
    prior_query_grads, returned_sent = tied((prior_query_grads, returned_sent), *forward_cube.held)
    returned_mine = shifted(returned_sent, "dp", -1)
    self_key_grads, self_value_grads, grad_self_queries = self_own_back(
        meta,
        self_queries,
        grad_self_attended,
        self_attended,
        self_logs,
        self_key_rows,
        self_values,
        prior_query_grads,
    )
    forward_parts = tied(forward_cube.parts, grad_self_queries)
    forward_parts = fold(tuple(forward_parts), True, False)
    forward_cube.level += 1
    forward_cube.held, forward_cube.parts = (), []
    (grad_self_queries,) = tied((grad_self_queries,), *forward_parts)
    self_parts = weight_grads(
        count,
        me_list,
        (hidden_zero, prior_hidden),
        (grad_self_queries, self_key_grads, prior_key_grads, self_value_grads, prior_value_grads),
        (
            (thirds[0], ((((0, 0),), scale),)),
            (thirds[1], ((((0, 1), (1, 2)), 1.0),)),
            (thirds[2], ((((0, 3), (1, 4)), 1.0),)),
        ),
        24,
    )
    self_cube = CubeSum(count, thirds)
    self_cube.add(self_parts)
    (grad_self_queries,) = tied((grad_self_queries,), *self_parts)
    zero_part = back_sum(
        (grad_self_queries, self_key_grads, self_value_grads),
        (w_self_query, w_self_key, w_self_value),
        (scale, 1.0, 1.0),
        256,
    )
    zero_other = core_swap(zero_part)
    (returned_mine,) = tied((returned_mine,), zero_part)
    returned_theirs = core_swap(returned_mine)
    self_cube.advance(zero_part)
    forward_cube.add(tied(forward_parts, *self_cube.held))
    self_query_bias_grad = jnp.sum(grad_self_queries.astype(F32), axis=0) * scale
    self_value_bias_grad = jnp.sum(self_value_grads.astype(F32), axis=0) + jnp.sum(prior_value_grads.astype(F32), axis=0)
    zero_other, returned_theirs = tied((zero_other, returned_theirs), *self_cube.held)
    d_tokens, sums_zero = norm_back(
        core_list, zero_part, zero_other, tokens, grad_start_low, ln0_gain, (returned_mine, returned_theirs, row_count - skipped), None, False
    )
    self_cube.advance(sums_zero)
    (sums_zero,) = tied((sums_zero,), *self_cube.held)
    butterfly = ButterflySum(
        (
            sums_zero[0],
            sums_zero[1],
            self_query_bias_grad,
            self_value_bias_grad,
            sums_one[2],
            sums_one[0],
            sums_one[1],
            query_bias_grad,
            value_bias_grad,
            sums_two[2],
            sums_two[0],
            sums_two[1],
            up_bias_grad[0],
            sums_two[3],
        )
    )
    butterfly.step()
    self_cube.advance(butterfly.total)
    butterfly.total, cross_first, *forward_cube.parts = tied(
        (butterfly.total, cross_first, *forward_cube.parts), *self_cube.held
    )
    cross_sums = both_second(cross_first)
    butterfly.step()
    down_other, memory_other = tied((down_other, memory_other), *self_cube.held)
    layer_out = (middle.astype(F32) + (down_part.astype(F32) + down_other.astype(F32)) + b_down).astype(BF)
    d_memory = memory_total(
        memory_rows, jnp.stack([last_image, core]), memory_part, memory_other, returned_mine[row_count - skipped :], returned_theirs[row_count - skipped :]
    )
    self_sums = self_cube.finish()
    small_sums = butterfly.finish()
    forward_sums = forward_cube.finish()
    cross_sums = cross_sums.astype(F32)
    local = w_query.shape[1]

    def cut(table, number):
        return table[:, number * local : (number + 1) * local]

    pieces = forward_sums.astype(F32).reshape(forward_sums.shape[0], -1, 2, tile)
    summed_up = pieces[:, :, 0].reshape(forward_sums.shape[0], -1)
    summed_down = pieces[:, :, 1].reshape(forward_sums.shape[0], -1).T
    return (
        layer_out,
        d_tokens,
        d_memory,
        small_sums[0],
        small_sums[1],
        cut(self_sums, 0),
        small_sums[2],
        cut(self_sums, 1),
        cut(self_sums, 2),
        small_sums[3],
        cut(cross_sums, 4).T,
        small_sums[4],
        small_sums[5],
        small_sums[6],
        cut(cross_sums, 0),
        small_sums[7],
        cut(cross_sums, 1),
        cut(cross_sums, 2),
        small_sums[8],
        cut(cross_sums, 3).T,
        small_sums[9],
        small_sums[10],
        small_sums[11],
        summed_up,
        small_sums[12],
        summed_down,
        small_sums[13],
    )


def solution(mesh):
    in_specs = (
        P("dp", None),
        P("dp"),
        P("dp"),
        P("dp", None, None),
        P(),
        P(),
        P(None, "tensor"),
        P("tensor"),
        P(None, "tensor"),
        P(None, "tensor"),
        P("tensor"),
        P("tensor", None),
        P(),
        P(),
        P(),
        P(None, "tensor"),
        P("tensor"),
        P(None, "tensor"),
        P(None, "tensor"),
        P("tensor"),
        P("tensor", None),
        P(),
        P(),
        P(),
        P(None, "tensor"),
        P("tensor"),
        P("tensor", None),
        P(),
        P("dp", None),
    )
    out_specs = (
        P("dp", None),
        P("dp", None),
        P("dp", None, None),
        P(),
        P(),
        P("dp", "tensor"),
        P("tensor"),
        P("dp", "tensor"),
        P("dp", "tensor"),
        P("tensor"),
        P("tensor", "dp"),
        P(),
        P(),
        P(),
        P("dp", "tensor"),
        P("tensor"),
        P("dp", "tensor"),
        P("dp", "tensor"),
        P("tensor"),
        P("tensor", "dp"),
        P(),
        P(),
        P(),
        P("dp", "tensor"),
        P("tensor"),
        P("tensor", "dp"),
        P(),
    )
    return jax.shard_map(
        per_device, mesh=mesh, in_specs=in_specs, out_specs=out_specs, check_vma=False
    )
```

```python
import functools
import math

import jax
import jax.numpy as jnp
from jax import lax
from jax.experimental import pallas as pl
from jax.experimental.pallas import tpu as pltpu
from jax.sharding import PartitionSpec as P

HEAD_WIDTH = 64


EPSILON = 1e-05


def shifted(value, axis, steps):
    count = lax.axis_size(axis)
    initial, last = (max(0, -steps), min(count, count - steps))
    return lax.ppermute(value, axis, [(source, source + steps) for source in range(initial, last)])


class ButterflySum:
    def __init__(self, vectors):
        self.sizes = [vector.shape[0] for vector in vectors]
        self.total = jnp.concatenate(vectors).reshape(-1, 128)
        self.count = lax.axis_size("dp")
        self.bit = 1

    def step(self):
        pairs = [(i, i ^ self.bit) for i in range(self.count)]
        self.total = self.total + lax.ppermute(self.total, "dp", pairs)
        self.bit *= 2

    def finish(self):
        while self.bit < self.count:
            self.step()
        flat = self.total.reshape(-1)
        pieces, at = [], 0
        for size in self.sizes:
            pieces.append(flat[at : at + size])
            at += size
        return pieces


BF = jnp.bfloat16
F32 = jnp.float32
NEG = -1e30
TILE = 256
HEAD_WIDTH = 64
PAIR = 2 * HEAD_WIDTH
MIB = 1024 * 1024


def nt(left, right):
    return lax.dot_general(left, right, (((1,), (1,)), ((), ())), preferred_element_type=F32)


def nn(left, right):
    return lax.dot_general(left, right, (((1,), (0,)), ((), ())), preferred_element_type=F32)


def head_half(pair, half):
    lane = lax.broadcasted_iota(jnp.int32, pair.shape, 1)
    keep = lane < HEAD_WIDTH if half == 0 else lane >= HEAD_WIDTH
    return jnp.where(keep, pair, jnp.zeros_like(pair))


def span(index, size=TILE):
    return pl.ds(pl.multiple_of(index * size, size), size)


HEAD_ROWS = 80


def column_max(values):
    rows = values.shape[0]
    groups = max(1, rows // 64)
    step = -(-(rows // groups) // 8) * 8
    parts = []
    at = 0
    while at < rows:
        end = min(rows, at + step)
        parts.append(jnp.max(values[at:end], axis=0, keepdims=True))
        at = end
    while len(parts) > 1:
        parts = [jnp.maximum(*parts[i : i + 2]) if i + 1 < len(parts) else parts[i] for i in range(0, len(parts), 2)]
    return parts[0]


def extended(values, target, columns):
    turned = values.T
    extra = jnp.where(lax.broadcasted_iota(jnp.int32, (HEAD_ROWS - HEAD_WIDTH, turned.shape[1]), 0) == 0, 1.0, 0.0).astype(BF)
    for h in range(turned.shape[0] // HEAD_WIDTH):
        base = h * HEAD_ROWS
        target[base : base + HEAD_WIDTH, columns] = turned[h * HEAD_WIDTH : (h + 1) * HEAD_WIDTH, :]
        target[base + HEAD_WIDTH : base + HEAD_ROWS, columns] = extra


def lane_rows(i):
    return i * TILE + lax.broadcasted_iota(jnp.int32, (1, TILE), 1)


def self_forward_body(meta, q_ref, kp_ref, k_ref, vp_ref, v_ref, o_ref, log_ref,
                      vpt, vt, qm, bias, m_s, acc, done, scores):
    rows = q_ref.shape[0]
    pairs = q_ref.shape[1] // PAIR
    b1, b2, p0 = meta[0], meta[1], meta[2]
    tiles = rows // TILE
    offset = rows - kp_ref.shape[0]
    prior_tiles = kp_ref.shape[0] // TILE
    first_prior = (p0 - offset) // TILE
    prior_rows = (b1 + TILE - 1) // TILE

    def turn_own(j, c):
        extended(v_ref[span(j), :], vt, span(j))
        return c

    lax.fori_loop(0, tiles, turn_own, 0)

    def turn_prior(j, c):
        extended(vp_ref[span(j), :], vpt, span(j))
        return c

    lax.fori_loop(jnp.where(b1 > 0, first_prior, prior_tiles), prior_tiles, turn_prior, 0)

    def key_step(keys, values_t, j):
        for pair in range(pairs):
            key_pair = keys[span(j), pair * PAIR : pair * PAIR + PAIR]
            for half in range(2):
                scores[2 * pair + half] = nt(key_pair, qm[2 * pair + half])
        for pair in range(pairs):
            for half in range(2):
                h = 2 * pair + half
                heads = slice(h * HEAD_ROWS, (h + 1) * HEAD_ROWS)
                s = scores[h] + bias[...]
                m_old = m_s[h : h + 1, :]
                m_new = jnp.maximum(m_old, column_max(s))
                alpha = jnp.exp(m_old - m_new)
                e = jnp.exp(s - m_new)
                m_s[h : h + 1, :] = m_new
                acc[heads, :] = acc[heads, :] * alpha + nn(values_t[heads, span(j)], e.astype(BF))

    def row_tile(i, c):
        t = lane_rows(i)
        start = jnp.where(t < b1, 0, jnp.where(t < b2, b1, b2))
        for pair in range(pairs):
            q_pair = q_ref[span(i), pair * PAIR : pair * PAIR + PAIR]
            for half in range(2):
                qm[2 * pair + half] = head_half(q_pair, half)
        m_s[...] = jnp.full_like(m_s, NEG)
        acc[...] = jnp.zeros_like(acc)

        def prior(j, c2):
            r = offset + j * TILE + lax.broadcasted_iota(jnp.int32, (TILE, TILE), 0)
            bias[...] = jnp.where((r >= p0) & (t < b1), 0.0, NEG)
            key_step(kp_ref, vpt, j)
            return c2

        lax.fori_loop(jnp.where(i < prior_rows, first_prior, prior_tiles), prior_tiles, prior, 0)
        t_first = i * TILE
        lowest = jnp.where(t_first < b1, 0, jnp.where(t_first < b2, b1, b2))

        def own(j, c2):
            r = j * TILE + lax.broadcasted_iota(jnp.int32, (TILE, TILE), 0)
            bias[...] = jnp.where((r <= t) & (r >= start), 0.0, NEG)
            key_step(k_ref, vt, j)
            return c2

        lax.fori_loop(lowest // TILE, i + 1, own, 0)
        for h in range(2 * pairs):
            base = h * HEAD_ROWS
            total = acc[base + HEAD_WIDTH : base + HEAD_WIDTH + 1, :]
            log_ref[h : h + 1, span(i)] = m_s[h : h + 1, :] + jnp.log(total)
            done[h * HEAD_WIDTH : (h + 1) * HEAD_WIDTH, :] = acc[base : base + HEAD_WIDTH, :] * (1.0 / total)
        o_ref[span(i), :] = done[...].T.astype(BF)
        return c

    lax.fori_loop(0, tiles, row_tile, 0)


SMEM_SPEC = pl.BlockSpec(memory_space=pltpu.SMEM)
VMEM_SPEC = pl.BlockSpec(memory_space=pltpu.VMEM)
ANY_SPEC = pl.BlockSpec(memory_space=pl.ANY)


def self_forward(meta, q, k_prior, k, v_prior, v):
    rows, width = q.shape
    heads = width // HEAD_WIDTH
    return pl.pallas_call(
        self_forward_body,
        out_shape=(jax.ShapeDtypeStruct((rows, width), BF), jax.ShapeDtypeStruct((heads, rows), F32)),
        in_specs=[SMEM_SPEC] + [VMEM_SPEC] * 5,
        out_specs=(VMEM_SPEC, VMEM_SPEC),
        scratch_shapes=[
            pltpu.VMEM((heads * HEAD_ROWS, k_prior.shape[0]), BF),
            pltpu.VMEM((heads * HEAD_ROWS, rows), BF),
            pltpu.VMEM((heads, TILE, PAIR), BF),
            pltpu.VMEM((TILE, TILE), F32),
            pltpu.VMEM((heads, TILE), F32),
            pltpu.VMEM((heads * HEAD_ROWS, TILE), F32),
            pltpu.VMEM((width, TILE), F32),
            pltpu.VMEM((heads, TILE, TILE), F32),
        ],
        compiler_params=pltpu.CompilerParams(vmem_limit_bytes=16 * MIB),
        cost_estimate=pl.CostEstimate(flops=2 * 2 * rows * rows * width, bytes_accessed=8 * rows * width * 2, transcendentals=rows * rows * heads),
        name="self_forward",
    )(meta, q, k_prior, k, v_prior, v)


def grad_rows(do_ref, o_ref, i, width):
    heads = width // HEAD_WIDTH
    product = do_ref[span(i), :].astype(F32) * o_ref[span(i), :].astype(F32)
    high = product.astype(BF)
    low = (product - high.astype(F32)).astype(BF)
    head = lax.broadcasted_iota(jnp.int32, (heads, width), 0)
    column = lax.broadcasted_iota(jnp.int32, (heads, width), 1) // HEAD_WIDTH
    pick = jnp.where(head == column, 1.0, 0.0).astype(BF)
    return nt(pick, high) + nt(pick, low)


def halves(source, i, target, pairs):
    for pair in range(pairs):
        value = source[span(i), pair * PAIR : pair * PAIR + PAIR]
        for half in range(2):
            target[2 * pair + half] = head_half(value, half)


def grad_step(pairs, keys, values, keys_t, key_slice, key_lanes, qm, dom, shift, delta, bias, dk, dv, dqt, scores, grads):
    for pair in range(pairs):
        cols = slice(pair * PAIR, pair * PAIR + PAIR)
        key_pair = keys[key_slice, cols]
        value_pair = values[key_slice, cols]
        for half in range(2):
            h = 2 * pair + half
            scores[h] = nt(key_pair, qm[h])
            grads[h] = nt(value_pair, dom[h])
    for pair in range(pairs):
        cols = slice(pair * PAIR, pair * PAIR + PAIR)
        dv_pair = dv[key_slice, cols]
        dk_pair = dk[key_slice, cols]
        for half in range(2):
            h = 2 * pair + half
            heads = slice(h * HEAD_WIDTH, (h + 1) * HEAD_WIDTH)
            s = scores[h]
            if bias is not None:
                s = s + bias[...]
            p = jnp.exp(s - shift[h : h + 1, :])
            dp = grads[h]
            ds = (p * (dp - delta[h : h + 1, :])).astype(BF)
            dv_pair = dv_pair + nn(p.astype(BF), dom[h])
            dk_pair = dk_pair + nn(ds, qm[h])
            dqt[heads, :] = dqt[heads, :] + nn(keys_t[heads, key_lanes], ds)
        dv[key_slice, cols] = dv_pair
        dk[key_slice, cols] = dk_pair


def self_prior_back_body(meta, q_ref, do_ref, o_ref, log_ref, k_ref, v_ref, dk_ref, dv_ref, dq_ref,
                         kt, qm, dom, bias, delta, shift, dqt, dk, dv, scores, grads):
    rows, width = q_ref.shape
    pairs = width // PAIR
    b1, p0 = meta[0], meta[2]
    tiles = rows // TILE
    offset = rows - k_ref.shape[0]
    prior_tiles = k_ref.shape[0] // TILE
    first_prior = (p0 - offset) // TILE
    prior_rows = (b1 + TILE - 1) // TILE
    dk[...] = jnp.zeros_like(dk)
    dv[...] = jnp.zeros_like(dv)

    def turn(j, c):
        kt[:, span(j)] = k_ref[span(j), :].T
        return c

    lax.fori_loop(jnp.where(b1 > 0, first_prior, prior_tiles), prior_tiles, turn, 0)

    def row_tile(i, c):
        dqt[...] = jnp.zeros_like(dqt)
        t = lane_rows(i)

        @pl.when(i < prior_rows)
        def _():
            halves(q_ref, i, qm, pairs)
            halves(do_ref, i, dom, pairs)
            delta[...] = grad_rows(do_ref, o_ref, i, width)
            shift[...] = log_ref[:, span(i)]

        def prior(j, c2):
            r = offset + j * TILE + lax.broadcasted_iota(jnp.int32, (TILE, TILE), 0)
            bias[...] = jnp.where((r >= p0) & (t < b1), 0.0, NEG)
            grad_step(pairs, k_ref, v_ref, kt, span(j), span(j), qm, dom, shift, delta, bias, dk, dv, dqt, scores, grads)
            return c2

        lax.fori_loop(jnp.where(i < prior_rows, first_prior, prior_tiles), prior_tiles, prior, 0)
        dq_ref[span(i), :] = dqt[...].T
        return c

    lax.fori_loop(0, tiles, row_tile, 0)
    dk_ref[...] = dk[...].astype(BF)
    dv_ref[...] = dv[...].astype(BF)


def self_own_back_body(meta, q_ref, do_ref, o_ref, log_ref, k_ref, v_ref, dqp_ref, dk_ref, dv_ref, dq_ref,
                       kt, qm, dom, bias, delta, shift, dqt, dk, dv, scores, grads):
    rows, width = q_ref.shape
    pairs = width // PAIR
    b1, b2 = meta[0], meta[1]
    tiles = rows // TILE
    dk[...] = jnp.zeros_like(dk)
    dv[...] = jnp.zeros_like(dv)

    def turn(j, c):
        kt[:, span(j)] = k_ref[span(j), :].T
        return c

    lax.fori_loop(0, tiles, turn, 0)

    def row_tile(i, c):
        dqt[...] = jnp.zeros_like(dqt)
        t = lane_rows(i)
        start = jnp.where(t < b1, 0, jnp.where(t < b2, b1, b2))
        halves(q_ref, i, qm, pairs)
        halves(do_ref, i, dom, pairs)
        delta[...] = grad_rows(do_ref, o_ref, i, width)
        shift[...] = log_ref[:, span(i)]
        t_first = i * TILE
        lowest = jnp.where(t_first < b1, 0, jnp.where(t_first < b2, b1, b2))

        def own(j, c2):
            r = j * TILE + lax.broadcasted_iota(jnp.int32, (TILE, TILE), 0)
            bias[...] = jnp.where((r <= t) & (r >= start), 0.0, NEG)
            grad_step(pairs, k_ref, v_ref, kt, span(j), span(j), qm, dom, shift, delta, bias, dk, dv, dqt, scores, grads)
            return c2

        lax.fori_loop(lowest // TILE, i + 1, own, 0)
        dq_ref[span(i), :] = (dqp_ref[span(i), :] + dqt[...].T).astype(BF)
        return c

    lax.fori_loop(0, tiles, row_tile, 0)
    dk_ref[...] = dk[...].astype(BF)
    dv_ref[...] = dv[...].astype(BF)


def self_back_scratch(keys, width):
    heads = width // HEAD_WIDTH
    return [
        pltpu.VMEM((width, keys), BF),
        pltpu.VMEM((heads, TILE, PAIR), BF),
        pltpu.VMEM((heads, TILE, PAIR), BF),
        pltpu.VMEM((TILE, TILE), F32),
        pltpu.VMEM((heads, TILE), F32),
        pltpu.VMEM((heads, TILE), F32),
        pltpu.VMEM((width, TILE), F32),
        pltpu.VMEM((keys, width), F32),
        pltpu.VMEM((keys, width), F32),
        pltpu.VMEM((heads, TILE, TILE), F32),
        pltpu.VMEM((heads, TILE, TILE), F32),
    ]


def self_prior_back(meta, q, do, o, logs, k_prior, v_prior):
    rows, width = q.shape
    return pl.pallas_call(
        self_prior_back_body,
        out_shape=(jax.ShapeDtypeStruct(k_prior.shape, BF), jax.ShapeDtypeStruct(k_prior.shape, BF),
                   jax.ShapeDtypeStruct((rows, width), F32)),
        in_specs=[SMEM_SPEC] + [VMEM_SPEC] * 6,
        out_specs=(VMEM_SPEC,) * 3,
        scratch_shapes=self_back_scratch(k_prior.shape[0], width),
        compiler_params=pltpu.CompilerParams(vmem_limit_bytes=22 * MIB),
        cost_estimate=pl.CostEstimate(flops=3 * rows * rows * width, bytes_accessed=8 * rows * width * 2, transcendentals=rows * rows * 4),
        name="self_prior_back",
    )(meta, q, do, o, logs, k_prior, v_prior)


def self_own_back(meta, q, do, o, logs, k, v, dq_prior):
    rows, width = q.shape
    return pl.pallas_call(
        self_own_back_body,
        out_shape=(jax.ShapeDtypeStruct((rows, width), BF),) * 3,
        in_specs=[SMEM_SPEC] + [VMEM_SPEC] * 7,
        out_specs=(VMEM_SPEC,) * 3,
        scratch_shapes=self_back_scratch(rows, width),
        compiler_params=pltpu.CompilerParams(vmem_limit_bytes=26 * MIB),
        cost_estimate=pl.CostEstimate(flops=5 * rows * rows * width, bytes_accessed=8 * rows * width * 2, transcendentals=rows * rows * 4),
        name="self_own_back",
    )(meta, q, do, o, logs, k, v, dq_prior)


def segment(meta, index, rows):
    first = jnp.where(index == 0, 0, jnp.where(index == 1, meta[0], meta[1]))
    last = jnp.where(index == 0, meta[0], jnp.where(index == 1, meta[1], rows))
    return first, last, meta[3 + index]


def gather_tables(kp_ref, k_ref, vp_ref, v_ref, k_all, v_all, sems):
    own = k_ref.shape[0]
    copies = [
        pltpu.make_async_copy(k_ref, k_all.at[:own, :], sems.at[0]),
        pltpu.make_async_copy(v_ref, v_all.at[:own, :], sems.at[1]),
        pltpu.make_async_copy(kp_ref, k_all.at[own:, :], sems.at[2]),
        pltpu.make_async_copy(vp_ref, v_all.at[own:, :], sems.at[3]),
    ]
    for copy in copies:
        copy.start()
    for copy in copies:
        copy.wait()


def segments(meta, rows):
    return ((0, meta[0], None), (meta[0], meta[1], meta[4]), (meta[1], rows, meta[5]))


def cross_forward_body(used, meta, q_ref, kp_ref, k_ref, vp_ref, v_ref, o_ref, log_ref, vpt, vt, qm, acc, scores):
    rows, width = q_ref.shape
    pairs = width // PAIR
    padded = kp_ref.shape[0]
    images = k_ref.shape[0] // padded
    for slot in range(images):
        extended(v_ref[slot * padded : (slot + 1) * padded, :], vt.at[slot], slice(None))
    extended(vp_ref[...], vpt, slice(None))
    for first, last, slot in segments(meta, rows):
        own = slot is not None
        keys = pl.ds(pl.multiple_of(slot * padded, 16), padded) if own else slice(None)
        key_table = k_ref if own else kp_ref
        value_table = vt.at[slot] if own else vpt

        def tile(i, c):
            halves(q_ref, i, qm, pairs)
            t = lane_rows(i)
            inside = (t >= first) & (t < last)
            for pair in range(pairs):
                key_pair = key_table[keys, pair * PAIR : pair * PAIR + PAIR]
                for half in range(2):
                    scores[2 * pair + half] = nt(key_pair, qm[2 * pair + half])
            for h in range(2 * pairs):
                heads = slice(h * HEAD_WIDTH, (h + 1) * HEAD_WIDTH)
                s = scores[h]
                if used < padded:
                    row = lax.broadcasted_iota(jnp.int32, s.shape, 0)
                    s = jnp.where(row < used, s, NEG)
                m = column_max(s)
                e = jnp.exp(s - m)
                mixed = nn(value_table[h * HEAD_ROWS : (h + 1) * HEAD_ROWS, :], e.astype(BF))
                total = mixed[HEAD_WIDTH : HEAD_WIDTH + 1, :]
                acc[heads, :] = mixed[:HEAD_WIDTH, :] * (1.0 / total)
                log_ref[h : h + 1, span(i)] = jnp.where(
                    inside, m + jnp.log(total), log_ref[h : h + 1, span(i)]
                )
            column = i * TILE + lax.broadcasted_iota(jnp.int32, (TILE, width), 0)
            keep = (column >= first) & (column < last)
            o_ref[span(i), :] = jnp.where(keep, acc[...].T, o_ref[span(i), :].astype(F32)).astype(BF)
            return c

        lax.fori_loop(first // TILE, jnp.where(last > first, (last + TILE - 1) // TILE, 0), tile, 0)


def cross_forward(used, meta, q, k_prior, k, v_prior, v):
    rows, width = q.shape
    heads = width // HEAD_WIDTH
    padded = k_prior.shape[0]
    return pl.pallas_call(
        functools.partial(cross_forward_body, used),
        out_shape=(jax.ShapeDtypeStruct((rows, width), BF), jax.ShapeDtypeStruct((heads, rows), F32)),
        in_specs=[SMEM_SPEC] + [VMEM_SPEC] * 5,
        out_specs=(VMEM_SPEC, VMEM_SPEC),
        scratch_shapes=[
            pltpu.VMEM((heads * HEAD_ROWS, padded), BF),
            pltpu.VMEM((k.shape[0] // padded, heads * HEAD_ROWS, padded), BF),
            pltpu.VMEM((heads, TILE, PAIR), BF),
            pltpu.VMEM((width, TILE), F32),
            pltpu.VMEM((heads, padded, TILE), F32),
        ],
        compiler_params=pltpu.CompilerParams(vmem_limit_bytes=20 * MIB),
        cost_estimate=pl.CostEstimate(flops=16 * rows * padded * width, bytes_accessed=8 * rows * width * 2, transcendentals=rows * padded * heads),
        name="cross_forward",
    )(meta, q, k_prior, k, v_prior, v)


def cross_back_body(used, meta, q_ref, do_ref, o_ref, log_ref, kp_ref, k_ref, vp_ref, v_ref, dkp_ref, dk_ref, dvp_ref, dv_ref,
                    dq_ref, k_all, v_all, kt, qm, dom, delta, shift, dqt, dk, dv, scores, grads, sems):
    rows, width = q_ref.shape
    pairs = width // PAIR
    padded = kp_ref.shape[0]
    images = k_all.shape[0] // padded
    gather_tables(kp_ref, k_ref, vp_ref, v_ref, k_all, v_all, sems)
    for item in (dk, dv):
        item[...] = jnp.zeros_like(item)

    def turn(slot, c):
        kt[slot] = k_all[pl.ds(pl.multiple_of(slot * padded, 16), padded), :].T
        return c

    lax.fori_loop(0, images, turn, 0)

    def one(index, c0):
        first, last, slot = segment(meta, index, rows)
        keys = pl.ds(pl.multiple_of(slot * padded, 16), padded)

        def tile(i, c):
            halves(q_ref, i, qm, pairs)
            halves(do_ref, i, dom, pairs)
            t = lane_rows(i)
            inside = (t >= first) & (t < last)
            delta[...] = grad_rows(do_ref, o_ref, i, width)
            shift[...] = jnp.where(inside, log_ref[:, span(i)], -NEG)
            dqt[...] = jnp.zeros_like(dqt)
            grad_step(pairs, k_all, v_all, kt.at[slot], keys, slice(None), qm, dom, shift, delta, None, dk, dv, dqt, scores, grads)
            column = i * TILE + lax.broadcasted_iota(jnp.int32, (TILE, width), 0)
            keep = (column >= first) & (column < last)
            dq_ref[span(i), :] = jnp.where(keep, dqt[...].T, dq_ref[span(i), :].astype(F32)).astype(BF)
            return c

        lax.fori_loop(first // TILE, jnp.where(last > first, (last + TILE - 1) // TILE, 0), tile, 0)
        return c0

    lax.fori_loop(0, 3, one, 0)
    inner = lax.broadcasted_iota(jnp.int32, (padded, width), 0) < used
    for source, own_target, prior_target in ((dk, dk_ref, dkp_ref), (dv, dv_ref, dvp_ref)):
        for slot in range(images):
            part = slice(slot * padded, (slot + 1) * padded)
            value = jnp.where(inner, source[part, :], 0.0).astype(BF)
            if slot < images - 1:
                own_target[part, :] = value
            else:
                prior_target[...] = value


def cross_back(used, meta, q, do, o, logs, k_prior, k, v_prior, v):
    rows, width = q.shape
    heads = width // HEAD_WIDTH
    padded = k_prior.shape[0]
    every = padded + k.shape[0]
    tables = (k_prior, k, v_prior, v)
    return pl.pallas_call(
        functools.partial(cross_back_body, used),
        out_shape=tuple(jax.ShapeDtypeStruct(table.shape, BF) for table in tables) + (jax.ShapeDtypeStruct((rows, width), BF),),
        in_specs=[SMEM_SPEC] + [VMEM_SPEC] * 4 + [ANY_SPEC] * 4,
        out_specs=(VMEM_SPEC,) * 5,
        scratch_shapes=[
            pltpu.VMEM((every, width), BF),
            pltpu.VMEM((every, width), BF),
            pltpu.VMEM((every // padded, width, padded), BF),
            pltpu.VMEM((heads, TILE, PAIR), BF),
            pltpu.VMEM((heads, TILE, PAIR), BF),
            pltpu.VMEM((heads, TILE), F32),
            pltpu.VMEM((heads, TILE), F32),
            pltpu.VMEM((width, TILE), F32),
            pltpu.VMEM((every, width), F32),
            pltpu.VMEM((every, width), F32),
            pltpu.VMEM((heads, padded, TILE), F32),
            pltpu.VMEM((heads, padded, TILE), F32),
            pltpu.SemaphoreType.DMA((4,)),
        ],
        compiler_params=pltpu.CompilerParams(vmem_limit_bytes=44 * MIB),
        cost_estimate=pl.CostEstimate(flops=40 * rows * padded * width, bytes_accessed=12 * rows * width * 2, transcendentals=rows * padded * heads),
        name="cross_back",
    )(meta, q, do, o, logs, *tables)


SQRT_HALF = 0.7071067811865476
GAUSS = 0.3989422804014327
ROW_CHUNK = 256


def error_function(x):
    x = jnp.clip(x, -4.0, 4.0)
    z = x * x
    top = -2.72614225801306e-10
    for term in (2.77068142495902e-08, -2.10102402082508e-06, -5.69250639462346e-05,
                 -7.34990630326855e-04, -2.95459980854025e-03, -1.60960333262415e-02):
        top = top * z + term
    low = -1.45660718464996e-05
    for term in (-2.13374055278905e-04, -1.68282697438203e-03, -7.37332916720468e-03, -1.42647390514189e-02):
        low = low * z + term
    return x * top / low


def row_norm(values):
    mean = jnp.mean(values, axis=-1, keepdims=True)
    centered = values - mean
    inverse = lax.rsqrt(jnp.mean(centered * centered, axis=-1, keepdims=True) + EPSILON)
    return centered * inverse, inverse


def chunk_place(index, inner, outer):
    return (index % inner) * outer + index // inner


def feed_forward_body(inner, outer, start_ref, own_ref, other_ref, b_out, gain, shift_in, dy_ref, w_up, b_up, w_down,
                      y1_ref, down_ref, dh_ref, grads_ref, db_ref,
                      h2, h2t, dyt, acc_down, acc_dh, u_s, da_s, g_s, du_s):
    step = pl.program_id(0)
    rows, width = dy_ref.shape
    tile = w_up.shape[1]
    chunks = rows // ROW_CHUNK

    @pl.when(step == 0)
    def _():
        for r in range(chunks):
            part = slice(r * ROW_CHUNK, (r + 1) * ROW_CHUNK)
            y1 = start_ref[part, :].astype(F32) + (own_ref[part, :].astype(F32) + other_ref[part, :].astype(F32)) + b_out[...]
            y1_ref[part, :] = y1.astype(BF)
            normed, _ = row_norm(y1)
            low = (normed * gain[...] + shift_in[...]).astype(BF)
            h2[part, :] = low
            h2t[:, part] = low.T
            dyt[:, part] = dy_ref[part, :].T
        acc_down[...] = jnp.zeros_like(acc_down)
        acc_dh[...] = jnp.zeros_like(acc_dh)

    for r in range(chunks):
        part = slice(r * ROW_CHUNK, (r + 1) * ROW_CHUNK)
        u_s[part, :] = nn(h2[part, :], w_up[...]) + b_up[...]
        da_s[part, :] = nt(dy_ref[part, :], w_down[...])
    total = jnp.zeros((1, tile), F32)
    for r in range(chunks):
        part = slice(r * ROW_CHUNK, (r + 1) * ROW_CHUNK)
        u = u_s[part, :]
        half = 0.5 + 0.5 * error_function(u * SQRT_HALF)
        g = (u * half).astype(BF)
        slope = half + u * (GAUSS * jnp.exp(-0.5 * u * u))
        du = (da_s[part, :] * slope).astype(BF)
        g_s[part, :] = g
        du_s[part, :] = du
        total = total + jnp.sum(du.astype(F32), axis=0, keepdims=True)
        down = nn(g, w_down[...])
        dh = nt(du, w_up[...])
        acc_down[part, :] += down
        acc_dh[part, :] += dh

    db_ref[...] = total
    piece = width // (inner * outer)
    for source, turned, at in ((du_s, h2t, 0), (g_s, dyt, tile)):
        for r in range(width // ROW_CHUNK):
            part = slice(r * ROW_CHUNK, (r + 1) * ROW_CHUNK)
            product = nn(turned[part, :], source[...]).astype(BF)
            for c in range(ROW_CHUNK // piece):
                place = chunk_place(r * (ROW_CHUNK // piece) + c, inner, outer) * piece
                grads_ref[place : place + piece, at : at + tile] = product[c * piece : (c + 1) * piece, :]

    @pl.when(step == pl.num_programs(0) - 1)
    def _():
        down_ref[...] = acc_down[...].astype(BF)
        dh_ref[...] = acc_dh[...].astype(BF)


def feed_forward(inner, outer, tile, start, own, other, b_out, gain, shift_in, dy, w_up, b_up, w_down):
    rows, width = dy.shape
    hidden = w_up.shape[1]
    whole = lambda shape: pl.BlockSpec(shape, lambda k: (0, 0), pipeline_mode=pl.Buffered(1))
    row = whole((1, width))
    full = whole((rows, width))
    return pl.pallas_call(
        functools.partial(feed_forward_body, inner, outer),
        grid=(hidden // tile,),
        out_shape=(
            jax.ShapeDtypeStruct((rows, width), BF),
            jax.ShapeDtypeStruct((rows, width), BF),
            jax.ShapeDtypeStruct((rows, width), BF),
            jax.ShapeDtypeStruct((width, 2 * hidden), BF),
            jax.ShapeDtypeStruct((1, hidden), F32),
        ),
        in_specs=[full, full, full, row, row, row, full,
                  pl.BlockSpec((width, tile), lambda k: (0, k)),
                  pl.BlockSpec((1, tile), lambda k: (0, k)),
                  pl.BlockSpec((tile, width), lambda k: (k, 0))],
        out_specs=(full, full, full, pl.BlockSpec((width, 2 * tile), lambda k: (0, k)), pl.BlockSpec((1, tile), lambda k: (0, k))),
        scratch_shapes=[
            pltpu.VMEM((rows, width), BF),
            pltpu.VMEM((width, rows), BF),
            pltpu.VMEM((width, rows), BF),
            pltpu.VMEM((rows, width), F32),
            pltpu.VMEM((rows, width), F32),
            pltpu.VMEM((rows, tile), F32),
            pltpu.VMEM((rows, tile), F32),
            pltpu.VMEM((rows, tile), BF),
            pltpu.VMEM((rows, tile), BF),
        ],
        compiler_params=pltpu.CompilerParams(vmem_limit_bytes=54 * MIB),
        cost_estimate=pl.CostEstimate(flops=12 * rows * width * hidden, bytes_accessed=30 * rows * width, transcendentals=rows * hidden * 2),
        name="feed_forward",
    )(start, own, other, b_out.reshape(1, -1), gain.reshape(1, -1), shift_in.reshape(1, -1), dy, w_up, b_up.reshape(1, -1), w_down)

def norm_project_body(flags, weight_flags, *refs):
    has_extra, emit_base, emit_hidden = flags
    refs = list(refs)
    values = refs.pop(0)[...].astype(F32)
    if has_extra:
        own, other, offset = refs.pop(0), refs.pop(0), refs.pop(0)
        values = values + (own[...].astype(F32) + other[...].astype(F32)) + offset[...]
    gain, shift_in = refs.pop(0), refs.pop(0)
    weights = []
    for has_bias, factor in weight_flags:
        weight = refs.pop(0)
        weights.append((weight, refs.pop(0) if has_bias else None, factor))
    if emit_base:
        refs.pop(0)[...] = values.astype(BF)
    normed, _ = row_norm(values)
    hidden = (normed * gain[...] + shift_in[...]).astype(BF)
    if emit_hidden:
        refs.pop(0)[...] = hidden
    for weight, offset, factor in weights:
        product = nn(hidden, weight[...])
        if offset is not None:
            product = product + offset[...]
        if factor != 1.0:
            product = product * factor
        refs.pop(0)[...] = product.astype(BF)


def norm_project(base, extra, gain, shift_in, weights, emit_base, emit_hidden):
    rows, width = base.shape
    tile = ROW_CHUNK
    block = pl.BlockSpec((tile, width), lambda i: (i, 0))
    fixed = lambda shape: pl.BlockSpec(shape, lambda i: (0, 0), pipeline_mode=pl.Buffered(1))
    operands, specs = [base], [block]
    if extra is not None:
        own, other, offset = extra
        operands += [own, other, offset.reshape(1, -1)]
        specs += [block, block, fixed((1, width))]
    operands += [gain.reshape(1, -1), shift_in.reshape(1, -1)]
    specs += [fixed((1, width))] * 2
    shapes, outs = [], []
    if emit_base:
        shapes.append(jax.ShapeDtypeStruct((rows, width), BF))
        outs.append(block)
    if emit_hidden:
        shapes.append(jax.ShapeDtypeStruct((rows, width), BF))
        outs.append(block)
    for weight, offset, _ in weights:
        operands.append(weight)
        specs.append(fixed(weight.shape))
        if offset is not None:
            operands.append(offset.reshape(1, -1))
            specs.append(fixed((1, weight.shape[1])))
        shapes.append(jax.ShapeDtypeStruct((rows, weight.shape[1]), BF))
        outs.append(pl.BlockSpec((tile, weight.shape[1]), lambda i: (i, 0)))
    flops = sum(2 * rows * width * weight.shape[1] for weight, _, _ in weights)
    return pl.pallas_call(
        functools.partial(norm_project_body, (extra is not None, emit_base, emit_hidden),
                          tuple((offset is not None, factor) for _, offset, factor in weights)),
        grid=(rows // tile,),
        out_shape=tuple(shapes),
        in_specs=specs,
        out_specs=tuple(outs),
        compiler_params=pltpu.CompilerParams(vmem_limit_bytes=12 * MIB),
        cost_estimate=pl.CostEstimate(flops=2 * flops, bytes_accessed=10 * rows * width, transcendentals=0),
        name="norm_project",
    )(*operands)


def norm_back_body(flags, *refs):
    skip, has_back, has_weight, grad_sum = flags
    refs = list(refs)
    core = refs.pop(0)
    own, other, base, grad, gain = (refs.pop(0) for _ in range(5))
    step = pl.program_id(0)
    total = own[...].astype(F32) + other[...].astype(F32)
    if has_back:
        mine, theirs = refs.pop(0)[...].astype(F32), refs.pop(0)[...].astype(F32)
        first = core[0] == 0
        back = jnp.concatenate([jnp.where(first, mine, theirs), jnp.where(first, theirs, mine)], 1)
        total = total + jnp.where(step >= skip, back, 0.0)
    if has_weight:
        weight = refs.pop(0)
    normed, inverse = row_norm(base[...].astype(F32))
    scaled = total * gain[...]
    inner = (
        scaled
        - jnp.mean(scaled, axis=-1, keepdims=True)
        - normed * jnp.mean(scaled * normed, axis=-1, keepdims=True)
    )
    result = grad[...].astype(F32) + inner * inverse
    low = result.astype(BF)
    refs.pop(0)[...] = low
    if has_weight:
        refs.pop(0)[...] = nt(low, weight[...]).astype(BF)
    sums = refs.pop(0)

    @pl.when(step == 0)
    def _():
        sums[...] = jnp.zeros_like(sums)

    sums[0:1, :] += jnp.sum(total * normed, axis=0, keepdims=True)
    sums[1:2, :] += jnp.sum(total, axis=0, keepdims=True)
    if has_weight:
        sums[2:3, :] += jnp.sum(low.astype(F32), axis=0, keepdims=True)
        if grad_sum:
            sums[3:4, :] += jnp.sum(grad[...].astype(F32), axis=0, keepdims=True)


def norm_back(core, own, other, base, grad, gain, returned, weight, grad_sum):
    rows, width = own.shape
    tile = ROW_CHUNK
    block = pl.BlockSpec((tile, width), lambda i: (i, 0))
    fixed = lambda shape: pl.BlockSpec(shape, lambda i: (0, 0), pipeline_mode=pl.Buffered(1))
    operands = [core, own, other, base, grad, gain.reshape(1, -1)]
    specs = [SMEM_SPEC, block, block, block, block, fixed((1, width))]
    skip = 0
    if returned is not None:
        skip = (rows - returned[2]) // tile
        operands += list(returned[:2])
        specs += [pl.BlockSpec((tile, width // 2), lambda i: (jnp.maximum(i - skip, 0), 0))] * 2
    shapes, outs = [], []
    if weight is not None:
        operands.append(weight)
        specs.append(fixed(weight.shape))
    shapes.append(jax.ShapeDtypeStruct((rows, width), BF))
    outs.append(block)
    if weight is not None:
        shapes.append(jax.ShapeDtypeStruct((rows, weight.shape[0]), BF))
        outs.append(pl.BlockSpec((tile, weight.shape[0]), lambda i: (i, 0)))
    shapes.append(jax.ShapeDtypeStruct((8, width), F32))
    outs.append(pl.BlockSpec((8, width), lambda i: (0, 0)))
    return pl.pallas_call(
        functools.partial(norm_back_body, (skip, returned is not None, weight is not None, grad_sum)),
        grid=(rows // tile,),
        out_shape=tuple(shapes),
        in_specs=specs,
        out_specs=tuple(outs),
        compiler_params=pltpu.CompilerParams(vmem_limit_bytes=18 * MIB),
        cost_estimate=pl.CostEstimate(flops=4 * rows * width * 512, bytes_accessed=16 * rows * width, transcendentals=0),
        name="norm_back",
    )(*operands)


def memory_project_body(memory, w_key, w_value, offset, padded, keys, values):
    rows = memory.shape[1]
    padded[rows // 16 * 16 :, :] = jnp.zeros((padded.shape[0] - rows // 16 * 16, padded.shape[1]), BF)
    padded[:rows, :] = memory[0]
    low = padded[...]
    keys[...] = nn(low, w_key[...]).astype(BF)
    values[...] = (nn(low, w_value[...]) + offset[...]).astype(BF)


def memory_project(memory, padded, w_key, w_value, offset):
    images, rows, width = memory.shape
    half = w_key.shape[1]
    fixed = lambda shape: pl.BlockSpec(shape, lambda i: (0, 0), pipeline_mode=pl.Buffered(1))
    return pl.pallas_call(
        memory_project_body,
        grid=(images,),
        out_shape=(
            jax.ShapeDtypeStruct((images * padded, width), BF),
            jax.ShapeDtypeStruct((images * padded, half), BF),
            jax.ShapeDtypeStruct((images * padded, half), BF),
        ),
        in_specs=[pl.BlockSpec((1, rows, width), lambda i: (i, 0, 0)), fixed(w_key.shape), fixed(w_value.shape), fixed((1, half))],
        out_specs=(
            pl.BlockSpec((padded, width), lambda i: (i, 0)),
            pl.BlockSpec((padded, half), lambda i: (i, 0)),
            pl.BlockSpec((padded, half), lambda i: (i, 0)),
        ),
        compiler_params=pltpu.CompilerParams(vmem_limit_bytes=14 * MIB),
        cost_estimate=pl.CostEstimate(flops=4 * images * padded * width * half, bytes_accessed=6 * images * padded * width, transcendentals=0),
        name="memory_project",
    )(memory, w_key, w_value, offset.reshape(1, -1))


def back_sum_body(factors, *refs):
    count = len(factors)
    total = None
    for at, factor in enumerate(factors):
        product = nt(refs[at][...], refs[count + at][...])
        if factor != 1.0:
            product = product * factor
        total = product if total is None else total + product
    refs[2 * count][...] = total.astype(BF)


def back_sum(grads, weights, factors, tile):
    rows, inner = grads[0].shape
    width = weights[0].shape[0]
    return pl.pallas_call(
        functools.partial(back_sum_body, factors),
        grid=(rows // tile,),
        out_shape=jax.ShapeDtypeStruct((rows, width), BF),
        in_specs=[pl.BlockSpec((tile, inner), lambda i: (i, 0))] * len(grads)
        + [pl.BlockSpec(weight.shape, lambda i: (0, 0), pipeline_mode=pl.Buffered(1)) for weight in weights],
        out_specs=pl.BlockSpec((tile, width), lambda i: (i, 0)),
        compiler_params=pltpu.CompilerParams(vmem_limit_bytes=10 * MIB),
        cost_estimate=pl.CostEstimate(flops=4 * rows * inner * width * len(grads), bytes_accessed=4 * rows * inner * len(grads), transcendentals=0),
        name="back_sum",
    )(*grads, *weights)


def bit_orders(count, turns):
    bits = list(range(count.bit_length() - 1))
    return tuple(tuple(bits[turn:turns] + bits[:turn] + bits[turns:]) for turn in range(turns))


def place_code(position, order):
    code = 0
    for rank, bit in enumerate(order):
        if position >> (len(order) - 1 - rank) & 1:
            code |= 1 << bit
    return code


def weight_grads_body(count, sides, left_count, right_count, me, *refs):
    lefts, rights = refs[:left_count], refs[left_count : left_count + right_count]
    outs = refs[left_count + right_count : left_count + right_count + 2 * len(sides)]
    turned = refs[left_count + right_count + 2 * len(sides) : -1]
    natural = refs[-1]
    width = lefts[0].shape[1]
    columns = rights[0].shape[1]
    piece = width // count
    for left, target in zip(lefts, turned):
        for r in range(width // ROW_CHUNK):
            part = slice(r * ROW_CHUNK, (r + 1) * ROW_CHUNK)
            target[part, :] = left[:, part].T
    number = 0
    for side, (order, products) in enumerate(sides):
        keep, send = outs[2 * side], outs[2 * side + 1]
        for at, (terms, factor) in enumerate(products):
            store = natural.at[number % 2]
            number += 1
            for r in range(width // ROW_CHUNK):
                part = slice(r * ROW_CHUNK, (r + 1) * ROW_CHUNK)
                total = None
                for left, right in terms:
                    product = nn(turned[left][part, :], rights[right][...])
                    total = product if total is None else total + product
                store[part, :] = (total * factor if factor != 1.0 else total).astype(BF)
            place = slice(at * columns, (at + 1) * columns)
            for position in range(count):
                source = pl.multiple_of((me[0] ^ place_code(position, order)) * piece, piece)
                target = keep if position < count // 2 else send
                row = position % (count // 2) * piece
                target[row : row + piece, place] = store[pl.ds(source, piece), :]


def placed_grads_body(inner, outer, products, left_count, right_count, *refs):
    lefts, rights = refs[:left_count], refs[left_count : left_count + right_count]
    target = refs[left_count + right_count]
    turned = refs[left_count + right_count + 1 :]
    width = lefts[0].shape[1]
    columns = rights[0].shape[1]
    piece = width // (inner * outer)
    for left, store in zip(lefts, turned):
        for r in range(width // ROW_CHUNK):
            part = slice(r * ROW_CHUNK, (r + 1) * ROW_CHUNK)
            store[part, :] = left[:, part].T
    for at, (terms, factor) in enumerate(products):
        for r in range(width // ROW_CHUNK):
            part = slice(r * ROW_CHUNK, (r + 1) * ROW_CHUNK)
            total = None
            for left, right in terms:
                product = nn(turned[left][part, :], rights[right][...])
                total = product if total is None else total + product
            low = (total * factor if factor != 1.0 else total).astype(BF)
            for c in range(ROW_CHUNK // piece):
                place = chunk_place(r * (ROW_CHUNK // piece) + c, inner, outer) * piece
                target[place : place + piece, at * columns : (at + 1) * columns] = low[c * piece : (c + 1) * piece, :]


def placed_grads(inner, outer, lefts, rights, products):
    width = lefts[0].shape[1]
    columns = rights[0].shape[1]
    flops = sum(2 * width * columns * lefts[left].shape[0] for terms, _ in products for left, _ in terms)
    return pl.pallas_call(
        functools.partial(placed_grads_body, inner, outer, products, len(lefts), len(rights)),
        out_shape=jax.ShapeDtypeStruct((width, columns * len(products)), BF),
        in_specs=[VMEM_SPEC] * (len(lefts) + len(rights)),
        out_specs=VMEM_SPEC,
        scratch_shapes=[pltpu.VMEM((width, left.shape[0]), BF) for left in lefts],
        compiler_params=pltpu.CompilerParams(vmem_limit_bytes=34 * MIB),
        cost_estimate=pl.CostEstimate(flops=flops, bytes_accessed=16 * width * width, transcendentals=0),
        name="placed_grads",
    )(*lefts, *rights)


def weight_grads(count, me, lefts, rights, sides, limit):
    width = lefts[0].shape[1]
    columns = rights[0].shape[1]
    shapes = []
    flops = 0
    for _, products in sides:
        shapes += [jax.ShapeDtypeStruct((width // 2, columns * len(products)), BF)] * 2
        flops += sum(2 * width * columns * lefts[left].shape[0] for terms, _ in products for left, _ in terms)
    return pl.pallas_call(
        functools.partial(weight_grads_body, count, sides, len(lefts), len(rights)),
        out_shape=tuple(shapes),
        in_specs=[SMEM_SPEC] + [VMEM_SPEC] * (len(lefts) + len(rights)),
        out_specs=(VMEM_SPEC,) * len(shapes),
        scratch_shapes=[pltpu.VMEM((width, left.shape[0]), BF) for left in lefts] + [pltpu.VMEM((2, width, columns), BF)],
        compiler_params=pltpu.CompilerParams(vmem_limit_bytes=limit * MIB),
        cost_estimate=pl.CostEstimate(flops=2 * flops, bytes_accessed=16 * width * width, transcendentals=0),
        name="weight_grads",
    )(me, *lefts, *rights)


def fold_body(joined, sides, *refs):
    ins, outs = refs[: 2 * sides], refs[2 * sides :]
    at = 0
    for side in range(sides):
        keep, got = ins[2 * side], ins[2 * side + 1]
        rows, columns = keep.shape
        total = keep[...].astype(F32) + got[...].astype(F32)
        if len(outs) == 1:
            outs[0][...] = total
            continue
        out_keep, out_send = (outs[0], outs[1]) if joined else (outs[2 * side], outs[2 * side + 1])
        out_keep[:, at : at + columns] = total[: rows // 2].astype(BF)
        out_send[:, at : at + columns] = total[rows // 2 :].astype(BF)
        at += columns if joined else 0


def fold(parts, joined, last):
    sides = len(parts) // 2
    rows = parts[0].shape[0]
    widths = [part.shape[1] for part in parts[::2]]
    columns = sum(widths)
    if last:
        shapes = (jax.ShapeDtypeStruct((rows, columns), F32),)
    elif joined:
        shapes = (jax.ShapeDtypeStruct((rows // 2, columns), BF),) * 2
    else:
        shapes = tuple(jax.ShapeDtypeStruct((rows // 2, wide), BF) for wide in widths for _ in range(2))
    return pl.pallas_call(
        functools.partial(fold_body, joined, sides),
        out_shape=shapes,
        in_specs=[VMEM_SPEC] * len(parts),
        out_specs=(VMEM_SPEC,) * len(shapes),
        cost_estimate=pl.CostEstimate(flops=rows * columns, bytes_accessed=6 * rows * columns, transcendentals=0),
        compiler_params=pltpu.CompilerParams(vmem_limit_bytes=11 * MIB),
        name="fold",
    )(*parts)


def tied(values, *tokens):
    return lax.optimization_barrier(tuple(values) + tokens)[: len(values)]


def exchanged(value, bit, count):
    return lax.ppermute(value, "dp", [(i, i ^ (1 << bit)) for i in range(count)])


class CubeSum:
    def __init__(self, count, orders):
        self.count, self.level = count, 0
        self.orders = orders
        self.held, self.parts = (), []

    def add(self, parts):
        first = len(self.held) // 2
        self.held += tuple(parts)
        for side in range(len(parts) // 2):
            bit = self.orders[first + side][self.level]
            self.parts += [parts[2 * side], exchanged(parts[2 * side + 1], bit, self.count)]

    def advance(self, *tokens):
        levels = len(self.orders[0])
        last = self.level == levels - 1
        parts = tied(self.parts, *tokens) if tokens else self.parts
        result = fold(tuple(parts), self.level + 1 == len(self.orders), last)
        self.level += 1
        if last:
            return result[0]
        self.held, self.parts = (), []
        self.add(result)
        return None

    def finish(self):
        while True:
            result = self.advance()
            if result is not None:
                return result


def memory_total_body(where, own, other, mine, theirs, target):
    image = pl.program_id(0)
    rows = target.shape[1]
    half = mine.shape[1]
    last = jnp.where(image == where[0], 1.0, 0.0)
    first_core = where[1] == 0
    target_rows = slice(0, rows)
    for side in range(2):
        columns = slice(side * half, (side + 1) * half)
        extra = jnp.where(first_core if side == 0 else jnp.logical_not(first_core), mine[...].astype(F32), theirs[...].astype(F32))
        total = own[:, columns].astype(F32) + other[:, columns].astype(F32) + last * extra
        target[0, target_rows, columns] = total[:rows].astype(BF)


def memory_total(rows, where, own, other, mine, theirs):
    padded = mine.shape[0]
    images, width = own.shape[0] // padded, own.shape[1]
    block = pl.BlockSpec((padded, width), lambda i: (i, 0))
    half = pl.BlockSpec(mine.shape, lambda i: (0, 0))
    return pl.pallas_call(
        memory_total_body,
        grid=(images,),
        out_shape=jax.ShapeDtypeStruct((images, rows, width), BF),
        in_specs=[SMEM_SPEC, block, block, half, half],
        out_specs=pl.BlockSpec((1, rows, width), lambda i: (i, 0, 0)),
        compiler_params=pltpu.CompilerParams(vmem_limit_bytes=12 * MIB),
        cost_estimate=pl.CostEstimate(flops=0, bytes_accessed=8 * images * padded * width, transcendentals=0),
        name="memory_total",
    )(where, own, other, mine, theirs)


def core_swap(value):
    return lax.ppermute(value, "tensor", [(0, 1), (1, 0)])


def core_half(value, core):
    half = value.shape[1] // 2
    return jnp.where(core == 0, value[:, :half], value[:, half:])


def other_half(value, core):
    half = value.shape[1] // 2
    return jnp.where(core == 0, value[:, half:], value[:, :half])


def rejoined(mine, theirs, core):
    return jnp.concatenate([jnp.where(core == 0, mine, theirs), jnp.where(core == 0, theirs, mine)], 1)


def fetched(value, core):
    mine = shifted(core_half(value, core), "dp", 1)
    return rejoined(mine, core_swap(mine), core)


def given_start(partial, core):
    low = partial.astype(BF)
    return core_half(low, core), core_swap(other_half(low, core))


def given_total(halves_in):
    mine, other = halves_in
    return (mine.astype(F32) + other.astype(F32)).astype(BF)


def outer_split(inner, outer, me, source):
    rows, columns = source.shape
    piece = rows // outer
    order = tuple(range(outer.bit_length() - 1))

    def body(me_ref, source_ref, keep, send):
        mine = me_ref[0] // inner
        for position in range(outer):
            at = pl.multiple_of((mine ^ place_code(position, order)) * piece, piece)
            target = keep if position < outer // 2 else send
            row = position % (outer // 2) * piece
            target[row : row + piece, :] = source_ref[pl.ds(at, piece), :]

    half = jax.ShapeDtypeStruct((rows // 2, columns), source.dtype)
    return pl.pallas_call(
        body,
        out_shape=(half, half),
        in_specs=[SMEM_SPEC, VMEM_SPEC],
        out_specs=(VMEM_SPEC, VMEM_SPEC),
        compiler_params=pltpu.CompilerParams(vmem_limit_bytes=14 * MIB),
        cost_estimate=pl.CostEstimate(flops=0, bytes_accessed=4 * rows * columns, transcendentals=0),
        name="outer_split",
    )(me, source)


def two_level_scatter(stacked, count):
    inner = min(4, count)
    outer = count // inner
    near = [[o * inner + i for i in range(inner)] for o in range(outer)]
    far = [[o * inner + i for o in range(outer)] for i in range(inner)]
    first = lax.psum_scatter(stacked, "dp", scatter_dimension=0, axis_index_groups=near, tiled=True)

    def second(held):
        return lax.psum_scatter(held, "dp", scatter_dimension=0, axis_index_groups=far, tiled=True)

    return first, second


def per_device(
    tokens,
    page_ids,
    image_of_page,
    memory,
    ln0_gain,
    ln0_bias,
    w_self_query,
    b_self_query,
    w_self_key,
    w_self_value,
    b_self_value,
    w_self_out,
    b_self_out,
    ln1_gain,
    ln1_bias,
    w_query,
    b_query,
    w_key,
    w_value,
    b_value,
    w_out,
    b_out,
    ln2_gain,
    ln2_bias,
    w_up,
    b_up,
    w_down,
    b_down,
    cotangent,
):
    count = lax.axis_size("dp")
    me = lax.axis_index("dp")
    core = lax.axis_index("tensor")
    row_count, width = tokens.shape
    image_count, memory_rows = (memory.shape[0], memory.shape[1])
    scale = 1.0 / math.sqrt(HEAD_WIDTH)
    padded_rows = -(-memory_rows // 16) * 16
    first_page = me * image_count
    local_page = page_ids - first_page
    begins = [jnp.sum((local_page < page).astype(jnp.int32)) for page in range(image_count)]
    prior_begin = shifted(jnp.full((128,), begins[1], jnp.int32), "dp", 1)[0]
    slots = [jnp.int32(image_count)] + [image_of_page[page] - first_page for page in range(image_count)]
    meta = jnp.stack(begins + [prior_begin] + slots).astype(jnp.int32)
    last_image = image_of_page[image_count - 1] - first_page
    skipped = row_count // 4
    last_memory = lax.dynamic_index_in_dim(memory, last_image, 0, keepdims=False)
    last_memory = jnp.pad(last_memory, ((0, padded_rows - memory_rows), (0, 0)))
    tokens_mine = shifted(core_half(tokens[skipped:], core), "dp", 1)
    memory_mine_in = shifted(core_half(last_memory, core), "dp", 1)

    def project(rows, weight, bias=None):
        product = jnp.dot(rows, weight, preferred_element_type=F32)
        return (product if bias is None else product + bias).astype(BF)

    hidden_zero, self_queries, self_key_rows, self_values = norm_project(
        tokens,
        None,
        ln0_gain,
        ln0_bias,
        ((w_self_query, b_self_query, scale), (w_self_key, None, 1.0), (w_self_value, b_self_value, 1.0)),
        False,
        True,
    )
    flat_memory, keys_here, values_here = memory_project(memory, padded_rows, w_key, w_value, b_value)
    (tokens_mine,) = tied((tokens_mine,), self_queries, keys_here)
    prior_tokens = rejoined(tokens_mine, core_swap(tokens_mine), core)
    prior_hidden, prior_keys, prior_values = norm_project(
        prior_tokens,
        None,
        ln0_gain,
        ln0_bias,
        ((w_self_key, None, 1.0), (w_self_value, b_self_value, 1.0)),
        False,
        True,
    )
    self_attended, self_logs = self_forward(
        meta, self_queries, prior_keys, self_key_rows, prior_values, self_values
    )
    self_attended, memory_mine_in = tied((self_attended, memory_mine_in))
    prior_memory = rejoined(memory_mine_in, core_swap(memory_mine_in), core)
    self_part = project(self_attended, w_self_out)
    self_other = core_swap(self_part)
    prior_image_keys = project(prior_memory, w_key)
    prior_image_values = project(prior_memory, w_value, b_value)
    start, hidden_one, queries = norm_project(
        tokens, (self_part, self_other, b_self_out), ln1_gain, ln1_bias, ((w_query, b_query, scale),), True, True
    )
    attended, log_totals = cross_forward(
        memory_rows, meta, queries, prior_image_keys, keys_here, prior_image_values, values_here
    )
    cross_part = project(attended, w_out)
    cross_other = core_swap(cross_part)
    inner = min(4, count)
    tile = 512
    middle, down_part, grad_part, forward_grads, up_bias_grad = feed_forward(
        inner, count // inner, tile, start, cross_part, cross_other, b_out, ln2_gain, ln2_bias, cotangent, w_up, b_up, w_down
    )
    grad_other = core_swap(grad_part)
    forward_first, _ = two_level_scatter(forward_grads, count)
    down_other = core_swap(down_part)
    core_list = jnp.full((1,), core, jnp.int32)
    me_list = jnp.full((1,), me, jnp.int32)
    grad_branch, grad_attended, sums_two = norm_back(
        core_list, grad_part, grad_other, middle, cotangent, ln2_gain, None, w_out, True
    )
    (grad_attended,) = tied((grad_attended,), down_other)
    prior_image_key_grads, key_grads, prior_image_value_grads, value_grads, grad_queries = cross_back(
        memory_rows,
        meta,
        queries,
        grad_attended,
        attended,
        log_totals,
        prior_image_keys,
        keys_here,
        prior_image_values,
        values_here,
    )
    hidden_part = back_sum((grad_queries,), (w_query,), (scale,), 256)
    hidden_other = core_swap(hidden_part)
    (grad_queries,) = tied((grad_queries,), hidden_part)
    pair, thirds = bit_orders(count, 2), bit_orders(count, 3)
    thirds = bit_orders(count, 3)
    memory_start = given_start(
        back_sum((prior_image_key_grads, prior_image_value_grads), (w_key, w_value), (1.0, 1.0), padded_rows), core
    )
    memory_part = back_sum((key_grads, value_grads), (w_key, w_value), (1.0, 1.0), padded_rows)
    memory_other = core_swap(memory_part)
    value_bias_grad = jnp.sum(value_grads.astype(F32), axis=0) + jnp.sum(prior_image_value_grads.astype(F32), axis=0)
    query_bias_grad = jnp.sum(grad_queries.astype(F32), axis=0) * scale
    (hidden_other,) = tied((hidden_other,), memory_part)
    memory_half = given_total(memory_start)
    grad_start_low, grad_self_attended, sums_one = norm_back(
        core_list, hidden_part, hidden_other, start, grad_branch, ln1_gain, None, w_self_out, False
    )
    cross_grads = placed_grads(
        inner,
        count // inner,
        (hidden_one, flat_memory, prior_memory, grad_branch, grad_start_low),
        (grad_queries, key_grads, prior_image_key_grads, value_grads, prior_image_value_grads, attended, self_attended),
        (
            (((0, 0),), scale),
            (((1, 1), (2, 2)), 1.0),
            (((1, 3), (2, 4)), 1.0),
            (((3, 5),), 1.0),
            (((4, 6),), 1.0),
        ),
    )
    cross_first, both_second = two_level_scatter(cross_grads, count)
    (grad_self_attended,) = tied((grad_self_attended,), memory_other, cross_grads)
    prior_key_grads, prior_value_grads, prior_query_grads = self_prior_back(
        meta, self_queries, grad_self_attended, self_attended, self_logs, prior_keys, prior_values
    )
    zero_start = given_start(
        back_sum((prior_key_grads, prior_value_grads), (w_self_key, w_self_value), (1.0, 1.0), 256), core
    )
    (forward_first,) = tied((forward_first,), zero_start[0])
    outer_bits = tuple(range(inner.bit_length() - 1, count.bit_length() - 1))
    forward_cube = CubeSum(count, (outer_bits,))
    forward_cube.add(outer_split(inner, count // inner, me_list, forward_first))
    returned_sent = jnp.concatenate([given_total(zero_start), memory_half], 0)
    prior_query_grads, returned_sent = tied((prior_query_grads, returned_sent), *forward_cube.held)
    returned_mine = shifted(returned_sent, "dp", -1)
    self_key_grads, self_value_grads, grad_self_queries = self_own_back(
        meta,
        self_queries,
        grad_self_attended,
        self_attended,
        self_logs,
        self_key_rows,
        self_values,
        prior_query_grads,
    )
    forward_parts = tied(forward_cube.parts, grad_self_queries)
    forward_parts = fold(tuple(forward_parts), True, False)
    forward_cube.level += 1
    forward_cube.held, forward_cube.parts = (), []
    (grad_self_queries,) = tied((grad_self_queries,), *forward_parts)
    self_parts = weight_grads(
        count,
        me_list,
        (hidden_zero, prior_hidden),
        (grad_self_queries, self_key_grads, prior_key_grads, self_value_grads, prior_value_grads),
        (
            (thirds[0], ((((0, 0),), scale),)),
            (thirds[1], ((((0, 1), (1, 2)), 1.0),)),
            (thirds[2], ((((0, 3), (1, 4)), 1.0),)),
        ),
        24,
    )
    self_cube = CubeSum(count, thirds)
    self_cube.add(self_parts)
    (grad_self_queries,) = tied((grad_self_queries,), *self_parts)
    zero_part = back_sum(
        (grad_self_queries, self_key_grads, self_value_grads),
        (w_self_query, w_self_key, w_self_value),
        (scale, 1.0, 1.0),
        256,
    )
    zero_other = core_swap(zero_part)
    (returned_mine,) = tied((returned_mine,), zero_part)
    returned_theirs = core_swap(returned_mine)
    self_cube.advance(zero_part)
    forward_cube.add(tied(forward_parts, *self_cube.held))
    self_query_bias_grad = jnp.sum(grad_self_queries.astype(F32), axis=0) * scale
    self_value_bias_grad = jnp.sum(self_value_grads.astype(F32), axis=0) + jnp.sum(prior_value_grads.astype(F32), axis=0)
    zero_other, returned_theirs = tied((zero_other, returned_theirs), *self_cube.held)
    d_tokens, sums_zero = norm_back(
        core_list, zero_part, zero_other, tokens, grad_start_low, ln0_gain, (returned_mine, returned_theirs, row_count - skipped), None, False
    )
    self_cube.advance(sums_zero)
    (sums_zero,) = tied((sums_zero,), *self_cube.held)
    butterfly = ButterflySum(
        (
            sums_zero[0],
            sums_zero[1],
            self_query_bias_grad,
            self_value_bias_grad,
            sums_one[2],
            sums_one[0],
            sums_one[1],
            query_bias_grad,
            value_bias_grad,
            sums_two[2],
            sums_two[0],
            sums_two[1],
            up_bias_grad[0],
            sums_two[3],
        )
    )
    butterfly.step()
    self_cube.advance(butterfly.total)
    butterfly.total, cross_first, *forward_cube.parts = tied(
        (butterfly.total, cross_first, *forward_cube.parts), *self_cube.held
    )
    cross_sums = both_second(cross_first)
    butterfly.step()
    down_other, memory_other = tied((down_other, memory_other), *self_cube.held)
    layer_out = (middle.astype(F32) + (down_part.astype(F32) + down_other.astype(F32)) + b_down).astype(BF)
    d_memory = memory_total(
        memory_rows, jnp.stack([last_image, core]), memory_part, memory_other, returned_mine[row_count - skipped :], returned_theirs[row_count - skipped :]
    )
    self_sums = self_cube.finish()
    small_sums = butterfly.finish()
    forward_sums = forward_cube.finish()
    cross_sums = cross_sums.astype(F32)
    local = w_query.shape[1]

    def cut(table, number):
        return table[:, number * local : (number + 1) * local]

    pieces = forward_sums.astype(F32).reshape(forward_sums.shape[0], -1, 2, tile)
    summed_up = pieces[:, :, 0].reshape(forward_sums.shape[0], -1)
    summed_down = pieces[:, :, 1].reshape(forward_sums.shape[0], -1).T
    return (
        layer_out,
        d_tokens,
        d_memory,
        small_sums[0],
        small_sums[1],
        cut(self_sums, 0),
        small_sums[2],
        cut(self_sums, 1),
        cut(self_sums, 2),
        small_sums[3],
        cut(cross_sums, 4).T,
        small_sums[4],
        small_sums[5],
        small_sums[6],
        cut(cross_sums, 0),
        small_sums[7],
        cut(cross_sums, 1),
        cut(cross_sums, 2),
        small_sums[8],
        cut(cross_sums, 3).T,
        small_sums[9],
        small_sums[10],
        small_sums[11],
        summed_up,
        small_sums[12],
        summed_down,
        small_sums[13],
    )


def solution(mesh):
    in_specs = (
        P("dp", None),
        P("dp"),
        P("dp"),
        P("dp", None, None),
        P(),
        P(),
        P(None, "tensor"),
        P("tensor"),
        P(None, "tensor"),
        P(None, "tensor"),
        P("tensor"),
        P("tensor", None),
        P(),
        P(),
        P(),
        P(None, "tensor"),
        P("tensor"),
        P(None, "tensor"),
        P(None, "tensor"),
        P("tensor"),
        P("tensor", None),
        P(),
        P(),
        P(),
        P(None, "tensor"),
        P("tensor"),
        P("tensor", None),
        P(),
        P("dp", None),
    )
    out_specs = (
        P("dp", None),
        P("dp", None),
        P("dp", None, None),
        P(),
        P(),
        P("dp", "tensor"),
        P("tensor"),
        P("dp", "tensor"),
        P("dp", "tensor"),
        P("tensor"),
        P("tensor", "dp"),
        P(),
        P(),
        P(),
        P("dp", "tensor"),
        P("tensor"),
        P("dp", "tensor"),
        P("dp", "tensor"),
        P("tensor"),
        P("tensor", "dp"),
        P(),
        P(),
        P(),
        P("dp", "tensor"),
        P("tensor"),
        P("tensor", "dp"),
        P(),
    )
    return jax.shard_map(
        per_device, mesh=mesh, in_specs=in_specs, out_specs=out_specs, check_vma=False
    )
```
